32 devices in a mesh: dp: 4 (over y, x), fsdp: 8 (over z, core).
Axes of the slice: x: 2, y: 2, z: 4, core: 2. Of those that a mesh axis runs over, the one named last changes fastest.
Arguments:
- clean: bfloat16 [640, 12288], P(('dp', 'fsdp')), may hold values from -1 to 1
- noise: bfloat16 [640, 12288], P(('dp', 'fsdp')), may hold values from -5 to 5
- crop_labels: int32 [640, 16, 16], P(('dp', 'fsdp')), may hold values from 0 to 4, as said below
- time_steps: int32 [640, 4], P(('dp', 'fsdp')), may hold values from 0 to 999
- stem_weight: float32 [256, 48], P('fsdp'), may hold values from -0.875 to 0.875
- kernels_weight: float32 [2304, 512], P('fsdp'), may hold values from -0.125 to 0.125
- embed_weight: float32 [128, 512], P('fsdp'), may hold values from -0.5 to 0.5
- project_weight: float32 [512, 256], P('fsdp'), may hold values from -0.25 to 0.25
- attention_weight: float32 [256, 1024], P('fsdp'), may hold values from -0.375 to 0.375
- readout_weight: float32 [2304, 48], P('fsdp'), may hold values from -0.125 to 0.125
- norm_vectors: float32 [256, 15], P('fsdp'), may hold values from 0.1 to 1.9
- stem_momentum: float32 [256, 48], P('fsdp'), may hold values from -0.0078125 to 0.0078125
- kernels_momentum: float32 [2304, 512], P('fsdp'), may hold values from -0.0078125 to 0.0078125
- embed_momentum: float32 [128, 512], P('fsdp'), may hold values from -0.0078125 to 0.0078125
- project_momentum: float32 [512, 256], P('fsdp'), may hold values from -0.0078125 to 0.0078125
- attention_momentum: float32 [256, 1024], P('fsdp'), may hold values from -0.0078125 to 0.0078125
- readout_momentum: float32 [2304, 48], P('fsdp'), may hold values from -0.75 to 0.75
- norm_momentum: float32 [256, 15], P('fsdp'), may hold values from -0.03125 to 0.03125
- stem_average: float32 [256, 48], P('fsdp'), may hold values from -0.875 to 0.875
- kernels_average: float32 [2304, 512], P('fsdp'), may hold values from -0.125 to 0.125
- embed_average: float32 [128, 512], P('fsdp'), may hold values from -0.5 to 0.5
- project_average: float32 [512, 256], P('fsdp'), may hold values from -0.25 to 0.25
- attention_average: float32 [256, 1024], P('fsdp'), may hold values from -0.375 to 0.375
- readout_average: float32 [2304, 48], P('fsdp'), may hold values from -6 to 6
- norm_average: float32 [256, 15], P('fsdp'), may hold values from 0.1 to 1.9
Outputs:
- mean_loss: float32 [], replicated
- stem_momentum_next: float32 [256, 48], P('fsdp')
- kernels_momentum_next: float32 [2304, 512], P('fsdp')
- embed_momentum_next: float32 [128, 512], P('fsdp')
- project_momentum_next: float32 [512, 256], P('fsdp')
- attention_momentum_next: float32 [256, 1024], P('fsdp')
- readout_momentum_next: float32 [2304, 48], P('fsdp')
- norm_momentum_next: float32 [256, 15], P('fsdp')
- stem_weight_next: float32 [256, 48], P('fsdp')
- kernels_weight_next: float32 [2304, 512], P('fsdp')
- embed_weight_next: float32 [128, 512], P('fsdp')
- project_weight_next: float32 [512, 256], P('fsdp')
- attention_weight_next: float32 [256, 1024], P('fsdp')
- readout_weight_next: float32 [2304, 48], P('fsdp')
- norm_vectors_next: float32 [256, 15], P('fsdp')
- stem_average_next: float32 [256, 48], P('fsdp')
- kernels_average_next: float32 [2304, 512], P('fsdp')
- embed_average_next: float32 [128, 512], P('fsdp')
- project_average_next: float32 [512, 256], P('fsdp')
- attention_average_next: float32 [256, 1024], P('fsdp')
- readout_average_next: float32 [2304, 48], P('fsdp')
- norm_average_next: float32 [256, 15], P('fsdp')
The draws below stay inside these ranges and needn't reach their ends.
Inputs may be any that keep to these rules, and one draw needn't show every extreme that they name: `crop_labels`: in each canvas a column cut splits the 16 x 16 grid into a left and a right part, each split by its own row cut; every side of the four rectangles is 4 to 12 cells. Rectangles 1 and 4 carry their numbers always, rectangles 2 and 3 carry theirs or 0.
All inputs are finite; a program needn't handle non-finite values.
Results may differ from the reference program's by a relative error of at most 0.011.
The reference program's roundings to bfloat16 on the way count: a program that leaves them out, or rounds other values in their place, can miss the bound.
Values may be sent and summed in bfloat16 or wider, within the bound.
No kernel may reach another device: no remote copies, remote signals or barrier semaphores. Data moves between devices by JAX's collectives and lax.ppermute only.
A program may use at most 512 MiB of HBM per device.

```python
import math
import jax
import jax.numpy as jnp
from jax import lax

C = 256
GROUPS = 32
TEMB = 128
TEMB_HID = 512
SIDE = 16
PATCH = 4
CROPS = 4
TSTEPS = 1000
NORM_ROWS = 15
CANV_DEV = 20
CANVASES = 640
IMAGE = 64
DEVICES = 32


def draw_crop_labels(key, part):
    keys_all = jax.random.split(key, 5)
    shape_cut = (CANVASES, 1, 1)
    column_cut = jax.random.randint(keys_all[0], shape_cut, 4, SIDE - 3)
    left_cut = jax.random.randint(keys_all[1], shape_cut, 4, SIDE - 3)
    right_cut = jax.random.randint(keys_all[2], shape_cut, 4, SIDE - 3)
    second_kept = jax.random.randint(keys_all[3], shape_cut, 0, 2)
    third_kept = jax.random.randint(keys_all[4], shape_cut, 0, 2)
    rows_index = jnp.arange(SIDE, dtype=jnp.int32).reshape(1, SIDE, 1)
    cols_index = jnp.arange(SIDE, dtype=jnp.int32).reshape(1, 1, SIDE)
    on_left = cols_index < column_cut
    upper = jnp.where(on_left, rows_index < left_cut, rows_index < right_cut)
    labels = jnp.where(on_left, jnp.where(upper, 1, 2 * second_kept), jnp.where(upper, 3 * third_kept, 4))
    return labels.astype(jnp.int32)


def plant(entries, rng, least, high):
    extent = entries.shape
    index_at = [jax.random.randint(jax.random.fold_in(rng, axis), (), 0, extent[axis]) for axis in range(len(extent))]
    entries = entries.at[tuple(index_at)].set(least)
    longest = extent.index(max(extent))
    index_at[longest] = (index_at[longest] + 1) % extent[longest]
    return entries.at[tuple(index_at)].set(high)


def block_levels(own_key, dims, cuts, low, high):
    def one(dim, shards_of):
        steps = jax.random.uniform(jax.random.fold_in(jax.random.fold_in(own_key, 6), dim), (shards_of,), jnp.float32, low / len(cuts), high / len(cuts))
        return jnp.repeat(jnp.exp(steps), dims[dim] // shards_of).reshape((-1,) + (1,) * (len(dims) - dim - 1))

    level = one(*cuts[0])
    for cut in cuts[1:]:
        level = level * one(*cut)
    return level


def normal_values(rng, dims, width, bound, cuts=(), kind=jnp.bfloat16):
    factor_of = block_levels(rng, dims, cuts, -0.22, 0.18) if cuts else 1.0
    drawn = jax.random.normal(rng, dims, jnp.float32) * width * factor_of
    return jnp.minimum(jnp.maximum(drawn, -bound), bound).astype(kind)


def setup_inputs(seed: int = 0) -> dict:
    seeds = jax.random.split(jax.random.key(seed), 26)
    return {
        "clean": jnp.clip(jax.random.uniform(seeds[0], (CANVASES, 3 * IMAGE * IMAGE), jnp.float32, -1.0, 1.0) * block_levels(seeds[0], (CANVASES, 3 * IMAGE * IMAGE), ((0, 32),), -0.4, 0.0), -1.0, 1.0).astype(jnp.bfloat16),
        "noise": normal_values(seeds[1], (CANVASES, 3 * IMAGE * IMAGE), 1.0, 5.0, ((0, 32),)),
        "crop_labels": draw_crop_labels(jax.random.fold_in(seeds[25], 71), 0),
        "time_steps": plant(jax.random.randint(seeds[3], (CANVASES, CROPS), 0, TSTEPS), jax.random.fold_in(seeds[3], 1), 0, TSTEPS - 1).astype(jnp.int32),
        "stem_weight": normal_values(seeds[4], (C, 3 * PATCH * PATCH), (3 * PATCH * PATCH) ** -0.5, 0.875, ((0, 8),), jnp.float32),
        "kernels_weight": normal_values(seeds[5], (9 * C, 2 * C), (9 * C) ** -0.5, 0.125, ((0, 8),), jnp.float32),
        "embed_weight": normal_values(seeds[6], (TEMB, TEMB_HID), TEMB ** -0.5, 0.5, ((0, 8),), jnp.float32),
        "project_weight": normal_values(seeds[7], (TEMB_HID, C), TEMB_HID ** -0.5, 0.25, ((0, 8),), jnp.float32),
        "attention_weight": normal_values(seeds[8], (C, 4 * C), C ** -0.5, 0.375, ((0, 8),), jnp.float32),
        "readout_weight": normal_values(seeds[9], (9 * C, 3 * PATCH * PATCH), (9 * C) ** -0.5, 0.125, ((0, 8),), jnp.float32),
        "norm_vectors": jnp.clip(1.0 + 0.18 * jax.random.normal(seeds[10], (C, NORM_ROWS), jnp.float32), 0.1, 1.9),
        "stem_momentum": normal_values(seeds[11], (C, 3 * PATCH * PATCH), (2.0 * (CANV_DEV * DEVICES * 3072) ** -0.5), 0.0078125, ((0, 8),), jnp.float32),
        "kernels_momentum": normal_values(seeds[12], (9 * C, 2 * C), (2.0 * (CANV_DEV * DEVICES * 3072) ** -0.5), 0.0078125, ((0, 8),), jnp.float32),
        "embed_momentum": normal_values(seeds[13], (TEMB, TEMB_HID), (2.0 * (CANV_DEV * DEVICES * 3072) ** -0.5), 0.0078125, ((0, 8),), jnp.float32),
        "project_momentum": normal_values(seeds[14], (TEMB_HID, C), (2.0 * (CANV_DEV * DEVICES * 3072) ** -0.5), 0.0078125, ((0, 8),), jnp.float32),
        "attention_momentum": normal_values(seeds[15], (C, 4 * C), (2.0 * (CANV_DEV * DEVICES * 3072) ** -0.5), 0.0078125, ((0, 8),), jnp.float32),
        "readout_momentum": normal_values(seeds[16], (9 * C, 3 * PATCH * PATCH), 0.05, 0.75, ((0, 8),), jnp.float32),
        "norm_momentum": normal_values(seeds[17], (C, NORM_ROWS), (8.0 * (CANV_DEV * DEVICES * 3072) ** -0.5), 0.03125, ((0, 8),), jnp.float32),
        "stem_average": normal_values(seeds[18], (C, 3 * PATCH * PATCH), (3 * PATCH * PATCH) ** -0.5, 0.875, ((0, 8),), jnp.float32),
        "kernels_average": normal_values(seeds[19], (9 * C, 2 * C), (9 * C) ** -0.5, 0.125, ((0, 8),), jnp.float32),
        "embed_average": normal_values(seeds[20], (TEMB, TEMB_HID), TEMB ** -0.5, 0.5, ((0, 8),), jnp.float32),
        "project_average": normal_values(seeds[21], (TEMB_HID, C), TEMB_HID ** -0.5, 0.25, ((0, 8),), jnp.float32),
        "attention_average": normal_values(seeds[22], (C, 4 * C), C ** -0.5, 0.375, ((0, 8),), jnp.float32),
        "readout_average": normal_values(seeds[23], (9 * C, 3 * PATCH * PATCH), (0.0006 * (CANV_DEV * DEVICES * 3072) ** 0.5), 6.0, ((0, 8),), jnp.float32),
        "norm_average": jnp.clip(1.0 + 0.18 * jax.random.normal(seeds[24], (C, NORM_ROWS), jnp.float32), 0.1, 1.9),
    }


highest = lax.Precision.HIGHEST
eps_norm = 1e-05
lr_scale = 0.01
momentum_rate = 0.5
average_rate = 0.5
masked_score = -1000000000.0
block_canvases = 16

@jax.custom_vjp
def low(v):
    return lax.optimization_barrier(v.astype(jnp.bfloat16)).astype(jnp.float32)

@jax.custom_vjp
def low_back(v):
    return v

def low_keep(v):
    return (low(v), None)

def low_pass(kept, grad):
    return (grad,)

def back_keep(v):
    return (v, None)

def back_low(kept, grad):
    return (low(grad),)
low.defvjp(low_keep, low_pass)
low_back.defvjp(back_keep, back_low)

def product(left_side, right_side):
    return low_back(jnp.matmul(low(left_side), low(right_side), precision=highest))

def crop_onehot(crop_labels):
    flat_labels = crop_labels.reshape(crop_labels.shape[0], -1)
    return (flat_labels[..., None] == jnp.arange(1, CROPS + 1, dtype=jnp.int32)).astype(jnp.float32)

def noise_levels(time_steps):
    beta_values = jnp.linspace(0.0001, 0.02, TSTEPS, dtype=jnp.float32)
    alpha_bars = jnp.exp(jnp.cumsum(jnp.log(1.0 - beta_values)))
    picked = (time_steps[..., None] == jnp.arange(TSTEPS, dtype=jnp.int32)).astype(jnp.float32)
    chosen = lax.optimization_barrier(jnp.sum(picked * alpha_bars, axis=-1))
    return (jnp.sqrt(chosen), jnp.sqrt(1.0 - chosen))

def time_features(time_steps):
    half_width = TEMB // 2
    frequency = jnp.exp(-math.log(10000.0) * jnp.arange(half_width, dtype=jnp.float32) / (half_width - 1))
    angles = time_steps.astype(jnp.float32)[..., None] * frequency
    return jnp.concatenate([jnp.sin(angles), jnp.cos(angles)], axis=-1)

def to_patches(canvas_image):
    canvas_count = canvas_image.shape[0]
    blocked = canvas_image.reshape(canvas_count, 3, SIDE, PATCH, SIDE, PATCH)
    return blocked.transpose(0, 2, 4, 1, 3, 5).reshape(canvas_count, SIDE * SIDE, 3 * PATCH * PATCH)

def token_values(crop_table, per_crop):
    return jnp.einsum('bpk,bk->bp', crop_table, per_crop, precision=highest)[..., None]

def group_norm(values, crop_table, norm_gain, norm_shift):
    canvas_count, channels = (values.shape[0], values.shape[2])
    group_width = channels // GROUPS
    crop_counts = jnp.maximum(lax.optimization_barrier(jnp.sum(crop_table, axis=1)), 1.0)[..., None] * group_width
    crop_sums = jnp.einsum('bpk,bpc->bkc', crop_table, values, precision=highest)
    crop_means = lax.optimization_barrier(jnp.sum(crop_sums.reshape(canvas_count, CROPS, GROUPS, group_width), axis=-1)) / crop_counts
    token_mean = jnp.einsum('bpk,bkc->bpc', crop_table, jnp.repeat(crop_means, group_width, axis=-1), precision=highest)
    centred = values - token_mean
    crop_squares = jnp.einsum('bpk,bpc->bkc', crop_table, centred * centred, precision=highest)
    crop_spread = lax.optimization_barrier(jnp.sum(crop_squares.reshape(canvas_count, CROPS, GROUPS, group_width), axis=-1)) / crop_counts
    token_scale = jnp.einsum('bpk,bkc->bpc', crop_table, jnp.repeat(lax.rsqrt(crop_spread + eps_norm), group_width, axis=-1), precision=highest)
    inside = lax.optimization_barrier(jnp.sum(crop_table, axis=-1))[..., None]
    return (centred * token_scale * norm_gain + norm_shift) * inside

def norm_swish(values, crop_table, norm_gain, norm_shift):
    return jax.nn.silu(group_norm(values, crop_table, norm_gain, norm_shift))

def conv_columns(values, crop_labels):
    canvas_count, grid_side = (crop_labels.shape[0], crop_labels.shape[1])
    grid_values = values.reshape(canvas_count, grid_side, grid_side, -1)
    padded = jnp.pad(grid_values, ((0, 0), (1, 1), (1, 1), (0, 0)))
    border = jnp.pad(crop_labels, ((0, 0), (1, 1), (1, 1)), constant_values=-1)
    shifted = []
    for down_step in range(3):
        for side_step in range(3):
            same_crop = border[:, down_step:down_step + grid_side, side_step:side_step + grid_side] == crop_labels
            shifted.append(padded[:, down_step:down_step + grid_side, side_step:side_step + grid_side] * same_crop[..., None].astype(values.dtype))
    return jnp.concatenate(shifted, axis=-1).reshape(canvas_count, grid_side * grid_side, -1)

def forward(params, piece):
    stem_weight, kernels_weight, embed_weight, project_weight, attention_weight, readout_weight, norm_vectors = params
    clean, noise, crop_labels, time_steps = piece
    vector_rows = low(norm_vectors).T
    channels = stem_weight.shape[0]
    crop_table = crop_onehot(crop_labels)
    inside = lax.optimization_barrier(jnp.sum(crop_table, axis=-1))
    signal_scale, noise_scale = noise_levels(time_steps)
    target = to_patches(noise)
    mixed_input = token_values(crop_table, signal_scale) * to_patches(clean) + token_values(crop_table, noise_scale) * target
    stem_out = product(mixed_input, stem_weight.T) + vector_rows[0]
    hidden = jax.nn.silu(product(time_features(time_steps), embed_weight))
    time_bias = product(hidden, project_weight) + vector_rows[1]
    token_time = jnp.einsum('bpk,bkc->bpc', crop_table, time_bias, precision=highest)
    act_one = norm_swish(stem_out, crop_table, vector_rows[2], vector_rows[3])
    conv_one = product(conv_columns(act_one, crop_labels), kernels_weight[:, :channels]) + vector_rows[4] + token_time
    act_two = norm_swish(conv_one, crop_table, vector_rows[5], vector_rows[6])
    resid_one = stem_out + product(conv_columns(act_two, crop_labels), kernels_weight[:, channels:]) + vector_rows[7]
    normed = group_norm(resid_one, crop_table, vector_rows[8], vector_rows[9])
    triple = product(normed, attention_weight[:, :3 * channels])
    query = triple[..., :channels] + vector_rows[10]
    key_part = triple[..., channels:2 * channels]
    value_part = triple[..., 2 * channels:] + vector_rows[11]
    flat_labels = crop_labels.reshape(crop_labels.shape[0], -1)
    same_crop = flat_labels[:, :, None] == flat_labels[:, None, :]
    scores = low_back(jnp.einsum('bpc,bqc->bpq', low(query), low(key_part), precision=highest)) * channels ** (-0.5)
    probs = jax.nn.softmax(jnp.where(same_crop, scores, masked_score), axis=-1)
    mixed = low_back(jnp.einsum('bpq,bqc->bpc', low(probs), low(value_part), precision=highest))
    resid_two = resid_one + product(mixed, attention_weight[:, 3 * channels:]) + vector_rows[12]
    act_final = norm_swish(resid_two, crop_table, vector_rows[13], vector_rows[14])
    predicted = product(conv_columns(act_final, crop_labels), readout_weight)
    error = (predicted - target) * inside[..., None]
    return jnp.sum(error * error)

def reference(clean, noise, crop_labels, time_steps, stem_weight, kernels_weight, embed_weight, project_weight, attention_weight, readout_weight, norm_vectors, stem_momentum, kernels_momentum, embed_momentum, project_momentum, attention_momentum, readout_momentum, norm_momentum, stem_average, kernels_average, embed_average, project_average, attention_average, readout_average, norm_average):
    params = (stem_weight, kernels_weight, embed_weight, project_weight, attention_weight, readout_weight, norm_vectors)
    moments = (stem_momentum, kernels_momentum, embed_momentum, project_momentum, attention_momentum, readout_momentum, norm_momentum)
    averages = (stem_average, kernels_average, embed_average, project_average, attention_average, readout_average, norm_average)
    count = PATCH * PATCH * jnp.sum((crop_labels > 0).astype(jnp.float32))
    blocks = crop_labels.shape[0] // block_canvases

    def split(array):
        return array.reshape((blocks, block_canvases) + array.shape[1:])
    pieces = (split(clean.astype(jnp.float32)), split(noise.astype(jnp.float32)), split(crop_labels), split(time_steps))

    def accumulate(carry, piece):
        total, grads = carry
        value, pull_back = jax.vjp(lambda *weights: forward(weights, piece), *params)
        extra = pull_back(jnp.ones_like(value) / count)
        return ((total + value, tuple((earlier + added for earlier, added in zip(grads, extra)))), None)
    start = (jnp.zeros((), jnp.float32), tuple((jnp.zeros_like(weight_now) for weight_now in params)))
    (total, grads), unused = lax.scan(accumulate, start, pieces)
    rate = lr_scale * jnp.sqrt(count)
    moment_next = [momentum_rate * old_moment + grad for old_moment, grad in zip(moments, grads)]
    master_next = [master - rate * (grad + momentum_rate * moment) for master, grad, moment in zip(params, grads, moment_next)]
    average_next = [average_rate * old_average + (1.0 - average_rate) * master for old_average, master in zip(averages, master_next)]
    return (total / count, moment_next[0], moment_next[1], moment_next[2], moment_next[3], moment_next[4], moment_next[5], moment_next[6], master_next[0], master_next[1], master_next[2], master_next[3], master_next[4], master_next[5], master_next[6], average_next[0], average_next[1], average_next[2], average_next[3], average_next[4], average_next[5], average_next[6])
```

```python
import math

import jax
import jax.numpy as jnp
import numpy as np
from jax import lax
from jax.experimental import pallas as pl
from jax.experimental.pallas import tpu as pltpu
from jax.sharding import PartitionSpec as P

GROUPS = 32
TEMB = 128
SIDE = 16
PATCH = 4
CROPS = 4
TSTEPS = 1000
TOK = SIDE * SIDE
CH = 256
PIX = 3 * PATCH * PATCH
PAIR = 2
ROWS = PAIR * TOK
GRIDROWS = PAIR * SIDE
VIRT = 8

eps_norm = 1e-05
lr_scale = 0.01
momentum_rate = 0.5
average_rate = 0.5
far_score = -1e30
f32 = jnp.float32
bf16 = jnp.bfloat16


def pack_rows(parts):
    stem, kernels, embed, project, attention, readout, norm = parts
    dtype = kernels.dtype

    def wide(left, right):
        fill = jnp.zeros((left.shape[0], 128 - right.shape[1]), dtype)
        return jnp.concatenate([left, right, fill], axis=1)

    half = project.shape[0] // 2
    none = jnp.zeros((embed.shape[0], 0), dtype)
    return jnp.concatenate(
        [
            wide(kernels, readout),
            wide(attention[:, :512], stem),
            wide(attention[:, 512:], norm),
            wide(jnp.concatenate([project[:half], project[half:]], axis=1), none[:1].repeat(half, 0)),
            wide(embed, none),
        ],
        axis=0,
    )


def unpack_rows(rows, k, a, p, e):
    half = p // 2
    at = [0, k, k + a, k + 2 * a, k + 2 * a + half, k + 2 * a + half + e]
    r1, r2, r3, r4, r5 = [rows[..., at[i] : at[i + 1], :] for i in range(5)]
    attention = jnp.concatenate([r2[..., :512], r3[..., :512]], axis=-1)
    project = jnp.concatenate([r4[..., :256], r4[..., 256:512]], axis=-2)
    return (
        r2[..., 512 : 512 + PIX],
        r1[..., :512],
        r5[..., :512],
        project,
        attention,
        r1[..., 512 : 512 + PIX],
        r3[..., 512 : 512 + 15],
    )


def repack(packed, parts_now, parts_next):
    if parts_now == parts_next:
        return packed
    cut = [n // parts_now for n in (9 * CH, CH, 2 * CH, CH // 2)]
    pieces = unpack_rows(packed, *cut)
    whole = [piece.reshape(-1, piece.shape[-1]) for piece in pieces]
    split = [piece.reshape(parts_next, -1, piece.shape[-1]) for piece in whole]
    return jax.vmap(lambda *p: pack_rows(p))(*split)


KROW = 9 * CH // VIRT
AROW = CH // VIRT
PROW = CH // VIRT
EROW = TEMB // VIRT
PACKED = KROW + 2 * AROW + PROW + EROW


def lane_groups(value):
    lane = lax.broadcasted_iota(jnp.int32, (8, 128), 1)
    tiles = []
    for t in range(2):
        x = value[:, t * 128 : (t + 1) * 128]
        for s in (1, 2, 4):
            x = x + jnp.where((lane & s) == 0, pltpu.roll(x, 128 - s, 1), pltpu.roll(x, s, 1))
        tiles.append(x)
    return jnp.concatenate(tiles, axis=1)


def nt(a, b):
    return lax.dot_general(a, b, (((1,), (1,)), ((), ())), preferred_element_type=f32)


def nn(a, b):
    return lax.dot_general(a, b, (((1,), (0,)), ((), ())), preferred_element_type=f32)


def step_kernel(
    quad_ref, geo_ref, scale_ref, wp_ref, feat_ref, xt_ref, tg_ref, inv_ref, cnt_ref,
    out_ref, loss_ref,
    wk1, wk2, wt1, wt2, wr, wrt, wqkv, wat, wo, wot, ws, wpj, wem, vec, tbs, hpre, wrn,
    gk1, gk2, gr, ga, gs, gv, dtb, lacc,
    x0, x1, x2, x3, sp1, sp2, sp4, xs, us, xv1, xv2, xc3, nrm, qs, ks, vs, prob, mix, gtop, gres, dys,
    dpc, dyp, trip, mvu, mvd, tab, ctab, pref,
):
    step = pl.program_id(0)
    last = pl.num_programs(0) - 1

    @pl.when(step == 0)
    def _():
        for f in range(VIRT):
            wk1[pl.ds(f * KROW, KROW), :] = wp_ref[f, :KROW, 0:256]
            wk2[pl.ds(f * KROW, KROW), :] = wp_ref[f, :KROW, 256:512]
            wrn[pl.ds(f * KROW, KROW), :] = wp_ref[f, :KROW, 512:640]
            att = slice(KROW, KROW + AROW)
            att2 = slice(KROW + AROW, KROW + 2 * AROW)
            wqkv[pl.ds(f * AROW, AROW), 0:512] = wp_ref[f, att, 0:512]
            wqkv[pl.ds(f * AROW, AROW), 512:768] = wp_ref[f, att2, 0:256]
            wo[pl.ds(f * AROW, AROW), :] = wp_ref[f, att2, 256:512]
            pr = KROW + 2 * AROW
            wpj[pl.ds(f * 2 * PROW, PROW), :] = wp_ref[f, pr : pr + PROW, 0:256]
            wpj[pl.ds(f * 2 * PROW + PROW, PROW), :] = wp_ref[f, pr : pr + PROW, 256:512]
            wem[pl.ds(f * EROW, EROW), :] = wp_ref[f, pr + PROW : pr + PROW + EROW, 0:512]
        stem = jnp.concatenate([wp_ref[f, KROW : KROW + AROW, 512:640] for f in range(VIRT)], axis=0)
        norm = jnp.concatenate([wp_ref[f, KROW + AROW : KROW + 2 * AROW, 512:640] for f in range(VIRT)], axis=0)
        ws[...] = stem.T
        vec[...] = norm.T.astype(f32)[:16]
        for dy in range(3):
            for dx in range(3):
                rows = pl.ds((dy * 3 + dx) * 256, 256)
                wt1[pl.ds(dy * 256, 256), dx * 256 : (dx + 1) * 256] = wk1[rows, :].T
                wt2[pl.ds(dy * 256, 256), dx * 256 : (dx + 1) * 256] = wk2[rows, :].T
        for j in range(3):
            wat[pl.ds(j * 256, 256), :] = wqkv[:, j * 256 : (j + 1) * 256].T
        wot[...] = wo[...].T
        for dx in range(3):
            rows = [wrn[pl.ds(dy * 768 + dx * 256, 256), :].astype(f32) for dy in range(3)]
            tile0 = (rows[0] + pltpu.roll(rows[1], 64, 1)).astype(bf16)
            tile1 = rows[2].astype(bf16)
            wr[pl.ds(dx * 256, 256), 0:128] = tile0
            wr[pl.ds(dx * 256, 256), 128:256] = tile1
            wrt[0:128, dx * 256 : (dx + 1) * 256] = tile0.T
            wrt[128:256, dx * 256 : (dx + 1) * 256] = tile1.T
        hp = nn(feat_ref[...], wem[...])
        hpre[...] = hp
        tbs[...] = nn(jax.nn.silu(hp).astype(bf16), wpj[...]) + vec[1:2, :]
        for ref in (gk1, gk2, gr, ga, gs, gv, lacc, pref):
            ref[...] = jnp.zeros_like(ref)
        for ref in (xv1, xv2):
            for b in range(PAIR):
                ref[pl.ds(b * TOK, 16), 0:768] = jnp.zeros((16, 768), bf16)
                ref[pl.ds(b * TOK + TOK - 16, 16), 1536:2304] = jnp.zeros((16, 768), bf16)
        for b in range(PAIR):
            dpc[pl.ds(b * TOK + TOK - 16, 16), 0:256] = jnp.zeros((16, 256), bf16)
            dpc[pl.ds(b * TOK, 16), 512:768] = jnp.zeros((16, 256), bf16)

    base = step * PAIR
    cuts = [geo_ref[(base + b) * 8] for b in range(PAIR)]
    lefts = [geo_ref[(base + b) * 8 + 1] for b in range(PAIR)]
    rights = [geo_ref[(base + b) * 8 + 2] for b in range(PAIR)]
    iota8 = lax.broadcasted_iota(jnp.int32, (8, 256), 0)
    iota8n = lax.broadcasted_iota(jnp.int32, (8, 128), 0)
    onleft = [[iota8 < (cuts[b] - 8 * h) for h in range(2)] for b in range(PAIR)]
    onleftn = [[iota8n < (cuts[b] - 8 * h) for h in range(2)] for b in range(PAIR)]
    hasl = [[(iota8n + 8 * h != 0) & (iota8n + 8 * h != cuts[b]) for h in range(2)] for b in range(PAIR)]
    hasr = [[(iota8n + 8 * h != 15) & (iota8n + 8 * h != cuts[b] - 1) for h in range(2)] for b in range(PAIR)]

    def quads(i):
        at = (base * SIDE + i) * 2
        return quad_ref[at], quad_ref[at + 1]

    for i in range(GRIDROWS):
        b, r = divmod(i, SIDE)
        upl = ((lefts[b] != r) & (r > 0)).astype(f32)
        upr = ((rights[b] != r) & (r > 0)).astype(f32)
        dnl = ((lefts[b] != r + 1) & (r < SIDE - 1)).astype(f32)
        dnr = ((rights[b] != r + 1) & (r < SIDE - 1)).astype(f32)
        for h in range(2):
            mvu[pl.ds(i * 16 + 8 * h, 8), :] = jnp.where(onleftn[b][h], upl, upr)
            mvd[pl.ds(i * 16 + 8 * h, 8), :] = jnp.where(onleftn[b][h], dnl, dnr)

    def put_table(slot, table):
        for q in range(4 * PAIR):
            tab[slot, q] = jnp.broadcast_to(table[q : q + 1, :], (8, 256))

    def pick(slot, i):
        left, right = quads(i)
        return tab[slot, left], tab[slot, right]

    def crop_sums(values_of):
        rows = [[], []]
        for b in range(PAIR):
            total = [None, None]
            left = [None, None]
            for r in range(SIDE):
                halves = [values_of(b * SIDE + r, h) for h in range(2)]
                for j in range(2):
                    a0, a1 = halves[0][j], halves[1][j]
                    lp = jnp.where(onleft[b][0], a0, 0.0) + jnp.where(onleft[b][1], a1, 0.0)
                    tp = a0 + a1
                    left[j] = lp if r == 0 else left[j] + lp
                    total[j] = tp if r == 0 else total[j] + tp
                    pref[b, j, 0, r + 1] = left[j]
                    pref[b, j, 1, r + 1] = total[j]
            for j in range(2):
                q0 = pref[b, j, 0, lefts[b]]
                q1 = left[j] - q0
                q2 = pref[b, j, 1, rights[b]] - pref[b, j, 0, rights[b]]
                q3 = (total[j] - left[j]) - q2
                rows[j] += [jnp.sum(q, axis=0, keepdims=True) for q in (q0, q1, q2, q3)]
        return [jnp.concatenate(part, axis=0) for part in rows]

    inv = inv_ref[...]
    cnt = cnt_ref[...]

    def forward_tables(n, xref, bias, gain, shift):
        def both(i, h):
            x = xref[pl.ds(i * 16 + h * 8, 8), :]
            return x, x * x

        s1, s2 = crop_sums(both)
        own = s1 * inv
        mean = lane_groups(own + bias) * 0.125
        apart = own + bias - mean
        var = lane_groups(jnp.maximum(s2 * inv - own * own, 0.0) + apart * apart) * 0.125
        scale = lax.rsqrt(var + eps_norm)
        a = scale * gain
        e = bias - mean
        put_table(n, a)
        put_table(4, e * a + shift)
        ctab[n, 0] = a
        ctab[n, 1] = scale
        ctab[n, 2] = e
        ctab[n, 3] = s1

    def backward_tables(n, s1, s2, gain):
        a, scale, e, sx = [ctab[n, j] for j in range(4)]
        sn = scale * (s2 + e * s1)
        m1 = lane_groups(gain * s1 * inv) * 0.125
        m2 = lane_groups(gain * sn * inv) * 0.125
        v = scale * scale * m2
        u = scale * m1 + e * v
        put_table(5, v)
        put_table(6, u)
        return a * s1 - v * sx - cnt * u, s1, sn

    def silu_pass(n, xref, spref, xvref, vertical):
        for i in range(GRIDROWS):
            b, r = divmod(i, SIDE)
            al, ar = pick(n, i)
            dl, dr = pick(4, i)
            for h in range(2):
                rows = pl.ds(i * 16 + h * 8, 8)
                x = xref[rows, :]
                y = x * jnp.where(onleft[b][h], al, ar) + jnp.where(onleft[b][h], dl, dr)
                hy = 0.5 * y
                t = jnp.tanh(hy)
                act = hy * t + hy
                sig = 0.5 * t + 0.5
                spref[rows, :] = sig + act - act * sig
                for c in range(2):
                    xs[c, pl.ds(8 + i * 16 + h * 8, 8), :] = act[:, c * 128 : (c + 1) * 128]
            at = 8 + i * 16
            for c in range(2):
                taps = []
                for dx in (-1, 0, 1):
                    pieces = []
                    for h in range(2):
                        piece = xs[c, pl.ds(at + h * 8 + dx, 8), :]
                        if dx == -1:
                            piece = jnp.where(hasl[b][h], piece, 0.0)
                        if dx == 1:
                            piece = jnp.where(hasr[b][h], piece, 0.0)
                        pieces.append(piece)
                    taps.append(jnp.concatenate(pieces, axis=0).astype(bf16))
                for k, tap in enumerate(taps):
                    lanes = slice(k * 256 + c * 128, k * 256 + c * 128 + 128)
                    if not vertical:
                        xvref[pl.ds(i * 16, 16), lanes] = tap
                        continue
                    mid = slice(768 + lanes.start, 768 + lanes.stop)
                    low = slice(1536 + lanes.start, 1536 + lanes.stop)
                    xvref[pl.ds(i * 16, 16), mid] = tap
                    if r < SIDE - 1:
                        xvref[pl.ds(i * 16 + 16, 16), lanes] = tap * mvu[pl.ds(i * 16 + 16, 16), :].astype(bf16)
                    if r > 0:
                        xvref[pl.ds(i * 16 - 16, 16), low] = tap * mvd[pl.ds(i * 16 - 16, 16), :].astype(bf16)

    def spread_grad(i, value):
        b, r = divmod(i, SIDE)
        low = value.astype(bf16)
        dpc[pl.ds(i * 16, 16), 256:512] = low
        for c in range(2):
            part = low[:, c * 128 : (c + 1) * 128]
            lanes = slice(c * 128, c * 128 + 128)
            if r > 0:
                dpc[pl.ds(i * 16 - 16, 16), lanes] = part * mvd[pl.ds(i * 16 - 16, 16), :].astype(bf16)
            if r < SIDE - 1:
                lanes = slice(512 + c * 128, 512 + c * 128 + 128)
                dpc[pl.ds(i * 16 + 16, 16), lanes] = part * mvu[pl.ds(i * 16 + 16, 16), :].astype(bf16)

    def tap_back(i, h, spref, xref):
        b = i // SIDE
        at = 8 + i * 16 + h * 8
        cols = []
        for c in range(2):
            d = us[2 + c, pl.ds(at, 8), :]
            d = d + jnp.where(hasr[b][h], us[c, pl.ds(at + 1, 8), :], 0.0)
            d = d + jnp.where(hasl[b][h], us[4 + c, pl.ds(at - 1, 8), :], 0.0)
            cols.append(d)
        rows = pl.ds(i * 16 + h * 8, 8)
        dy = jnp.concatenate(cols, axis=1) * spref[rows, :]
        dys[rows, :] = dy
        return dy, dy * xref[rows, :]

    def norm_grad(n, i, h, xref):
        b = i // SIDE
        rows = pl.ds(i * 16 + h * 8, 8)
        m = onleft[b][h]
        al, ar = pick(n, i)
        vl, vr = pick(5, i)
        ul, ur = pick(6, i)
        return dys[rows, :] * jnp.where(m, al, ar) - xref[rows, :] * jnp.where(m, vl, vr) - jnp.where(m, ul, ur)

    def put_us(lhs, rhs_ref):
        for dx in range(3):
            u = nn(lhs, rhs_ref[:, dx * 256 : (dx + 1) * 256])
            for c in range(2):
                us[dx * 2 + c, pl.ds(8, ROWS), :] = u[:, c * 128 : (c + 1) * 128]

    def weight_grad(acc, xref, first):
        for dx in range(3):
            turned = xref[:, first + dx * 256 : first + (dx + 1) * 256].T
            for dy in range(3):
                acc[pl.ds(dx * 256, 256), dy * 256 : (dy + 1) * 256] += nn(turned, dpc[:, dy * 256 : (dy + 1) * 256])

    def row(k):
        return vec[k : k + 1, :]

    x0[...] = nn(xt_ref[...], ws[...])
    forward_tables(0, x0, jnp.broadcast_to(row(0), (8, 256)), row(2), row(3))
    silu_pass(0, x0, sp1, xv1, True)
    x1[...] = nn(xv1[...], wk1[...])
    bias1 = tbs[pl.ds(step * 8, 8), :] + row(4)
    forward_tables(1, x1, bias1, row(5), row(6))
    silu_pass(1, x1, sp2, xv2, True)
    x2[...] = x0[...] + nn(xv2[...], wk2[...])
    forward_tables(2, x2, jnp.broadcast_to(row(0) + row(7), (8, 256)), row(8), row(9))
    for i in range(GRIDROWS):
        b = i // SIDE
        al, ar = pick(2, i)
        dl, dr = pick(4, i)
        halves = []
        for h in range(2):
            x = x2[pl.ds(i * 16 + h * 8, 8), :]
            halves.append(x * jnp.where(onleft[b][h], al, ar) + jnp.where(onleft[b][h], dl, dr))
        nrm[pl.ds(i * 16, 16), :] = jnp.concatenate(halves, axis=0).astype(bf16)
    qs[...] = (nn(nrm[...], wqkv[:, 0:256]) + row(10)).astype(bf16)
    ks[...] = nn(nrm[...], wqkv[:, 256:512]).astype(bf16)
    vs[...] = (nn(nrm[...], wqkv[:, 512:768]) + row(11)).astype(bf16)

    def quadrant(p, b):
        col, line = p & 15, p >> 4
        left = jnp.where(line < lefts[b], 0, 1)
        right = jnp.where(line < rights[b], 2, 3)
        return jnp.where(col < cuts[b], left, right)

    for b in range(PAIR):
        rows = pl.ds(b * TOK, TOK)
        s = nt(qs[rows, :], ks[rows, :])
        qp = quadrant(lax.broadcasted_iota(jnp.int32, (TOK, 1), 0), b)
        qq = quadrant(lax.broadcasted_iota(jnp.int32, (1, TOK), 1), b)
        s = jnp.where(qp == qq, s, far_score)
        top = jnp.max(s, axis=1, keepdims=True)
        ex = jnp.exp((s - top) * (CH**-0.5))
        p = ex * (1.0 / jnp.sum(ex, axis=1, keepdims=True))
        prob[rows, :] = p
        mix[rows, :] = nn(p.astype(bf16), vs[rows, :]).astype(bf16)
    x3[...] = x2[...] + nn(mix[...], wo[...])
    forward_tables(3, x3, jnp.broadcast_to(row(0) + row(7) + row(12), (8, 256)), row(13), row(14))
    silu_pass(3, x3, sp4, xc3, False)

    z = nn(xc3[...], wr[...])
    us[0, pl.ds(8, ROWS), :] = z[:, 0:128]
    us[1, pl.ds(8, ROWS), :] = z[:, 128:256]
    lane = lax.broadcasted_iota(jnp.int32, (8, 128), 1)
    scale = scale_ref[0]
    for i in range(GRIDROWS):
        b, r = divmod(i, SIDE)
        ql, qr = quads(i)
        inl = scale_ref[8 + base * 4 + ql]
        inr = scale_ref[8 + base * 4 + qr]
        for h in range(2):
            at = 8 + i * 16 + h * 8
            rows = pl.ds(i * 16 + h * 8, 8)
            y = pltpu.roll(us[0, pl.ds(at, 8), :], 64, 1)
            if r > 0:
                y = y + us[0, pl.ds(at - 16, 8), :] * mvu[rows, :]
            if r < SIDE - 1:
                y = y + us[1, pl.ds(at + 16, 8), :] * mvd[rows, :]
            inside = jnp.where(onleftn[b][h], inl, inr)
            err = jnp.where(lane < PIX, (y - tg_ref[rows, :].astype(f32)) * inside, 0.0)
            lacc[...] += err * err
            xs[0, pl.ds(at, 8), :] = (err * scale).astype(bf16).astype(f32)
    for i in range(GRIDROWS):
        b, r = divmod(i, SIDE)
        tile0, tile1 = [], []
        for h in range(2):
            at = 8 + i * 16 + h * 8
            rows = pl.ds(i * 16 + h * 8, 8)
            t0 = pltpu.roll(xs[0, pl.ds(at, 8), :], 64, 1)
            if r < SIDE - 1:
                t0 = t0 + xs[0, pl.ds(at + 16, 8), :] * mvd[rows, :]
            t1 = jnp.zeros((8, 128), f32)
            if r > 0:
                t1 = xs[0, pl.ds(at - 16, 8), :] * mvu[rows, :]
            tile0.append(t0)
            tile1.append(t1)
        dyp[pl.ds(i * 16, 16), 0:128] = jnp.concatenate(tile0, axis=0).astype(bf16)
        dyp[pl.ds(i * 16, 16), 128:256] = jnp.concatenate(tile1, axis=0).astype(bf16)

    for dx in range(3):
        gr[pl.ds(dx * 256, 256), :] += nn(xc3[:, dx * 256 : (dx + 1) * 256].T, dyp[...])
    put_us(dyp[...], wrt)
    s1, s2 = crop_sums(lambda i, h: tap_back(i, h, sp4, x3))
    sum3, db, dg = backward_tables(3, s1, s2, row(13))
    gv[13] += dg
    gv[14] += db
    gv[12] += sum3
    for i in range(GRIDROWS):
        halves = []
        for h in range(2):
            d = norm_grad(3, i, h, x3)
            gtop[pl.ds(i * 16 + h * 8, 8), :] = d
            halves.append(d)
        dpc[pl.ds(i * 16, 16), 256:512] = jnp.concatenate(halves, axis=0).astype(bf16)
    ga[:, 768:1024] += nn(mix[...].T, dpc[:, 256:512])
    mix[...] = nn(dpc[:, 256:512], wot[...]).astype(bf16)
    for b in range(PAIR):
        rows = pl.ds(b * TOK, TOK)
        dm = mix[rows, :]
        p = prob[rows, :]
        da = nt(dm, vs[rows, :] * jnp.asarray(CH**-0.5, bf16))
        t = da * p
        ds = (t - p * jnp.sum(t, axis=1, keepdims=True)).astype(bf16)
        dv = nn(p.astype(bf16).T, dm)
        dq = nn(ds, ks[rows, :])
        dk = nn(ds.T, qs[rows, :])
        for k, d in ((10, dq), (11, dv)):
            gv[k] += jnp.sum(d.reshape(TOK // 8, 8, CH), axis=0)
        trip[rows, 0:256] = dq.astype(bf16)
        trip[rows, 256:512] = dk.astype(bf16)
        trip[rows, 512:768] = dv.astype(bf16)
    turned = nrm[...].T
    for k in range(3):
        ga[:, k * 256 : (k + 1) * 256] += nn(turned, trip[:, k * 256 : (k + 1) * 256])
    dys[...] = nn(trip[...], wat[...])

    def plain(i, h):
        rows = pl.ds(i * 16 + h * 8, 8)
        dy = dys[rows, :]
        return dy, dy * x2[rows, :]

    s1, s2 = crop_sums(plain)
    sum2, db, dg = backward_tables(2, s1, s2, row(8))
    gv[8] += dg
    gv[9] += db
    sum2 = sum2 + sum3
    gv[7] += sum2
    for i in range(GRIDROWS):
        halves = []
        for h in range(2):
            rows = pl.ds(i * 16 + h * 8, 8)
            d = norm_grad(2, i, h, x2) + gtop[rows, :]
            gres[rows, :] = d
            halves.append(d)
        spread_grad(i, jnp.concatenate(halves, axis=0))
    weight_grad(gk2, xv2, 768)
    put_us(dpc[...], wt2)
    s1, s2 = crop_sums(lambda i, h: tap_back(i, h, sp2, x1))
    sum1, db, dg = backward_tables(1, s1, s2, row(5))
    gv[5] += dg
    gv[6] += db
    gv[4] += sum1
    dtb[pl.ds(step * 8, 8), :] = sum1
    for i in range(GRIDROWS):
        spread_grad(i, jnp.concatenate([norm_grad(1, i, h, x1) for h in range(2)], axis=0))
    weight_grad(gk1, xv1, 768)
    put_us(dpc[...], wt1)
    s1, s2 = crop_sums(lambda i, h: tap_back(i, h, sp1, x0))
    sum0, db, dg = backward_tables(0, s1, s2, row(2))
    gv[2] += dg
    gv[3] += db
    gv[0] += sum0 + sum2
    for i in range(GRIDROWS):
        halves = [norm_grad(0, i, h, x0) + gres[pl.ds(i * 16 + h * 8, 8), :] for h in range(2)]
        dpc[pl.ds(i * 16, 16), 256:512] = jnp.concatenate(halves, axis=0).astype(bf16)
    gs[...] += nn(xt_ref[...].T, dpc[:, 256:512])

    @pl.when(step == last)
    def _():
        low = dtb[...].astype(bf16)
        hp = hpre[...]
        sg = jax.nn.sigmoid(hp)
        gp = nn((hp * sg).astype(bf16).T, low).astype(bf16)
        hg = nt(low, wpj[...]) * (sg * (1.0 + hp * (1.0 - sg)))
        ge = nn(feat_ref[...].T, hg.astype(bf16)).astype(bf16)
        rows = [jnp.sum(gv[4 if k == 1 else k], axis=0, keepdims=True) for k in range(15)]
        gnorm = jnp.concatenate(rows + [jnp.zeros((113, 256), f32)], axis=0).T.astype(bf16)
        gstem = gs[...].T.astype(bf16)
        lane = lax.broadcasted_iota(jnp.int32, (8, 128), 1)
        for f in range(VIRT):
            for dy in range(3):
                lo, hi = max(f * KROW, dy * 768), min((f + 1) * KROW, (dy + 1) * 768)
                if lo >= hi:
                    continue
                src = pl.ds(lo - dy * 768, hi - lo)
                dst = pl.ds(lo - f * KROW, hi - lo)
                out_ref[f, dst, 0:256] = gk1[src, dy * 256 : (dy + 1) * 256].astype(bf16)
                out_ref[f, dst, 256:512] = gk2[src, dy * 256 : (dy + 1) * 256].astype(bf16)
                part = gr[src, (dy // 2) * 128 : (dy // 2) * 128 + 128]
                if dy == 1:
                    part = pltpu.roll(part, 64, 1)
                keep = lax.broadcasted_iota(jnp.int32, part.shape, 1) < PIX
                out_ref[f, dst, 512:640] = jnp.where(keep, part, 0.0).astype(bf16)
            at = f * AROW
            a1, a2 = KROW, KROW + AROW
            out_ref[f, a1:a2, 0:512] = ga[at : at + AROW, 0:512].astype(bf16)
            out_ref[f, a2 : a2 + AROW, 0:512] = ga[at : at + AROW, 512:1024].astype(bf16)
            out_ref[f, a1:a2, 512:640] = gstem[at : at + AROW, :]
            out_ref[f, a2 : a2 + AROW, 512:640] = gnorm[at : at + AROW, :]
            p0 = KROW + 2 * AROW
            out_ref[f, p0 : p0 + PROW, 0:256] = gp[f * 2 * PROW : f * 2 * PROW + PROW, :]
            out_ref[f, p0 : p0 + PROW, 256:512] = gp[f * 2 * PROW + PROW : (f + 1) * 2 * PROW, :]
            e0 = p0 + PROW
            out_ref[f, e0 : e0 + EROW, 0:512] = ge[f * EROW : (f + 1) * EROW, :]
            out_ref[f, p0 : e0 + EROW, 512:640] = jnp.zeros((PROW + EROW, 128), bf16)
        loss_ref[...] = lacc[...]


def run_step(packed, quad, geo, scal, feat, xt, tg, inv, cnt):
    canvases = xt.shape[0] // TOK
    steps = canvases // PAIR
    whole = pl.BlockSpec(memory_space=pltpu.VMEM)
    smem = pl.BlockSpec(memory_space=pltpu.SMEM)

    def rows(n, lanes):
        return pl.BlockSpec((n, lanes), lambda i, *_: (i, 0))

    def v(shape, dtype=f32):
        return pltpu.VMEM(shape, dtype)

    scratch = [
        v((2304, 256), bf16), v((2304, 256), bf16), v((768, 768), bf16), v((768, 768), bf16),
        v((768, 256), bf16), v((256, 768), bf16), v((256, 768), bf16), v((768, 256), bf16),
        v((256, 256), bf16), v((256, 256), bf16), v((128, 256), bf16), v((512, 256), bf16), v((128, 512), bf16),
        v((16, 256)), v((4 * canvases, 256)), v((4 * canvases, 512)), v((2304, 128), bf16),
        v((768, 768)), v((768, 768)), v((768, 256)), v((256, 1024)), v((128, 256)), v((15, 8, 256)),
        v((4 * canvases, 256)), v((8, 128)),
        v((ROWS, 256)), v((ROWS, 256)), v((ROWS, 256)), v((ROWS, 256)),
        v((ROWS, 256)), v((ROWS, 256)), v((ROWS, 256)),
        v((2, ROWS + 16, 128)), v((6, ROWS + 16, 128)),
        v((ROWS, 2304), bf16), v((ROWS, 2304), bf16), v((ROWS, 768), bf16),
        v((ROWS, 256), bf16), v((ROWS, 256), bf16), v((ROWS, 256), bf16), v((ROWS, 256), bf16),
        v((ROWS, 256)), v((ROWS, 256), bf16), v((ROWS, 256)), v((ROWS, 256)), v((ROWS, 256)),
        v((ROWS, 768), bf16), v((ROWS, 256), bf16), v((ROWS, 768), bf16),
        v((ROWS, 128)), v((ROWS, 128)),
        v((7, 8, 8, 256)), v((4, 4, 8, 256)), v((PAIR, 2, 2, 17, 8, 256)),
    ]
    return pl.pallas_call(
        step_kernel,
        grid_spec=pltpu.PrefetchScalarGridSpec(
            num_scalar_prefetch=2,
            grid=(steps,),
            in_specs=[
                smem, whole, whole, rows(ROWS, 128), rows(ROWS, 128), rows(8, 256), rows(8, 256),
            ],
            out_specs=[whole, whole],
            scratch_shapes=scratch,
        ),
        out_shape=[
            jax.ShapeDtypeStruct((VIRT, PACKED, 640), bf16),
            jax.ShapeDtypeStruct((8, 128), f32),
        ],
        compiler_params=pltpu.CompilerParams(
            dimension_semantics=("arbitrary",), vmem_limit_bytes=60 * 1024 * 1024
        ),
    )(quad, geo, scal, packed, feat, xt, tg, inv, cnt)


def signal_table():
    beta = np.linspace(0.0001, 0.02, TSTEPS, dtype=np.float64)
    return np.exp(np.cumsum(np.log(1.0 - beta))).astype(np.float32)


def time_features(time_steps):
    half_width = TEMB // 2
    frequency = jnp.exp(-math.log(10000.0) * jnp.arange(half_width, dtype=f32) / (half_width - 1))
    angles = time_steps.astype(f32)[..., None] * frequency
    return jnp.concatenate([jnp.sin(angles), jnp.cos(angles)], axis=-1)


def to_patches(image):
    blocked = image.reshape(-1, 3, SIDE, PATCH, SIDE, PATCH).transpose(0, 2, 4, 1, 3, 5)
    flat = blocked.reshape(-1, PIX)
    return jnp.pad(flat, ((0, 0), (0, 128 - PIX)))


def prepare(clean, noise, lab, time_steps):
    canvases = lab.shape[0]
    cut = jnp.sum(jnp.all(lab == lab[:, :, :1], axis=1).astype(jnp.int32), axis=1)
    left = jnp.sum((lab[:, :, 0] == lab[:, :1, 0]).astype(jnp.int32), axis=1)
    right = jnp.sum((lab[:, :, -1] == lab[:, :1, -1]).astype(jnp.int32), axis=1)
    own = jnp.stack([lab[:, 0, 0], lab[:, -1, 0], lab[:, 0, -1], lab[:, -1, -1]], axis=1)
    area = jnp.stack(
        [cut * left, cut * (SIDE - left), (SIDE - cut) * right, (SIDE - cut) * (SIDE - right)], axis=1
    ).astype(f32)
    geo = jnp.stack([cut, left, right] + [jnp.zeros_like(cut)] * 5, axis=1).reshape(-1)
    line = jnp.arange(SIDE, dtype=jnp.int32)
    first = (4 * (jnp.arange(canvases, dtype=jnp.int32) % PAIR))[:, None]
    quad = jnp.stack(
        [
            first + (line >= left[:, None]).astype(jnp.int32),
            first + 2 + (line >= right[:, None]).astype(jnp.int32),
        ],
        axis=-1,
    ).reshape(-1)
    hit = own[..., None] == jnp.arange(1, CROPS + 1, dtype=jnp.int32)
    times = jnp.sum(jnp.where(hit, time_steps[:, None, :], 0), axis=-1)
    feat = time_features(times).astype(bf16).reshape(-1, TEMB)
    picked = time_steps[..., None] == jnp.arange(TSTEPS, dtype=jnp.int32)
    chosen = jnp.sum(jnp.where(picked, jnp.asarray(signal_table()), 0.0), axis=-1)
    on_cell = lab[..., None] == jnp.arange(1, CROPS + 1, dtype=jnp.int32)

    def per_cell(values):
        cells = jnp.sum(jnp.where(on_cell, values[:, None, None, :], 0.0), axis=-1)
        return cells.reshape(canvases, 1, SIDE, 1, SIDE, 1)

    def grid(image):
        return image.reshape(canvases, 3, SIDE, PATCH, SIDE, PATCH)

    mixed = per_cell(jnp.sqrt(chosen)) * grid(clean).astype(f32) + per_cell(jnp.sqrt(1.0 - chosen)) * grid(noise).astype(f32)
    xt = to_patches(mixed.astype(bf16))
    tg = to_patches(noise)
    inv = jnp.broadcast_to((1.0 / jnp.maximum(area, 1.0)).reshape(-1, 1), (4 * canvases, CH))
    cnt = jnp.broadcast_to(area.reshape(-1, 1), (4 * canvases, CH))
    inside = (own > 0).astype(f32).reshape(-1)
    return quad, geo, inside, feat, xt, tg, inv, cnt


def on_device(clean, noise, crop_labels, time_steps, *state):
    masters, moments, averages = state[0:7], state[7:14], state[14:21]
    shards = lax.axis_size("fsdp")
    own = pack_rows([w.astype(bf16) for w in masters])
    packed = lax.all_gather(own, "fsdp", axis=0, tiled=False)
    count = lax.psum(PATCH * PATCH * jnp.sum((crop_labels > 0).astype(f32)), ("dp", "fsdp"))
    quad, geo, inside, feat, xt, tg, inv, cnt = prepare(clean, noise, crop_labels, time_steps)
    scal = jnp.concatenate([jnp.full((8,), 2.0 / count, f32), inside])
    grads, loss = run_step(repack(packed, shards, VIRT), quad, geo, scal, feat, xt, tg, inv, cnt)
    total_loss = lax.psum(jnp.sum(loss), ("dp", "fsdp"))
    mine = lax.psum_scatter(repack(grads, VIRT, shards), "fsdp", scatter_dimension=0, tiled=False)
    summed = lax.psum(mine, "dp").astype(f32)
    cut = [masters[1].shape[0], masters[0].shape[0], masters[3].shape[0], masters[2].shape[0]]
    grads = unpack_rows(summed, *cut)
    rate = lr_scale * jnp.sqrt(count)
    moment_next = tuple(momentum_rate * m + g for m, g in zip(moments, grads))
    master_next = tuple(w - rate * (g + momentum_rate * m) for w, g, m in zip(masters, grads, moment_next))
    average_next = tuple(average_rate * a + (1.0 - average_rate) * w for a, w in zip(averages, master_next))
    return (total_loss / count,) + moment_next + master_next + average_next


def solution(mesh):
    split = P(("dp", "fsdp"), None)
    in_specs = (split, split, P(("dp", "fsdp"), None, None), split) + (P("fsdp", None),) * 21
    out_specs = (P(),) + (P("fsdp", None),) * 21
    return jax.shard_map(on_device, mesh=mesh, in_specs=in_specs, out_specs=out_specs, check_vma=False)
```

```python
import functools
import math

import jax
import jax.numpy as jnp
import numpy as np
from jax import lax
from jax.experimental import pallas as pl
from jax.experimental.pallas import tpu as pltpu
from jax.sharding import PartitionSpec as P

GROUPS = 32
TEMB = 128
SIDE = 16
PATCH = 4
CROPS = 4
TSTEPS = 1000
TOK = SIDE * SIDE
CH = 256
PIX = 3 * PATCH * PATCH
PAIR = 4
ROWS = PAIR * TOK
VIRT = 8
TAIL = 48

eps_norm = 1e-05
lr_scale = 0.01
momentum_rate = 0.5
average_rate = 0.5
far_score = -1e30
f32 = jnp.float32
bf16 = jnp.bfloat16


def pad_to(value, rows, lanes):
    return jnp.pad(value, ((0, rows - value.shape[0]), (0, lanes - value.shape[1])))


def pack_rows(parts):
    stem, kernels, embed, project, attention, readout, norm = parts
    half = project.shape[0] // 2
    small = jnp.concatenate([pad_to(stem, 32, 128), pad_to(norm.T, 16, 128)], axis=0)
    tail = jnp.concatenate([pad_to(readout.T, TAIL, 384), small], axis=1)
    rows = [kernels, attention[:, :512], attention[:, 512:]]
    rows += [jnp.concatenate([project[:half], project[half:]], axis=1), embed, tail]
    rows = jnp.concatenate(rows, axis=0)
    return pad_to(rows, -(-rows.shape[0] // 8) * 8, 512)


def unpack_rows(rows, k, a, p, e):
    half = p // 2
    at = [0, k, k + a, k + 2 * a, k + 2 * a + half, k + 2 * a + half + e, k + 2 * a + half + e + TAIL]
    kernels, left, right, halves, embed, tail = [rows[at[i] : at[i + 1]] for i in range(6)]
    project = jnp.concatenate([halves[:, :256], halves[:, 256:]], axis=0)
    stem, norm = tail[:a, 384 : 384 + PIX], tail[32 : 32 + 15, 384 : 384 + a].T
    return stem, kernels, embed, project, jnp.concatenate([left, right], axis=1), tail[:, :k].T, norm


def repack(packed, parts_now, parts_next):
    if parts_now == parts_next:
        return packed
    cut = [n // parts_now for n in (9 * CH, CH, 2 * CH, CH // 2)]
    pieces = jax.vmap(lambda rows: unpack_rows(rows, *cut))(packed)
    whole = [piece.reshape(-1, piece.shape[-1]) for piece in pieces]
    split = [piece.reshape(parts_next, -1, piece.shape[-1]) for piece in whole]
    return jax.vmap(lambda *p: pack_rows(p))(*split)


KROW = 9 * CH // VIRT
AROW = CH // VIRT
PROW = CH // VIRT
EROW = TEMB // VIRT
TROW = KROW + 2 * AROW + PROW + EROW
PACKED = TROW + TAIL


def lane_groups(value):
    lane = lax.broadcasted_iota(jnp.int32, (8, 128), 1)
    tiles = []
    for t in range(2):
        x = value[:, t * 128 : (t + 1) * 128]
        for s in (1, 2, 4):
            x = x + jnp.where((lane & s) == 0, pltpu.roll(x, 128 - s, 1), pltpu.roll(x, s, 1))
        tiles.append(x)
    return jnp.concatenate(tiles, axis=1)


def quad_rows(q0, q1, q2, q3):
    sub = lax.broadcasted_iota(jnp.int32, (8, 128), 0)
    tiles = []
    for t in range(2):
        a, b, c, d = [q[:, t * 128 : (t + 1) * 128] for q in (q0, q1, q2, q3)]
        low = sub < 4
        u = jnp.where(low, a, pltpu.roll(b, 4, 0)) + jnp.where(low, pltpu.roll(a, 4, 0), b)
        v = jnp.where(low, c, pltpu.roll(d, 4, 0)) + jnp.where(low, pltpu.roll(c, 4, 0), d)
        even = (sub & 2) == 0
        w = jnp.where(even, u, pltpu.roll(v, 2, 0)) + jnp.where(even, pltpu.roll(u, 6, 0), v)
        w = w + jnp.where((sub & 1) == 0, pltpu.roll(w, 7, 0), pltpu.roll(w, 1, 0))
        tiles.append(w)
    return jnp.concatenate(tiles, axis=1)


QUAD_ROW = (0, 4, 2, 6)


def nt(a, b):
    return lax.dot_general(a, b, (((1,), (1,)), ((), ())), preferred_element_type=f32)


def nn(a, b):
    return lax.dot_general(a, b, (((1,), (0,)), ((), ())), preferred_element_type=f32)


PADROWS = TOK + 16


def scratch_list(canvases):
    n = 8 * canvases
    items = [
        ("wk1", (2304, 256), bf16), ("wk2", (2304, 256), bf16), ("wt1", (768, 768), bf16), ("wt2", (768, 768), bf16),
        ("wr", (768, 256), bf16), ("wrt", (256, 768), bf16), ("wqkv", (256, 768), bf16), ("wat", (768, 256), bf16),
        ("wo", (256, 256), bf16), ("wot", (256, 256), bf16), ("ws", (128, 256), bf16), ("wpj", (512, 256), bf16),
        ("wem", (128, 512), bf16), ("vec", (16, 256), f32), ("tbs", (n, 256), f32), ("hpre", (n, 512), f32),
        ("wrn", (2304, 128), bf16), ("grn", (2304 + 96, 128), f32), ("xt", (ROWS, 128), bf16),
        ("gk1", (768, 768), f32), ("gk2", (768, 768), f32), ("gr", (768, 256), f32), ("ga", (256, 1024), f32),
        ("gs", (128, 256), f32), ("gv", (15, 8, 256), f32), ("dtb", (n, 256), f32), ("lacc", (8, 128), f32),
        ("x0", (ROWS, 256), f32), ("x1", (ROWS, 256), f32), ("x2", (ROWS, 256), f32), ("x3", (ROWS, 256), f32),
        ("sp1", (ROWS, 256), f32), ("sp2", (ROWS, 256), f32), ("sp4", (ROWS, 256), f32),
        ("xs", (PAIR, 2, PADROWS, 128), f32), ("us", (PAIR, 6, PADROWS, 128), f32),
        ("side", (ROWS, 1536), bf16),
        ("xc1", (ROWS, 768), bf16), ("xc2", (ROWS, 768), bf16), ("xc3", (ROWS, 768), bf16),
        ("nrm", (ROWS, 256), bf16), ("qs", (ROWS, 256), bf16), ("ks", (ROWS, 256), bf16), ("vs", (ROWS, 256), bf16),
        ("prob", (ROWS, 256), f32), ("mix", (ROWS, 256), bf16), ("dmx", (ROWS, 256), bf16), ("dpo", (ROWS, 256), bf16),
        ("gtop", (ROWS, 256), f32), ("dys", (ROWS, 256), f32),
        ("dpc1", (ROWS, 768), bf16), ("dpc2", (ROWS, 768), bf16), ("dps", (ROWS, 256), bf16),
        ("dyp", (ROWS, 256), bf16), ("trip", (ROWS, 768), bf16),
        ("mvu", (ROWS, 128), f32), ("mvd", (ROWS, 128), f32), ("mbu", (ROWS, 128), bf16), ("mbd", (ROWS, 128), bf16),
        ("ctab", (PAIR, 4, 4, 8, 256), f32),
    ]
    for b in range(PAIR):
        items += [(f"pref{b}", (2, 2, 17, 8, 256), f32)]
        items += [(f"tab{b}_{slot}", (4, 8, 256), f32) for slot in range(7)]
    return items


def step_kernel(names, *refs):
    quad_ref, geo_ref, scale_ref, wp_ref, feat_ref, cp_ref, tg_ref, inv_ref, cnt_ref, out_ref, loss_ref = refs[:11]
    S = dict(zip(names, refs[11:]))
    wk1, wk2, wt1, wt2, wr, wrt, wqkv, wat, wo, wot = [S[k] for k in ("wk1", "wk2", "wt1", "wt2", "wr", "wrt", "wqkv", "wat", "wo", "wot")]
    ws, wpj, wem, vec, tbs, hpre, wrn = [S[k] for k in ("ws", "wpj", "wem", "vec", "tbs", "hpre", "wrn")]
    gk1, gk2, gr, ga, gs, gv, dtb, lacc = [S[k] for k in ("gk1", "gk2", "gr", "ga", "gs", "gv", "dtb", "lacc")]
    x0, x1, x2, x3, sp1, sp2, sp4, xs, us = [S[k] for k in ("x0", "x1", "x2", "x3", "sp1", "sp2", "sp4", "xs", "us")]
    side, xc1, xc2, xc3, nrm, qs, ks, vs = [S[k] for k in ("side", "xc1", "xc2", "xc3", "nrm", "qs", "ks", "vs")]
    prob, mix, dmx, dpo, gtop, dys = [S[k] for k in ("prob", "mix", "dmx", "dpo", "gtop", "dys")]
    dpc1, dpc2, dps, dyp, trip = [S[k] for k in ("dpc1", "dpc2", "dps", "dyp", "trip")]
    mvu, mvd, mbu, mbd, ctab = [S[k] for k in ("mvu", "mvd", "mbu", "mbd", "ctab")]
    grn, xt_ref = S["grn"], S["xt"]
    pref = [S[f"pref{b}"] for b in range(PAIR)]
    tab = [[S[f"tab{b}_{slot}"] for slot in range(7)] for b in range(PAIR)]
    step = pl.program_id(0)
    last = pl.num_programs(0) - 1
    canvases = tbs.shape[0] // 8

    @pl.when(step == 0)
    def _():
        for f in range(VIRT):
            wk1[pl.ds(f * KROW, KROW), :] = wp_ref[f, :KROW, 0:256]
            wk2[pl.ds(f * KROW, KROW), :] = wp_ref[f, :KROW, 256:512]
            back = wp_ref[f, TROW:PACKED, 0:384].astype(f32)
            back = jnp.concatenate([back, jnp.zeros((128 - TAIL, 384), f32)], axis=0).T
            wrn[pl.ds(f * KROW, KROW), :] = back[:KROW, :].astype(bf16)
            att = slice(KROW, KROW + AROW)
            att2 = slice(KROW + AROW, KROW + 2 * AROW)
            wqkv[pl.ds(f * AROW, AROW), 0:512] = wp_ref[f, att, 0:512]
            wqkv[pl.ds(f * AROW, AROW), 512:768] = wp_ref[f, att2, 0:256]
            wo[pl.ds(f * AROW, AROW), :] = wp_ref[f, att2, 256:512]
            pr = KROW + 2 * AROW
            wpj[pl.ds(f * 2 * PROW, PROW), :] = wp_ref[f, pr : pr + PROW, 0:256]
            wpj[pl.ds(f * 2 * PROW + PROW, PROW), :] = wp_ref[f, pr : pr + PROW, 256:512]
            wem[pl.ds(f * EROW, EROW), :] = wp_ref[f, pr + PROW : pr + PROW + EROW, 0:512]
        stem = jnp.concatenate([wp_ref[f, TROW : TROW + 32, 384:512] for f in range(VIRT)], axis=0)
        ws[...] = stem.T
        for t in range(2):
            tile = jnp.zeros((16, 128), f32)
            for j in range(4):
                part = wp_ref[4 * t + j, TROW + 32 : PACKED, 384:512].astype(f32)
                part = jnp.where(lax.broadcasted_iota(jnp.int32, (16, 128), 1) < AROW, part, 0.0)
                tile = tile + (pltpu.roll(part, j * AROW, 1) if j else part)
            vec[:, t * 128 : (t + 1) * 128] = tile
        for dy in range(3):
            for dx in range(3):
                rows = pl.ds((dy * 3 + dx) * 256, 256)
                wt1[pl.ds(dy * 256, 256), dx * 256 : (dx + 1) * 256] = wk1[rows, :].T
                wt2[pl.ds(dy * 256, 256), dx * 256 : (dx + 1) * 256] = wk2[rows, :].T
        for j in range(3):
            wat[pl.ds(j * 256, 256), :] = wqkv[:, j * 256 : (j + 1) * 256].T
        wot[...] = wo[...].T
        for dx in range(3):
            rows = [wrn[pl.ds(dy * 768 + dx * 256, 256), :].astype(f32) for dy in range(3)]
            tile0 = (rows[0] + pltpu.roll(rows[1], 64, 1)).astype(bf16)
            tile1 = rows[2].astype(bf16)
            wr[pl.ds(dx * 256, 256), 0:128] = tile0
            wr[pl.ds(dx * 256, 256), 128:256] = tile1
            wrt[0:128, dx * 256 : (dx + 1) * 256] = tile0.T
            wrt[128:256, dx * 256 : (dx + 1) * 256] = tile1.T
        hp = nn(feat_ref[...], wem[...])
        hpre[...] = hp
        tbs[...] = nn(jax.nn.silu(hp).astype(bf16), wpj[...]) + vec[1:2, :]
        for ref in [gk1, gk2, gr, ga, gs, gv, lacc, grn] + pref:
            ref[...] = jnp.zeros_like(ref)
        for b in range(PAIR):
            side[pl.ds(b * TOK, 16), 0:768] = jnp.zeros((16, 768), bf16)
            side[pl.ds(b * TOK + TOK - 16, 16), 768:1536] = jnp.zeros((16, 768), bf16)
        for ref in (dpc1, dpc2):
            for b in range(PAIR):
                ref[pl.ds(b * TOK + TOK - 16, 16), 0:256] = jnp.zeros((16, 256), bf16)
                ref[pl.ds(b * TOK, 16), 512:768] = jnp.zeros((16, 256), bf16)

    base = step * PAIR
    cuts = [geo_ref[(base + b) * 8] for b in range(PAIR)]
    lefts = [geo_ref[(base + b) * 8 + 1] for b in range(PAIR)]
    rights = [geo_ref[(base + b) * 8 + 2] for b in range(PAIR)]
    iota8 = lax.broadcasted_iota(jnp.int32, (8, 256), 0)
    iota8n = lax.broadcasted_iota(jnp.int32, (8, 128), 0)
    onleft = [[iota8 < (cuts[b] - 8 * h) for h in range(2)] for b in range(PAIR)]
    onleftn = [[iota8n < (cuts[b] - 8 * h) for h in range(2)] for b in range(PAIR)]
    hasl = [[(iota8n + 8 * h != 0) & (iota8n + 8 * h != cuts[b]) for h in range(2)] for b in range(PAIR)]
    hasr = [[(iota8n + 8 * h != 15) & (iota8n + 8 * h != cuts[b] - 1) for h in range(2)] for b in range(PAIR)]
    scale = scale_ref[0]
    lane = lax.broadcasted_iota(jnp.int32, (8, 128), 1)
    fill = []

    def row(k):
        return vec[k : k + 1, :]

    def stream(b):
        r0 = b * TOK
        mine = pl.ds(r0, TOK)
        inv = inv_ref[pl.ds(b * 8, 8), :]
        cnt = cnt_ref[pl.ds(b * 8, 8), :]

        def at(r, h=0, n=8):
            return pl.ds(r0 + r * 16 + h * 8, n)

        def quads(r):
            k = ((base + b) * SIDE + r) * 2
            return quad_ref[k], quad_ref[k + 1]

        def masks():
            for r in range(SIDE):
                upl = ((lefts[b] != r) & (r > 0)).astype(f32)
                upr = ((rights[b] != r) & (r > 0)).astype(f32)
                dnl = ((lefts[b] != r + 1) & (r < SIDE - 1)).astype(f32)
                dnr = ((rights[b] != r + 1) & (r < SIDE - 1)).astype(f32)
                up = jnp.concatenate([jnp.where(onleftn[b][h], upl, upr) for h in range(2)], axis=0)
                dn = jnp.concatenate([jnp.where(onleftn[b][h], dnl, dnr) for h in range(2)], axis=0)
                mvu[at(r, 0, 16), :] = up
                mvd[at(r, 0, 16), :] = dn
                mbu[at(r, 0, 16), :] = up.astype(bf16)
                mbd[at(r, 0, 16), :] = dn.astype(bf16)
                ql, qr = quads(r)
                level = 8 + 4 * canvases + (base + b) * 4
                al, ar = scale_ref[level + ql], scale_ref[level + qr]
                sl, sr = scale_ref[level + 4 * canvases + ql], scale_ref[level + 4 * canvases + qr]
                mixed = []
                for h in range(2):
                    m = onleftn[b][h]
                    noisy = jnp.where(m, sl, sr) * tg_ref[at(r, h), :]
                    mixed.append(jnp.where(m, al, ar) * cp_ref[at(r, h), :] + noisy)
                xt_ref[at(r, 0, 16), :] = jnp.concatenate(mixed, axis=0).astype(bf16)
            yield 100

        def put_table(slot, table):
            for q in range(4):
                k = QUAD_ROW[q]
                tab[b][slot][q] = jnp.broadcast_to(table[k : k + 1, :], (8, 256))

        def pick(slot, r):
            left, right = quads(r)
            return tab[b][slot][left], tab[b][slot][right]

        def crop_sums(values_of):
            total = [None, None]
            left = [None, None]
            p = pref[b]
            for r in range(SIDE):
                halves = [values_of(r, h) for h in range(2)]
                for j in range(2):
                    a0, a1 = halves[0][j], halves[1][j]
                    lp = jnp.where(onleft[b][0], a0, 0.0) + jnp.where(onleft[b][1], a1, 0.0)
                    tp = a0 + a1
                    left[j] = lp if r == 0 else left[j] + lp
                    total[j] = tp if r == 0 else total[j] + tp
                    p[j, 0, r + 1] = left[j]
                    p[j, 1, r + 1] = total[j]
                yield 16
            got = []
            for j in range(2):
                q0 = p[j, 0, lefts[b]]
                q1 = left[j] - q0
                q2 = p[j, 1, rights[b]] - p[j, 0, rights[b]]
                q3 = (total[j] - left[j]) - q2
                got.append(quad_rows(q0, q1, q2, q3))
            yield 100
            return got

        def forward_tables(n, xref, bias, gain, shift):
            def both(r, h):
                x = xref[at(r, h), :]
                return x, x * x

            s1, s2 = yield from crop_sums(both)
            own = s1 * inv
            mean = lane_groups(own + bias) * 0.125
            apart = own + bias - mean
            var = lane_groups(jnp.maximum(s2 * inv - own * own, 0.0) + apart * apart) * 0.125
            rs = lax.rsqrt(var + eps_norm)
            a = rs * gain
            e = bias - mean
            put_table(n, a)
            put_table(4, e * a + shift)
            ctab[b, n, 0] = a
            ctab[b, n, 1] = rs
            ctab[b, n, 2] = e
            ctab[b, n, 3] = s1
            yield 250

        def backward_tables(n, s1, s2, gain):
            a, rs, e, sx = [ctab[b, n, j] for j in range(4)]
            sn = rs * (s2 + e * s1)
            m1 = lane_groups(gain * s1 * inv) * 0.125
            m2 = lane_groups(gain * sn * inv) * 0.125
            v = rs * rs * m2
            u = rs * m1 + e * v
            put_table(5, v)
            put_table(6, u)
            return a * s1 - v * sx - cnt * u, s1, sn

        def silu_pass(n, xref, spref, xcref, vertical):
            for r in range(SIDE):
                al, ar = pick(n, r)
                dl, dr = pick(4, r)
                for h in range(2):
                    x = xref[at(r, h), :]
                    y = x * jnp.where(onleft[b][h], al, ar) + jnp.where(onleft[b][h], dl, dr)
                    hy = 0.5 * y
                    t = jnp.tanh(hy)
                    act = hy * t + hy
                    sig = 0.5 * t + 0.5
                    spref[at(r, h), :] = sig + act - act * sig
                    for c in range(2):
                        xs[b, c, pl.ds(8 + r * 16 + h * 8, 8), :] = act[:, c * 128 : (c + 1) * 128]
                k0 = 8 + r * 16
                for c in range(2):
                    taps = []
                    for dx in (-1, 0, 1):
                        pieces = []
                        for h in range(2):
                            piece = xs[b, c, pl.ds(k0 + h * 8 + dx, 8), :]
                            if dx == -1:
                                piece = jnp.where(hasl[b][h], piece, 0.0)
                            if dx == 1:
                                piece = jnp.where(hasr[b][h], piece, 0.0)
                            pieces.append(piece)
                        taps.append(jnp.concatenate(pieces, axis=0).astype(bf16))
                    for k, tap in enumerate(taps):
                        lanes = slice(k * 256 + c * 128, k * 256 + c * 128 + 128)
                        low = slice(768 + lanes.start, 768 + lanes.stop)
                        xcref[at(r, 0, 16), lanes] = tap
                        if vertical and r < SIDE - 1:
                            side[at(r + 1, 0, 16), lanes] = tap * mbu[at(r + 1, 0, 16), :]
                        if vertical and r > 0:
                            side[at(r - 1, 0, 16), low] = tap * mbd[at(r - 1, 0, 16), :]
                yield 30

        def spread_grad(dpc, r, value):
            low = value.astype(bf16)
            dpc[at(r, 0, 16), 256:512] = low
            for c in range(2):
                part = low[:, c * 128 : (c + 1) * 128]
                if r > 0:
                    dpc[at(r - 1, 0, 16), c * 128 : c * 128 + 128] = part * mbd[at(r - 1, 0, 16), :]
                if r < SIDE - 1:
                    dpc[at(r + 1, 0, 16), 512 + c * 128 : 640 + c * 128] = part * mbu[at(r + 1, 0, 16), :]

        def tap_back(spref, xref):
            def values(r, h):
                k = 8 + r * 16 + h * 8
                cols = []
                for c in range(2):
                    d = us[b, 2 + c, pl.ds(k, 8), :]
                    d = d + jnp.where(hasr[b][h], us[b, c, pl.ds(k + 1, 8), :], 0.0)
                    d = d + jnp.where(hasl[b][h], us[b, 4 + c, pl.ds(k - 1, 8), :], 0.0)
                    cols.append(d)
                dy = jnp.concatenate(cols, axis=1) * spref[at(r, h), :]
                dys[at(r, h), :] = dy
                return dy, dy * xref[at(r, h), :]

            return values

        def norm_grad(n, r, h, xref):
            m = onleft[b][h]
            al, ar = pick(n, r)
            vl, vr = pick(5, r)
            ul, ur = pick(6, r)
            dx = dys[at(r, h), :] * jnp.where(m, al, ar) - xref[at(r, h), :] * jnp.where(m, vl, vr)
            return dx - jnp.where(m, ul, ur)

        def nine(xcref):
            return jnp.concatenate([side[mine, 0:768], xcref[mine, :], side[mine, 768:1536]], axis=1)

        def put_us(lhs, rhs_ref):
            for dx in range(3):
                u = nn(lhs, rhs_ref[:, dx * 256 : (dx + 1) * 256])
                for c in range(2):
                    us[b, dx * 2 + c, pl.ds(8, TOK), :] = u[:, c * 128 : (c + 1) * 128]
                yield 64 * (lhs.shape[1] // 256)

        def later(job):
            if b % 2:
                job(pl.ds(r0 - TOK, 2 * TOK))

        def weight_grad(acc, xref, dref, width):
            def job(two):
                for dx in range(3):
                    turned = []

                    def one(dy, dx=dx, turned=turned):
                        if not turned:
                            turned.append(xref[two, dx * 256 : (dx + 1) * 256].T)
                        cols = slice(dy * 256, (dy + 1) * 256)
                        acc[pl.ds(dx * 256, 256), cols] += nn(turned[0], dref[two, cols])

                    for dy in range(width):
                        fill.append(lambda dy=dy, one=one: one(dy))

            later(job)

        yield from masks()
        x0[mine, :] = nn(xt_ref[mine, :], ws[...])
        yield 128
        yield from forward_tables(0, x0, jnp.broadcast_to(row(0), (8, 256)), row(2), row(3))
        yield from silu_pass(0, x0, sp1, xc1, True)
        x1[mine, :] = nn(nine(xc1), wk1[...])
        yield 128 * 9
        bias1 = tbs[pl.ds((base + b) * 8, 8), :] + row(4)
        yield from forward_tables(1, x1, bias1, row(5), row(6))
        yield from silu_pass(1, x1, sp2, xc2, True)
        x2[mine, :] = x0[mine, :] + nn(nine(xc2), wk2[...])
        yield 128 * 9
        yield from forward_tables(2, x2, jnp.broadcast_to(row(0) + row(7), (8, 256)), row(8), row(9))
        for r in range(SIDE):
            al, ar = pick(2, r)
            dl, dr = pick(4, r)
            halves = []
            for h in range(2):
                x = x2[at(r, h), :]
                halves.append(x * jnp.where(onleft[b][h], al, ar) + jnp.where(onleft[b][h], dl, dr))
            nrm[at(r, 0, 16), :] = jnp.concatenate(halves, axis=0).astype(bf16)
            yield 10
        ks[mine, :] = nn(nrm[mine, :], wqkv[:, 256:512]).astype(bf16)
        qs[mine, :] = (nn(nrm[mine, :], wqkv[:, 0:256]) + row(10)).astype(bf16)
        vs[mine, :] = (nn(nrm[mine, :], wqkv[:, 512:768]) + row(11)).astype(bf16)
        yield 128 * 2

        def quadrant(p):
            col, line = p & 15, p >> 4
            left = jnp.where(line < lefts[b], 0, 1)
            right = jnp.where(line < rights[b], 2, 3)
            return jnp.where(col < cuts[b], left, right)

        qq = quadrant(lax.broadcasted_iota(jnp.int32, (1, TOK), 1))
        part = 64
        scores = []
        for k in range(TOK // part):
            scores.append(nt(qs[pl.ds(r0 + k * part, part), :], ks[mine, :]))
        yield 128
        lows = []
        for k in range(TOK // part):
            rows = pl.ds(r0 + k * part, part)
            qp = quadrant(k * part + lax.broadcasted_iota(jnp.int32, (part, 1), 0))
            s = jnp.where(qp == qq, scores[k], far_score)
            top = jnp.max(s, axis=1, keepdims=True)
            ex = jnp.exp((s - top) * (CH**-0.5))
            p = ex * (1.0 / jnp.sum(ex, axis=1, keepdims=True))
            prob[rows, :] = p
            lows.append(p.astype(bf16))
            yield 60
        mix[mine, :] = nn(jnp.concatenate(lows, axis=0), vs[mine, :]).astype(bf16)
        yield 128
        x3[mine, :] = x2[mine, :] + nn(mix[mine, :], wo[...])
        yield 128
        yield from forward_tables(3, x3, jnp.broadcast_to(row(0) + row(7) + row(12), (8, 256)), row(13), row(14))
        yield from silu_pass(3, x3, sp4, xc3, False)

        z = nn(xc3[mine, :], wr[...])
        us[b, 0, pl.ds(8, TOK), :] = z[:, 0:128]
        us[b, 1, pl.ds(8, TOK), :] = z[:, 128:256]
        yield 128 * 3
        for r in range(SIDE):
            ql, qr = quads(r)
            inl = scale_ref[8 + (base + b) * 4 + ql]
            inr = scale_ref[8 + (base + b) * 4 + qr]
            for h in range(2):
                k = 8 + r * 16 + h * 8
                y = pltpu.roll(us[b, 0, pl.ds(k, 8), :], 64, 1)
                if r > 0:
                    y = y + us[b, 0, pl.ds(k - 16, 8), :] * mvu[at(r, h), :]
                if r < SIDE - 1:
                    y = y + us[b, 1, pl.ds(k + 16, 8), :] * mvd[at(r, h), :]
                inside = jnp.where(onleftn[b][h], inl, inr)
                err = jnp.where(lane < PIX, (y - tg_ref[at(r, h), :]) * inside, 0.0)
                lacc[...] += err * err
                xs[b, 0, pl.ds(k, 8), :] = (err * scale).astype(bf16).astype(f32)
            yield 15
        for r in range(SIDE):
            tile0, tile1 = [], []
            for h in range(2):
                k = 8 + r * 16 + h * 8
                t0 = pltpu.roll(xs[b, 0, pl.ds(k, 8), :], 64, 1)
                if r < SIDE - 1:
                    t0 = t0 + xs[b, 0, pl.ds(k + 16, 8), :] * mvd[at(r, h), :]
                t1 = jnp.zeros((8, 128), f32)
                if r > 0:
                    t1 = xs[b, 0, pl.ds(k - 16, 8), :] * mvu[at(r, h), :]
                tile0.append(t0)
                tile1.append(t1)
            dyp[at(r, 0, 16), 0:128] = jnp.concatenate(tile0, axis=0).astype(bf16)
            dyp[at(r, 0, 16), 128:256] = jnp.concatenate(tile1, axis=0).astype(bf16)
            yield 10

        yield from put_us(dyp[mine, :], wrt)
        weight_grad(gr, xc3, dyp, 1)
        s1, s2 = yield from crop_sums(tap_back(sp4, x3))
        sum3, db, dg = backward_tables(3, s1, s2, row(13))
        gv[13] += dg
        gv[14] += db
        gv[12] += sum3
        yield 200
        for r in range(SIDE):
            halves = []
            for h in range(2):
                d = norm_grad(3, r, h, x3)
                gtop[at(r, h), :] = d
                halves.append(d)
            dpo[at(r, 0, 16), :] = jnp.concatenate(halves, axis=0).astype(bf16)
            yield 14
        dmx[mine, :] = nn(dpo[mine, :], wot[...]).astype(bf16)
        yield 128

        def grad_out(two):
            def job():
                ga[:, 768:1024] += nn(mix[two, :].T, dpo[two, :])

            fill.append(job)

        later(grad_out)
        dm = dmx[mine, :]
        p = prob[mine, :]
        da = nt(dm, vs[mine, :] * jnp.asarray(CH**-0.5, bf16))
        t = da * p
        ds = (t - p * jnp.sum(t, axis=1, keepdims=True)).astype(bf16)
        yield 300
        dv = nn(p.astype(bf16).T, dm)
        trip[mine, 512:768] = dv.astype(bf16)
        gv[11] += jnp.sum(dv.reshape(TOK // 8, 8, CH), axis=0)
        yield 128
        dq = nn(ds, ks[mine, :])
        trip[mine, 0:256] = dq.astype(bf16)
        gv[10] += jnp.sum(dq.reshape(TOK // 8, 8, CH), axis=0)
        yield 128
        dk = nn(ds.T, qs[mine, :])
        trip[mine, 256:512] = dk.astype(bf16)
        yield 128
        dys[mine, :] = nn(trip[mine, :], wat[...])
        yield 128 * 3

        def grad_triple(two):
            turned = []
            for k in range(3):

                def job(k=k):
                    if not turned:
                        turned.append(nrm[two, :].T)
                    ga[:, k * 256 : (k + 1) * 256] += nn(turned[0], trip[two, k * 256 : (k + 1) * 256])

                fill.append(job)

        later(grad_triple)

        def plain(r, h):
            dy = dys[at(r, h), :]
            return dy, dy * x2[at(r, h), :]

        s1, s2 = yield from crop_sums(plain)
        sum2, db, dg = backward_tables(2, s1, s2, row(8))
        gv[8] += dg
        gv[9] += db
        sum2 = sum2 + sum3
        gv[7] += sum2
        yield 200
        for r in range(SIDE):
            halves = []
            for h in range(2):
                d = norm_grad(2, r, h, x2) + gtop[at(r, h), :]
                gtop[at(r, h), :] = d
                halves.append(d)
            spread_grad(dpc2, r, jnp.concatenate(halves, axis=0))
            yield 18
        yield from put_us(dpc2[mine, :], wt2)
        weight_grad(gk2, xc2, dpc2, 3)
        s1, s2 = yield from crop_sums(tap_back(sp2, x1))
        sum1, db, dg = backward_tables(1, s1, s2, row(5))
        gv[5] += dg
        gv[6] += db
        gv[4] += sum1
        dtb[pl.ds((base + b) * 8, 8), :] = sum1
        yield 200
        for r in range(SIDE):
            spread_grad(dpc1, r, jnp.concatenate([norm_grad(1, r, h, x1) for h in range(2)], axis=0))
            yield 16
        yield from put_us(dpc1[mine, :], wt1)
        weight_grad(gk1, xc1, dpc1, 3)
        s1, s2 = yield from crop_sums(tap_back(sp1, x0))
        sum0, db, dg = backward_tables(0, s1, s2, row(2))
        gv[2] += dg
        gv[3] += db
        gv[0] += sum0 + sum2
        yield 200
        for r in range(SIDE):
            halves = [norm_grad(0, r, h, x0) + gtop[at(r, h), :] for h in range(2)]
            dps[at(r, 0, 16), :] = jnp.concatenate(halves, axis=0).astype(bf16)
            yield 14

        def grad_stem(two):
            def job():
                gs[...] += nn(xt_ref[two, :].T, dps[two, :])

            fill.append(job)

        later(grad_stem)

    clocks = {b: float(b * SKEW) for b in range(PAIR)}
    streams = {b: stream(b) for b in range(PAIR)}
    filled = 0.0
    while streams:
        b = min(streams, key=lambda k: clocks[k])
        try:
            clocks[b] += next(streams[b])
        except StopIteration:
            del streams[b]
        now = min([clocks[k] for k in streams], default=1e18)
        while fill and filled < now:
            filled = max(filled, now if now < 1e17 else 0.0) + FILLCOST
            fill.pop(0)()

    @pl.when(step == last)
    def _():
        low = dtb[...].astype(bf16)
        hp = hpre[...]
        sg = jax.nn.sigmoid(hp)
        gp = (nn((hp * sg).astype(bf16).T, low) * 0.5).astype(bf16)
        hg = nt(low, wpj[...]) * (sg * (1.0 + hp * (1.0 - sg)))
        ge = (nn(feat_ref[...].T, hg.astype(bf16)) * 0.5).astype(bf16)
        twice = {10: 1.0, 11: 1.0}
        rows = [jnp.sum(gv[4 if k == 1 else k], axis=0, keepdims=True) * twice.get(k, 0.5) for k in range(15)]
        gnorm = jnp.concatenate(rows + [jnp.zeros((1, 256), f32)], axis=0)
        gstem = gs[...].T.astype(bf16)
        for dy in range(3):
            for lo in range(0, 768, 256):
                part = gr[pl.ds(lo, 256), (dy // 2) * 128 : (dy // 2) * 128 + 128]
                if dy == 1:
                    part = pltpu.roll(part, 64, 1)
                grn[pl.ds(dy * 768 + lo, 256), :] = part
        for f in range(VIRT):
            slot, z = (f % 2) ^ geo_ref[3], f // 2
            for dy in range(3):
                lo, hi = max(f * KROW, dy * 768), min((f + 1) * KROW, (dy + 1) * 768)
                if lo >= hi:
                    continue
                src = pl.ds(lo - dy * 768, hi - lo)
                dst = pl.ds(lo - f * KROW, hi - lo)
                out_ref[slot, z, dst, 0:256] = gk1[src, dy * 256 : (dy + 1) * 256].astype(bf16)
                out_ref[slot, z, dst, 256:512] = gk2[src, dy * 256 : (dy + 1) * 256].astype(bf16)
            k = f * AROW
            a1, a2, p0 = KROW, KROW + AROW, KROW + 2 * AROW
            e0 = p0 + PROW
            out_ref[slot, z, a1:a2, :] = ga[k : k + AROW, 0:512].astype(bf16)
            out_ref[slot, z, a2:p0, :] = ga[k : k + AROW, 512:1024].astype(bf16)
            out_ref[slot, z, p0:e0, 0:256] = gp[f * 2 * PROW : f * 2 * PROW + PROW, :]
            out_ref[slot, z, p0:e0, 256:512] = gp[f * 2 * PROW + PROW : (f + 1) * 2 * PROW, :]
            out_ref[slot, z, e0:TROW, :] = ge[f * EROW : (f + 1) * EROW, :]
            back = grn[pl.ds(f * KROW, 384), :].T[:TAIL, :]
            keep = lax.broadcasted_iota(jnp.int32, (TAIL, 384), 1) < KROW
            out_ref[slot, z, TROW:PACKED, 0:384] = jnp.where(keep, back, 0.0).astype(bf16)
            out_ref[slot, z, TROW : TROW + 32, 384:512] = gstem[k : k + AROW, :]
            tile = gnorm[:, (f // 4) * 128 : (f // 4) * 128 + 128]
            tile = pltpu.roll(tile, (128 - (f % 4) * AROW) % 128, 1)
            keep = lax.broadcasted_iota(jnp.int32, (16, 128), 1) < AROW
            out_ref[slot, z, TROW + 32 : PACKED, 384:512] = jnp.where(keep, tile, 0.0).astype(bf16)
        loss_ref[...] = lacc[...]


SKEW = 1400
FILLCOST = 128


def run_step(packed, quad, geo, scal, feat, cp, tg, inv, cnt):
    canvases = cp.shape[0] // TOK
    whole = pl.BlockSpec(memory_space=pltpu.VMEM)
    smem = pl.BlockSpec(memory_space=pltpu.SMEM)

    def rows(n, lanes):
        return pl.BlockSpec((n, lanes), lambda i, *_: (i, 0))

    items = scratch_list(canvases)
    return pl.pallas_call(
        functools.partial(step_kernel, [name for name, _, _ in items]),
        grid_spec=pltpu.PrefetchScalarGridSpec(
            num_scalar_prefetch=2,
            grid=(canvases // PAIR,),
            in_specs=[
                smem, whole, whole, rows(ROWS, 128), rows(ROWS, 128), rows(8 * PAIR, 256), rows(8 * PAIR, 256),
            ],
            out_specs=[whole, whole],
            scratch_shapes=[pltpu.VMEM(shape, dtype) for _, shape, dtype in items],
        ),
        out_shape=[
            jax.ShapeDtypeStruct((2, VIRT // 2, PACKED, 512), bf16),
            jax.ShapeDtypeStruct((8, 128), f32),
        ],
        compiler_params=pltpu.CompilerParams(
            dimension_semantics=("arbitrary",), vmem_limit_bytes=60 * 1024 * 1024
        ),
        name="unet_step",
    )(quad, geo, scal, packed, feat, cp, tg, inv, cnt)


def patch_kernel(clean_ref, noise_ref, cp_ref, np_ref, staged):
    n = clean_ref.shape[0]
    slot = staged.shape[0] // (2 * SIDE)
    for k, ref in enumerate((clean_ref, noise_ref)):
        for r in range(SIDE):
            for c in range(3):
                staged[pl.ds((k * SIDE + r) * slot, n), c * 256 : (c + 1) * 256] = ref[:, c * 4096 + r * 256 : c * 4096 + r * 256 + 256]
    src = lax.broadcasted_iota(jnp.int32, (768, 256), 0)
    place = ((src >> 2) & 15) * 128 + (src >> 8) * 16 + ((src >> 6) & 3) * 4 + (src & 3)
    for j in range(SIDE // 2):
        lane = lax.broadcasted_iota(jnp.int32, (768, 256), 1) + j * 256
        out = nn(staged[...], (place == lane).astype(bf16))
        for k, ref in enumerate((cp_ref, np_ref)):
            for r in range(SIDE):
                row = (k * SIDE + r) * slot
                for i in range(2):
                    ref[pl.ds(r * SIDE + 2 * j + i, n, stride=TOK), :] = out[row : row + n, i * 128 : (i + 1) * 128]


def patches(clean, noise):
    n = clean.shape[0]
    slot = -(-n // 16) * 16
    whole = pl.BlockSpec(memory_space=pltpu.VMEM)
    return pl.pallas_call(
        patch_kernel,
        in_specs=[whole, whole],
        out_specs=[whole, whole],
        out_shape=[jax.ShapeDtypeStruct((n * TOK, 128), f32)] * 2,
        scratch_shapes=[pltpu.VMEM((2 * SIDE * slot, 768), bf16)],
        compiler_params=pltpu.CompilerParams(vmem_limit_bytes=48 * 1024 * 1024),
        name="patches",
    )(clean, noise)


def pack_kernel(stem, kernels, embed, project, attention, readout, norm, out):
    a1, a2, p0 = KROW, KROW + AROW, KROW + 2 * AROW
    e0 = p0 + PROW
    out[0:a1, :] = kernels[...].astype(bf16)
    out[a1:a2, :] = attention[:, 0:512].astype(bf16)
    out[a2:p0, :] = attention[:, 512:1024].astype(bf16)
    out[p0:e0, 0:256] = project[0:PROW, :].astype(bf16)
    out[p0:e0, 256:512] = project[PROW : 2 * PROW, :].astype(bf16)
    out[e0:TROW, :] = embed[...].astype(bf16)
    out[TROW:PACKED, 256:512] = jnp.zeros((TAIL, 256), bf16)
    out[TROW:PACKED, 0:KROW] = readout[...].astype(bf16)
    out[TROW : TROW + 32, 384 : 384 + PIX] = stem[...].astype(bf16)
    out[TROW + 32 : TROW + 47, 384 : 384 + AROW] = norm[...].astype(bf16)


def pack_weights(masters):
    if masters[1].shape[0] != KROW:
        return pack_rows([w.astype(bf16) for w in masters])
    stem, kernels, embed, project, attention, readout, norm = masters
    return pl.pallas_call(
        pack_kernel, out_shape=jax.ShapeDtypeStruct((PACKED, 512), bf16), name="pack_weights"
    )(stem, kernels, embed, project, attention, readout.T, norm.T)


def update_kernel(place, rate, own, first, second, *refs):
    total = refs[-1]
    refs = refs[:-1]
    half, quarter = PACKED // 4, PACKED // 8
    for k in range(2):
        near, far = place[k], place[1 - k]
        at = k * 2 * half
        total[pl.ds(pl.multiple_of(at + near * half + far * quarter, 8), quarter), :] = own[k].astype(f32)
        total[pl.ds(pl.multiple_of(at + near * half + (1 - far) * quarter, 8), quarter), :] = first[k].astype(f32)
        there = at + (1 - near) * half
        total[pl.ds(pl.multiple_of(there + far * quarter, 8), quarter), :] = second[k, 0].astype(f32)
        total[pl.ds(pl.multiple_of(there + (1 - far) * quarter, 8), quarter), :] = second[k, 1].astype(f32)
    a1, a2, p0 = KROW, KROW + AROW, KROW + 2 * AROW
    e0 = p0 + PROW
    everything = slice(None)
    cuts = [
        (0, everything, everything, total[TROW : TROW + 32, 384:512][:, :PIX]),
        (1, everything, everything, total[0:a1, :]),
        (2, everything, everything, total[e0:TROW, :]),
        (3, slice(0, PROW), everything, total[p0:e0, 0:256]),
        (3, slice(PROW, 2 * PROW), everything, total[p0:e0, 256:512]),
        (4, everything, slice(0, 512), total[a1:a2, :]),
        (4, everything, slice(512, 1024), total[a2:p0, :]),
        (5, everything, everything, total[TROW:PACKED, 0:384][:, :KROW]),
        (6, everything, everything, total[TROW + 32 : PACKED, 384:512][:15, :AROW]),
    ]
    for n, rows, lanes, grad in cuts:
        w, m, a, m_out, w_out, a_out = [refs[n + 7 * j] for j in range(6)]
        m_next = momentum_rate * m[rows, lanes] + grad
        w_next = w[rows, lanes] - rate[0] * (grad + momentum_rate * m_next)
        m_out[rows, lanes] = m_next
        w_out[rows, lanes] = w_next
        a_out[rows, lanes] = average_rate * a[rows, lanes] + (1.0 - average_rate) * w_next


def turn(arrays):
    return [x.T if k in (5, 6) else x for k, x in enumerate(arrays)]


def update_fused(place, rate, own, first, second, masters, moments, averages):
    whole = pl.BlockSpec(memory_space=pltpu.VMEM)
    smem = pl.BlockSpec(memory_space=pltpu.SMEM)
    state = turn(masters) + turn(moments) + turn(averages)
    out = pl.pallas_call(
        update_kernel,
        in_specs=[smem, smem] + [whole] * 24,
        out_specs=[whole] * 21,
        out_shape=[jax.ShapeDtypeStruct(x.shape, f32) for x in state],
        scratch_shapes=[pltpu.VMEM((PACKED, 512), f32)],
        compiler_params=pltpu.CompilerParams(vmem_limit_bytes=32 * 1024 * 1024),
        name="update",
    )(place, rate, own, first, second, *state)
    return tuple(turn(out[0:7]) + turn(out[7:14]) + turn(out[14:21]))


def signal_table():
    beta = np.linspace(0.0001, 0.02, TSTEPS, dtype=np.float64)
    return np.exp(np.cumsum(np.log(1.0 - beta))).astype(np.float32)


def time_features(time_steps):
    half_width = TEMB // 2
    frequency = jnp.exp(-math.log(10000.0) * jnp.arange(half_width, dtype=f32) / (half_width - 1))
    angles = time_steps.astype(f32)[..., None] * frequency
    return jnp.concatenate([jnp.sin(angles), jnp.cos(angles)], axis=-1)


def prepare(clean, noise, lab, time_steps, count, core):
    canvases = lab.shape[0]
    cut = jnp.sum(jnp.all(lab == lab[:, :, :1], axis=1).astype(jnp.int32), axis=1)
    left = jnp.sum((lab[:, :, 0] == lab[:, :1, 0]).astype(jnp.int32), axis=1)
    right = jnp.sum((lab[:, :, -1] == lab[:, :1, -1]).astype(jnp.int32), axis=1)
    own = jnp.stack([lab[:, 0, 0], lab[:, -1, 0], lab[:, 0, -1], lab[:, -1, -1]], axis=1)
    area = jnp.stack(
        [cut * left, cut * (SIDE - left), (SIDE - cut) * right, (SIDE - cut) * (SIDE - right)], axis=1
    ).astype(f32)
    geo = jnp.stack([cut, left, right] + [jnp.full_like(cut, core)] * 5, axis=1).reshape(-1)
    line = jnp.arange(SIDE, dtype=jnp.int32)
    quad = jnp.stack(
        [(line >= left[:, None]).astype(jnp.int32), 2 + (line >= right[:, None]).astype(jnp.int32)],
        axis=-1,
    ).reshape(-1)
    hit = own[..., None] == jnp.arange(1, CROPS + 1, dtype=jnp.int32)
    times = jnp.sum(jnp.where(hit, time_steps[:, None, :], 0), axis=-1)
    eight = np.array([0, 0, 2, 2, 1, 1, 3, 3])
    feat = time_features(times[:, eight]).astype(bf16).reshape(-1, TEMB)
    area8 = area[:, eight].reshape(-1, 1)
    picked = times[..., None] == jnp.arange(TSTEPS, dtype=jnp.int32)
    chosen = jnp.sum(jnp.where(picked, jnp.asarray(signal_table()), 0.0), axis=-1)
    inv = jnp.broadcast_to(1.0 / jnp.maximum(area8, 1.0), (8 * canvases, CH))
    cnt = jnp.broadcast_to(area8, (8 * canvases, CH))
    inside = (own > 0).astype(f32)
    levels = [inside, jnp.sqrt(chosen), jnp.sqrt(1.0 - chosen)]
    scal = jnp.concatenate([jnp.full((8,), 2.0 / count, f32)] + [x.reshape(-1) for x in levels])
    cp, tg = patches(clean, noise)
    return quad, geo, scal, feat, cp, tg, inv, cnt


def exchange(value, axis, bit):
    return lax.ppermute(value, axis, [(i, i ^ bit) for i in range(lax.axis_size(axis))])


def sum_over_all(value):
    for axis in ("fsdp", "dp"):
        bit = 1
        while bit < lax.axis_size(axis):
            value = value + exchange(value, axis, bit)
            bit *= 2
    return value


def join(a, b):
    return (a.astype(f32) + b.astype(f32)).astype(bf16)


def halves(value, which):
    n = value.shape[1] // 2
    low, high = value[:, :n], value[:, n:]
    return jnp.where(which == 0, low, high), jnp.where(which == 0, high, low)


def reduce_grads(keep, send):
    total = join(keep, exchange(send, "fsdp", 1))
    near, far = lax.axis_index("dp") % 2, lax.axis_index("dp") // 2
    n = total.shape[1] // 2
    parts = [total[:, :n], total[:, n:]]
    for first, second in (((near, 1), (far, 2)), ((far, 2), (near, 1))):
        split = [halves(parts[0], first[0]), halves(parts[1], second[0])]
        came = [exchange(split[0][1], "dp", first[1]), exchange(split[1][1], "dp", second[1])]
        parts = [join(split[0][0], came[0]), join(split[1][0], came[1])]
    blocks = jnp.stack(parts, axis=1)
    chips, shards = blocks.shape[0], lax.axis_size("fsdp")
    chip = lax.axis_index("fsdp") // 2
    own = lax.dynamic_index_in_dim(blocks, chip, 0, keepdims=False).astype(f32)
    for j in range(1, chips):
        out = lax.dynamic_index_in_dim(blocks, (chip + j) % chips, 0, keepdims=False)
        own = own + lax.ppermute(out, "fsdp", [(i, (i + 2 * j) % shards) for i in range(shards)]).astype(f32)
    own = own.astype(bf16)
    first = jnp.stack([exchange(own[0], "dp", 2), exchange(own[1], "dp", 1)])
    both = jnp.stack([own, first], axis=1)
    second = jnp.stack([exchange(both[0], "dp", 1), exchange(both[1], "dp", 2)])
    return jnp.stack([near, far]).astype(jnp.int32), own, first, second


def assemble(place, own, first, second):
    n = own.shape[1]
    parts = []
    for k in range(2):
        near, far = place[k], place[1 - k]
        mine = jnp.where(far == 0, jnp.concatenate([own[k], first[k]]), jnp.concatenate([first[k], own[k]]))
        s = second[k]
        theirs = jnp.where(far == 0, jnp.concatenate([s[0], s[1]]), jnp.concatenate([s[1], s[0]]))
        parts.append(jnp.where(near == 0, jnp.concatenate([mine, theirs]), jnp.concatenate([theirs, mine])))
    return jnp.concatenate(parts).astype(f32)


def on_device(clean, noise, crop_labels, time_steps, *state):
    masters, moments, averages = state[0:7], state[7:14], state[14:21]
    shards = lax.axis_size("fsdp")
    core = lax.axis_index("fsdp") % 2
    packed = lax.all_gather(pack_weights(masters), "fsdp", axis=0, tiled=False)
    count = sum_over_all(PATCH * PATCH * jnp.sum((crop_labels > 0).astype(f32)).reshape(1, 1))[0, 0]
    direct = shards == VIRT
    inputs = prepare(clean, noise, crop_labels, time_steps, count, core if direct else 0)
    grads, loss = run_step(repack(packed, shards, VIRT), *inputs)
    total_loss = sum_over_all(jnp.sum(loss).reshape(1, 1))[0, 0]
    if direct:
        keep, send = grads[0], grads[1]
    else:
        blocks = repack(grads.transpose(1, 0, 2, 3).reshape(VIRT, PACKED, 512), VIRT, shards)
        blocks = blocks.reshape(shards // 2, 2, *blocks.shape[1:])
        keep = lax.dynamic_index_in_dim(blocks, core, 1, keepdims=False)
        send = lax.dynamic_index_in_dim(blocks, 1 - core, 1, keepdims=False)
    place, own, first, second = reduce_grads(keep, send)
    rate = lr_scale * jnp.sqrt(count)
    if direct:
        out = update_fused(place, rate.reshape(1), own, first, second, masters, moments, averages)
        return (total_loss / count,) + out
    cut = [masters[1].shape[0], masters[0].shape[0], masters[3].shape[0], masters[2].shape[0]]
    grads = unpack_rows(assemble(place, own, first, second), *cut)
    moment_next = tuple(momentum_rate * m + g for m, g in zip(moments, grads))
    master_next = tuple(w - rate * (g + momentum_rate * m) for w, g, m in zip(masters, grads, moment_next))
    average_next = tuple(average_rate * a + (1.0 - average_rate) * w for a, w in zip(averages, master_next))
    return (total_loss / count,) + moment_next + master_next + average_next


def solution(mesh):
    split = P(("dp", "fsdp"), None)
    in_specs = (split, split, P(("dp", "fsdp"), None, None), split) + (P("fsdp", None),) * 21
    out_specs = (P(),) + (P("fsdp", None),) * 21
    return jax.shard_map(on_device, mesh=mesh, in_specs=in_specs, out_specs=out_specs, check_vma=False)
```

```python
import functools
import math

import jax
import jax.numpy as jnp
import numpy as np
from jax import lax
from jax.experimental import pallas as pl
from jax.experimental.pallas import tpu as pltpu
from jax.sharding import PartitionSpec as P

GROUPS = 32
TEMB = 128
SIDE = 16
PATCH = 4
CROPS = 4
TSTEPS = 1000
TOK = SIDE * SIDE
CH = 256
PIX = 3 * PATCH * PATCH
PAIR = 4
ROWS = PAIR * TOK
VIRT = 8
TAIL = 48

eps_norm = 1e-05
lr_scale = 0.01
momentum_rate = 0.5
average_rate = 0.5
far_score = -1e30
f32 = jnp.float32
bf16 = jnp.bfloat16


def pad_to(value, rows, lanes):
    return jnp.pad(value, ((0, rows - value.shape[0]), (0, lanes - value.shape[1])))


def pack_rows(parts):
    stem, kernels, embed, project, attention, readout, norm = parts
    half = project.shape[0] // 2
    small = jnp.concatenate([pad_to(stem, 32, 128), pad_to(norm.T, 16, 128)], axis=0)
    tail = jnp.concatenate([pad_to(readout.T, TAIL, 384), small], axis=1)
    rows = [kernels, attention[:, :512], attention[:, 512:]]
    rows += [jnp.concatenate([project[:half], project[half:]], axis=1), embed, tail]
    rows = jnp.concatenate(rows, axis=0)
    return pad_to(rows, -(-rows.shape[0] // 8) * 8, 512)


def unpack_rows(rows, k, a, p, e):
    half = p // 2
    at = [0, k, k + a, k + 2 * a, k + 2 * a + half, k + 2 * a + half + e, k + 2 * a + half + e + TAIL]
    kernels, left, right, halves, embed, tail = [rows[at[i] : at[i + 1]] for i in range(6)]
    project = jnp.concatenate([halves[:, :256], halves[:, 256:]], axis=0)
    stem, norm = tail[:a, 384 : 384 + PIX], tail[32 : 32 + 15, 384 : 384 + a].T
    return stem, kernels, embed, project, jnp.concatenate([left, right], axis=1), tail[:, :k].T, norm


def repack(packed, parts_now, parts_next):
    if parts_now == parts_next:
        return packed
    cut = [n // parts_now for n in (9 * CH, CH, 2 * CH, CH // 2)]
    pieces = jax.vmap(lambda rows: unpack_rows(rows, *cut))(packed)
    whole = [piece.reshape(-1, piece.shape[-1]) for piece in pieces]
    split = [piece.reshape(parts_next, -1, piece.shape[-1]) for piece in whole]
    return jax.vmap(lambda *p: pack_rows(p))(*split)


KROW = 9 * CH // VIRT
AROW = CH // VIRT
PROW = CH // VIRT
EROW = TEMB // VIRT
TROW = KROW + 2 * AROW + PROW + EROW
PACKED = TROW + TAIL


def lane_groups(value):
    lane = lax.broadcasted_iota(jnp.int32, (8, 128), 1)
    tiles = []
    for t in range(2):
        x = value[:, t * 128 : (t + 1) * 128]
        for s in (1, 2, 4):
            x = x + jnp.where((lane & s) == 0, pltpu.roll(x, 128 - s, 1), pltpu.roll(x, s, 1))
        tiles.append(x)
    return jnp.concatenate(tiles, axis=1)


def quad_rows(q0, q1, q2, q3):
    sub = lax.broadcasted_iota(jnp.int32, (8, 128), 0)
    tiles = []
    for t in range(2):
        a, b, c, d = [q[:, t * 128 : (t + 1) * 128] for q in (q0, q1, q2, q3)]
        low = sub < 4
        u = jnp.where(low, a, pltpu.roll(b, 4, 0)) + jnp.where(low, pltpu.roll(a, 4, 0), b)
        v = jnp.where(low, c, pltpu.roll(d, 4, 0)) + jnp.where(low, pltpu.roll(c, 4, 0), d)
        even = (sub & 2) == 0
        w = jnp.where(even, u, pltpu.roll(v, 2, 0)) + jnp.where(even, pltpu.roll(u, 6, 0), v)
        w = w + jnp.where((sub & 1) == 0, pltpu.roll(w, 7, 0), pltpu.roll(w, 1, 0))
        tiles.append(w)
    return jnp.concatenate(tiles, axis=1)


QUAD_ROW = (0, 4, 2, 6)


def nt(a, b):
    return lax.dot_general(a, b, (((1,), (1,)), ((), ())), preferred_element_type=f32)


def nn(a, b):
    return lax.dot_general(a, b, (((1,), (0,)), ((), ())), preferred_element_type=f32)


PADROWS = TOK + 16


def scratch_list(canvases):
    n = 8 * canvases
    items = [
        ("wk1", (2304, 256), bf16), ("wk2", (2304, 256), bf16), ("wt1", (768, 768), bf16), ("wt2", (768, 768), bf16),
        ("wr", (768, 256), bf16), ("wrt", (256, 768), bf16), ("wqkv", (256, 768), bf16), ("wat", (768, 256), bf16),
        ("wo", (256, 256), bf16), ("wot", (256, 256), bf16), ("ws", (128, 256), bf16), ("wpj", (512, 256), bf16),
        ("wem", (128, 512), bf16), ("vec", (16, 256), f32), ("tbs", (n, 256), f32), ("hpre", (n, 512), f32),
        ("grn", (2304 + 96, 128), f32), ("xt", (ROWS, 128), bf16),
        ("gk1", (768, 768), f32), ("gk2", (768, 768), f32), ("gr", (768, 256), f32), ("ga", (256, 1024), f32),
        ("gs", (128, 256), f32), ("gv", (15, 8, 256), f32), ("dtb", (n, 256), f32), ("lacc", (8, 128), f32),
        ("x0", (ROWS, 256), f32), ("x1", (ROWS, 256), f32), ("x2", (ROWS, 256), f32), ("x3", (ROWS, 256), f32),
        ("sp1", (ROWS, 256), f32), ("sp2", (ROWS, 256), f32), ("sp4", (ROWS, 256), f32),
        ("xs", (PAIR, 2, PADROWS, 128), f32), ("us", (PAIR, 6, PADROWS, 128), f32),
        ("side", (ROWS, 1536), bf16),
        ("xc1", (ROWS, 768), bf16), ("xc2", (ROWS, 768), bf16), ("xc3", (ROWS, 768), bf16),
        ("nrm", (ROWS, 256), bf16), ("qs", (ROWS, 256), bf16), ("ks", (ROWS, 256), bf16), ("vs", (ROWS, 256), bf16),
        ("prob", (ROWS, 256), f32), ("pb", (ROWS, 256), bf16), ("dsb", (ROWS, 256), bf16), ("mix", (ROWS, 256), bf16), ("dmx", (ROWS, 256), bf16), ("dpo", (ROWS, 256), bf16),
        ("gtop", (ROWS, 256), f32), ("dys", (ROWS, 256), f32),
        ("dps", (ROWS, 256), bf16),
        ("dyp", (ROWS, 256), bf16), ("trip", (ROWS, 768), bf16),
        ("mvu", (ROWS, 128), f32), ("mvd", (ROWS, 128), f32), ("mbu", (ROWS, 128), bf16), ("mbd", (ROWS, 128), bf16),
        ("ctab", (PAIR, 4, 4, 8, 256), f32),
    ]
    for b in range(PAIR):
        items += [(f"pref{b}", (2, 2, 17, 8, 256), f32)]
        items += [(f"tab{b}_{slot}", (4, 2, 8, 256), f32) for slot in range(7)]
    return items


def step_kernel(names, *refs):
    quad_ref, geo_ref, scale_ref, wp_ref, feat_ref, cp_ref, tg_ref, inv_ref, cnt_ref, keep_ref, send_ref, loss_ref = refs[:12]
    S = dict(zip(names, refs[12:]))
    wk1, wk2, wt1, wt2, wr, wrt, wqkv, wat, wo, wot = [S[k] for k in ("wk1", "wk2", "wt1", "wt2", "wr", "wrt", "wqkv", "wat", "wo", "wot")]
    ws, wpj, wem, vec, tbs, hpre = [S[k] for k in ("ws", "wpj", "wem", "vec", "tbs", "hpre")]
    gk1, gk2, gr, ga, gs, gv, dtb, lacc = [S[k] for k in ("gk1", "gk2", "gr", "ga", "gs", "gv", "dtb", "lacc")]
    x0, x1, x2, x3, sp1, sp2, sp4, xs, us = [S[k] for k in ("x0", "x1", "x2", "x3", "sp1", "sp2", "sp4", "xs", "us")]
    side, xc1, xc2, xc3, nrm, qs, ks, vs = [S[k] for k in ("side", "xc1", "xc2", "xc3", "nrm", "qs", "ks", "vs")]
    prob, mix, dmx, dpo, gtop, dys = [S[k] for k in ("prob", "mix", "dmx", "dpo", "gtop", "dys")]
    dps, dyp, trip = [S[k] for k in ("dps", "dyp", "trip")]
    mvu, mvd, mbu, mbd, ctab = [S[k] for k in ("mvu", "mvd", "mbu", "mbd", "ctab")]
    grn, xt_ref, pb, dsb = S["grn"], S["xt"], S["pb"], S["dsb"]
    pref = [S[f"pref{b}"] for b in range(PAIR)]
    tab = [[S[f"tab{b}_{slot}"] for slot in range(7)] for b in range(PAIR)]
    step = pl.program_id(0)
    last = pl.num_programs(0) - 1
    canvases = tbs.shape[0] // 8

    @pl.when(step == 0)
    def _():
        for f in range(VIRT):
            wk1[pl.ds(f * KROW, KROW), :] = wp_ref[f, :KROW, 0:256]
            wk2[pl.ds(f * KROW, KROW), :] = wp_ref[f, :KROW, 256:512]
            back = wp_ref[f, TROW:PACKED, 0:384].astype(f32)
            back = jnp.concatenate([back, jnp.zeros((128 - TAIL, 384), f32)], axis=0).T
            grn[pl.ds(f * KROW, KROW), :] = back[:KROW, :]
            att = slice(KROW, KROW + AROW)
            att2 = slice(KROW + AROW, KROW + 2 * AROW)
            wqkv[pl.ds(f * AROW, AROW), 0:512] = wp_ref[f, att, 0:512]
            wqkv[pl.ds(f * AROW, AROW), 512:768] = wp_ref[f, att2, 0:256]
            wo[pl.ds(f * AROW, AROW), :] = wp_ref[f, att2, 256:512]
            pr = KROW + 2 * AROW
            wpj[pl.ds(f * 2 * PROW, PROW), :] = wp_ref[f, pr : pr + PROW, 0:256]
            wpj[pl.ds(f * 2 * PROW + PROW, PROW), :] = wp_ref[f, pr : pr + PROW, 256:512]
            wem[pl.ds(f * EROW, EROW), :] = wp_ref[f, pr + PROW : pr + PROW + EROW, 0:512]
        stem = jnp.concatenate([wp_ref[f, TROW : TROW + 32, 384:512] for f in range(VIRT)], axis=0)
        ws[...] = stem.T
        for t in range(2):
            tile = jnp.zeros((16, 128), f32)
            for j in range(4):
                part = wp_ref[4 * t + j, TROW + 32 : PACKED, 384:512].astype(f32)
                part = jnp.where(lax.broadcasted_iota(jnp.int32, (16, 128), 1) < AROW, part, 0.0)
                tile = tile + (pltpu.roll(part, j * AROW, 1) if j else part)
            vec[:, t * 128 : (t + 1) * 128] = tile
        for dy in range(3):
            for dx in range(3):
                rows = pl.ds((dy * 3 + dx) * 256, 256)
                wt1[pl.ds(dy * 256, 256), dx * 256 : (dx + 1) * 256] = wk1[rows, :].T
                wt2[pl.ds(dy * 256, 256), dx * 256 : (dx + 1) * 256] = wk2[rows, :].T
        for j in range(3):
            wat[pl.ds(j * 256, 256), :] = wqkv[:, j * 256 : (j + 1) * 256].T
        wot[...] = wo[...].T
        for dx in range(3):
            rows = [grn[pl.ds(dy * 768 + dx * 256, 256), :] for dy in range(3)]
            tile0 = (rows[0] + pltpu.roll(rows[1], 64, 1)).astype(bf16)
            tile1 = rows[2].astype(bf16)
            wr[pl.ds(dx * 256, 256), 0:128] = tile0
            wr[pl.ds(dx * 256, 256), 128:256] = tile1
            wrt[0:128, dx * 256 : (dx + 1) * 256] = tile0.T
            wrt[128:256, dx * 256 : (dx + 1) * 256] = tile1.T
        hp = nn(feat_ref[...], wem[...])
        hpre[...] = hp
        tbs[...] = nn(jax.nn.silu(hp).astype(bf16), wpj[...]) + vec[1:2, :]
        grn[pl.ds(2304, 96), :] = jnp.zeros((96, 128), f32)
        for ref in [gk1, gk2, gr, ga, gs, gv, lacc] + pref:
            ref[...] = jnp.zeros_like(ref)

    base = step * PAIR
    cuts = [geo_ref[(base + b) * 8] for b in range(PAIR)]
    lefts = [geo_ref[(base + b) * 8 + 1] for b in range(PAIR)]
    rights = [geo_ref[(base + b) * 8 + 2] for b in range(PAIR)]
    iota8 = lax.broadcasted_iota(jnp.int32, (8, 256), 0)
    iota8n = lax.broadcasted_iota(jnp.int32, (8, 128), 0)
    onleft = [[iota8 < (cuts[b] - 8 * h) for h in range(2)] for b in range(PAIR)]
    onleftn = [[iota8n < (cuts[b] - 8 * h) for h in range(2)] for b in range(PAIR)]
    hasl = [[(iota8n + 8 * h != 0) & (iota8n + 8 * h != cuts[b]) for h in range(2)] for b in range(PAIR)]
    hasr = [[(iota8n + 8 * h != 15) & (iota8n + 8 * h != cuts[b] - 1) for h in range(2)] for b in range(PAIR)]
    scale = scale_ref[0]
    lane = lax.broadcasted_iota(jnp.int32, (8, 128), 1)
    fill = []

    def row(k):
        return vec[k : k + 1, :]

    def stream(b):
        r0 = b * TOK
        mine = pl.ds(r0, TOK)
        inv = inv_ref[pl.ds(b * 8, 8), :]
        cnt = cnt_ref[pl.ds(b * 8, 8), :]

        def at(r, h=0, n=8):
            return pl.ds(r0 + r * 16 + h * 8, n)

        def kind(r):
            return quad_ref[(base + b) * SIDE + r]

        def quads(r):
            t = kind(r)
            return t & 1, 2 + (t >> 1)

        def masks():
            for r in range(SIDE):
                upl = ((lefts[b] != r) & (r > 0)).astype(f32)
                upr = ((rights[b] != r) & (r > 0)).astype(f32)
                dnl = ((lefts[b] != r + 1) & (r < SIDE - 1)).astype(f32)
                dnr = ((rights[b] != r + 1) & (r < SIDE - 1)).astype(f32)
                up = jnp.concatenate([jnp.where(onleftn[b][h], upl, upr) for h in range(2)], axis=0)
                dn = jnp.concatenate([jnp.where(onleftn[b][h], dnl, dnr) for h in range(2)], axis=0)
                mvu[at(r, 0, 16), :] = up
                mvd[at(r, 0, 16), :] = dn
                mbu[at(r, 0, 16), :] = up.astype(bf16)
                mbd[at(r, 0, 16), :] = dn.astype(bf16)
                ql, qr = quads(r)
                level = 8 + 4 * canvases + (base + b) * 4
                al, ar = scale_ref[level + ql], scale_ref[level + qr]
                sl, sr = scale_ref[level + 4 * canvases + ql], scale_ref[level + 4 * canvases + qr]
                mixed = []
                for h in range(2):
                    m = onleftn[b][h]
                    noisy = jnp.where(m, sl, sr) * tg_ref[at(r, h), :]
                    mixed.append(jnp.where(m, al, ar) * cp_ref[at(r, h), :] + noisy)
                xt_ref[at(r, 0, 16), :] = jnp.concatenate(mixed, axis=0).astype(bf16)
            yield 100

        def put_table(slot, table):
            of = [jnp.broadcast_to(table[k : k + 1, :], (8, 256)) for k in QUAD_ROW]
            for t in range(4):
                for h in range(2):
                    tab[b][slot][t, h] = jnp.where(onleft[b][h], of[t & 1], of[2 + (t >> 1)])

        def pick(slot, r, h):
            return tab[b][slot][kind(r), h]

        def crop_sums(values_of):
            total = [None, None]
            left = [None, None]
            p = pref[b]
            for r in range(SIDE):
                halves = [values_of(r, h) for h in range(2)]
                for j in range(2):
                    a0, a1 = halves[0][j], halves[1][j]
                    lp = jnp.where(onleft[b][0], a0, 0.0) + jnp.where(onleft[b][1], a1, 0.0)
                    tp = a0 + a1
                    left[j] = lp if r == 0 else left[j] + lp
                    total[j] = tp if r == 0 else total[j] + tp
                    p[j, 0, r + 1] = left[j]
                    p[j, 1, r + 1] = total[j]
                if r % GRAIN == GRAIN - 1:
                    yield 16 * GRAIN
            got = []
            for j in range(2):
                q0 = p[j, 0, lefts[b]]
                q1 = left[j] - q0
                q2 = p[j, 1, rights[b]] - p[j, 0, rights[b]]
                q3 = (total[j] - left[j]) - q2
                got.append(quad_rows(q0, q1, q2, q3))
            yield 100
            return got

        def forward_tables(n, xref, bias, gain, shift):
            def both(r, h):
                x = xref[at(r, h), :]
                return x, x * x

            s1, s2 = yield from crop_sums(both)
            own = s1 * inv
            mean = lane_groups(own + bias) * 0.125
            apart = own + bias - mean
            var = lane_groups(jnp.maximum(s2 * inv - own * own, 0.0) + apart * apart) * 0.125
            rs = lax.rsqrt(var + eps_norm)
            a = rs * gain
            e = bias - mean
            put_table(n, a)
            put_table(4, e * a + shift)
            ctab[b, n, 0] = a
            ctab[b, n, 1] = rs
            ctab[b, n, 2] = e
            ctab[b, n, 3] = s1
            yield 250

        def backward_tables(n, s1, s2, gain):
            a, rs, e, sx = [ctab[b, n, j] for j in range(4)]
            sn = rs * (s2 + e * s1)
            m1 = lane_groups(gain * s1 * inv) * 0.125
            m2 = lane_groups(gain * sn * inv) * 0.125
            v = rs * rs * m2
            u = rs * m1 + e * v
            put_table(5, v)
            put_table(6, u)
            return a * s1 - v * sx - cnt * u, s1, sn

        def silu_pass(n, xref, spref, xcref, vertical):
            if vertical:
                side[at(0, 0, 16), 0:768] = jnp.zeros((16, 768), bf16)
                side[at(SIDE - 1, 0, 16), 768:1536] = jnp.zeros((16, 768), bf16)
            for r in range(SIDE):
                acts = []
                for h in range(2):
                    x = xref[at(r, h), :]
                    y = x * pick(n, r, h) + pick(4, r, h)
                    hy = 0.5 * y
                    t = jnp.tanh(hy)
                    act = hy * t + hy
                    sig = 0.5 * t + 0.5
                    spref[at(r, h), :] = sig + act - act * sig
                    acts.append(act)
                    for c in range(2):
                        xs[b, c, pl.ds(8 + r * 16 + h * 8, 8), :] = act[:, c * 128 : (c + 1) * 128]
                k0 = 8 + r * 16
                if vertical:
                    below = mbu[at(r + 1, 0, 16), :] if r < SIDE - 1 else None
                    above = mbd[at(r - 1, 0, 16), :] if r > 0 else None
                for c in range(2):
                    taps = []
                    for dx in (-1, 0, 1):
                        pieces = []
                        for h in range(2):
                            if dx == 0:
                                pieces.append(acts[h][:, c * 128 : (c + 1) * 128])
                                continue
                            piece = xs[b, c, pl.ds(k0 + h * 8 + dx, 8), :]
                            if dx == -1:
                                piece = jnp.where(hasl[b][h], piece, 0.0)
                            if dx == 1:
                                piece = jnp.where(hasr[b][h], piece, 0.0)
                            pieces.append(piece)
                        taps.append(jnp.concatenate(pieces, axis=0).astype(bf16))
                    for k, tap in enumerate(taps):
                        lanes = slice(k * 256 + c * 128, k * 256 + c * 128 + 128)
                        low = slice(768 + lanes.start, 768 + lanes.stop)
                        xcref[at(r, 0, 16), lanes] = tap
                        if vertical and r < SIDE - 1:
                            side[at(r + 1, 0, 16), lanes] = tap * below
                        if vertical and r > 0:
                            side[at(r - 1, 0, 16), low] = tap * above
                if r % GRAIN == GRAIN - 1:
                    yield 30 * GRAIN

        def spread_grad(first, r, value):
            low = value.astype(bf16)
            side[at(r, 0, 16), first + 256 : first + 512] = low
            if r == 0:
                side[at(0, 0, 16), first + 512 : first + 768] = jnp.zeros((16, 256), bf16)
            if r == SIDE - 1:
                side[at(r, 0, 16), first : first + 256] = jnp.zeros((16, 256), bf16)
            below = mbu[at(r + 1, 0, 16), :] if r < SIDE - 1 else None
            above = mbd[at(r - 1, 0, 16), :] if r > 0 else None
            for c in range(2):
                part = low[:, c * 128 : (c + 1) * 128]
                if r > 0:
                    side[at(r - 1, 0, 16), first + c * 128 : first + c * 128 + 128] = part * above
                if r < SIDE - 1:
                    side[at(r + 1, 0, 16), first + 512 + c * 128 : first + 640 + c * 128] = part * below

        def tap_back(spref, xref):
            def values(r, h):
                k = 8 + r * 16 + h * 8
                cols = []
                for c in range(2):
                    d = us[b, 2 + c, pl.ds(k, 8), :]
                    d = d + jnp.where(hasr[b][h], us[b, c, pl.ds(k + 1, 8), :], 0.0)
                    d = d + jnp.where(hasl[b][h], us[b, 4 + c, pl.ds(k - 1, 8), :], 0.0)
                    cols.append(d)
                dy = jnp.concatenate(cols, axis=1) * spref[at(r, h), :]
                dys[at(r, h), :] = dy
                return dy, dy * xref[at(r, h), :]

            return values

        def norm_grad(n, r, h, xref):
            return dys[at(r, h), :] * pick(n, r, h) - xref[at(r, h), :] * pick(5, r, h) - pick(6, r, h)

        def nine(xcref):
            return jnp.concatenate([side[mine, 0:768], xcref[mine, :], side[mine, 768:1536]], axis=1)

        def put_us(lhs, rhs_ref):
            for dx in range(3):
                u = nn(lhs, rhs_ref[:, dx * 256 : (dx + 1) * 256])
                for c in range(2):
                    us[b, dx * 2 + c, pl.ds(8, TOK), :] = u[:, c * 128 : (c + 1) * 128]
                yield 64 * (lhs.shape[1] // 256)

        def later(job):
            if b % 2:
                job(pl.ds(r0 - TOK, 2 * TOK))

        def weight_grad(acc, xref, dref, first, width):
            def job(two):
                for dx in range(3):
                    turned = []

                    def one(dy, dx=dx, turned=turned):
                        if not turned:
                            turned.append(xref[two, dx * 256 : (dx + 1) * 256].T)
                        cols = slice(dy * 256, (dy + 1) * 256)
                        grad = dref[two, first + dy * 256 : first + (dy + 1) * 256]
                        acc[pl.ds(dx * 256, 256), cols] += nn(turned[0], grad)

                    for dy in range(width):
                        fill.append(lambda dy=dy, one=one: one(dy))

            later(job)

        yield from masks()
        x0[mine, :] = nn(xt_ref[mine, :], ws[...])
        yield 128
        yield from forward_tables(0, x0, jnp.broadcast_to(row(0), (8, 256)), row(2), row(3))
        yield from silu_pass(0, x0, sp1, xc1, True)
        x1[mine, :] = nn(nine(xc1), wk1[...])
        yield 128 * 9
        bias1 = tbs[pl.ds((base + b) * 8, 8), :] + row(4)
        yield from forward_tables(1, x1, bias1, row(5), row(6))
        yield from silu_pass(1, x1, sp2, xc2, True)
        x2[mine, :] = x0[mine, :] + nn(nine(xc2), wk2[...])
        yield 128 * 9
        yield from forward_tables(2, x2, jnp.broadcast_to(row(0) + row(7), (8, 256)), row(8), row(9))
        for r in range(SIDE):
            halves = [x2[at(r, h), :] * pick(2, r, h) + pick(4, r, h) for h in range(2)]
            nrm[at(r, 0, 16), :] = jnp.concatenate(halves, axis=0).astype(bf16)
            if r % GRAIN == GRAIN - 1:
                yield 10 * GRAIN
        ks[mine, :] = nn(nrm[mine, :], wqkv[:, 256:512]).astype(bf16)
        qs[mine, :] = (nn(nrm[mine, :], wqkv[:, 0:256]) + row(10)).astype(bf16)
        vs[mine, :] = (nn(nrm[mine, :], wqkv[:, 512:768]) + row(11)).astype(bf16)
        yield 128 * 2

        def quadrant(p):
            col, line = p & 15, p >> 4
            left = jnp.where(line < lefts[b], 0, 1)
            right = jnp.where(line < rights[b], 2, 3)
            return jnp.where(col < cuts[b], left, right)

        qq = quadrant(lax.broadcasted_iota(jnp.int32, (1, TOK), 1))
        part = 64
        scores = []
        for k in range(TOK // part):
            scores.append(nt(qs[pl.ds(r0 + k * part, part), :], ks[mine, :]))
        yield 128
        for k in range(TOK // part):
            rows = pl.ds(r0 + k * part, part)
            qp = quadrant(k * part + lax.broadcasted_iota(jnp.int32, (part, 1), 0))
            s = jnp.where(qp == qq, scores[k], far_score)
            top = jnp.max(s, axis=1, keepdims=True)
            ex = jnp.exp((s - top) * (CH**-0.5))
            p = ex * (1.0 / jnp.sum(ex, axis=1, keepdims=True))
            prob[rows, :] = p
            pb[rows, :] = p.astype(bf16)
            yield 60
        mix[mine, :] = nn(pb[mine, :], vs[mine, :]).astype(bf16)
        yield 128
        x3[mine, :] = x2[mine, :] + nn(mix[mine, :], wo[...])
        yield 128
        yield from forward_tables(3, x3, jnp.broadcast_to(row(0) + row(7) + row(12), (8, 256)), row(13), row(14))
        yield from silu_pass(3, x3, sp4, xc3, False)

        z = nn(xc3[mine, :], wr[...])
        us[b, 0, pl.ds(8, TOK), :] = z[:, 0:128]
        us[b, 1, pl.ds(8, TOK), :] = z[:, 128:256]
        yield 128 * 3
        for r in range(SIDE):
            ql, qr = quads(r)
            inl = scale_ref[8 + (base + b) * 4 + ql]
            inr = scale_ref[8 + (base + b) * 4 + qr]
            for h in range(2):
                k = 8 + r * 16 + h * 8
                y = pltpu.roll(us[b, 0, pl.ds(k, 8), :], 64, 1)
                if r > 0:
                    y = y + us[b, 0, pl.ds(k - 16, 8), :] * mvu[at(r, h), :]
                if r < SIDE - 1:
                    y = y + us[b, 1, pl.ds(k + 16, 8), :] * mvd[at(r, h), :]
                inside = jnp.where(onleftn[b][h], inl, inr)
                err = jnp.where(lane < PIX, (y - tg_ref[at(r, h), :]) * inside, 0.0)
                lacc[...] += err * err
                xs[b, 0, pl.ds(k, 8), :] = (err * scale).astype(bf16).astype(f32)
            yield 15
        for r in range(SIDE):
            tile0, tile1 = [], []
            for h in range(2):
                k = 8 + r * 16 + h * 8
                t0 = pltpu.roll(xs[b, 0, pl.ds(k, 8), :], 64, 1)
                if r < SIDE - 1:
                    t0 = t0 + xs[b, 0, pl.ds(k + 16, 8), :] * mvd[at(r, h), :]
                t1 = jnp.zeros((8, 128), f32)
                if r > 0:
                    t1 = xs[b, 0, pl.ds(k - 16, 8), :] * mvu[at(r, h), :]
                tile0.append(t0)
                tile1.append(t1)
            dyp[at(r, 0, 16), 0:128] = jnp.concatenate(tile0, axis=0).astype(bf16)
            dyp[at(r, 0, 16), 128:256] = jnp.concatenate(tile1, axis=0).astype(bf16)
            if r % GRAIN == GRAIN - 1:
                yield 10 * GRAIN

        yield from put_us(dyp[mine, :], wrt)
        weight_grad(gr, xc3, dyp, 0, 1)
        s1, s2 = yield from crop_sums(tap_back(sp4, x3))
        sum3, db, dg = backward_tables(3, s1, s2, row(13))
        gv[13] += dg
        gv[14] += db
        gv[12] += sum3
        yield 200
        for r in range(SIDE):
            halves = []
            for h in range(2):
                d = norm_grad(3, r, h, x3)
                gtop[at(r, h), :] = d
                halves.append(d)
            dpo[at(r, 0, 16), :] = jnp.concatenate(halves, axis=0).astype(bf16)
            if r % GRAIN == GRAIN - 1:
                yield 14 * GRAIN
        dmx[mine, :] = nn(dpo[mine, :], wot[...]).astype(bf16)
        yield 128

        def grad_out(two):
            def job():
                ga[:, 768:1024] += nn(mix[two, :].T, dpo[two, :])

            fill.append(job)

        later(grad_out)
        vlow = vs[mine, :] * jnp.asarray(CH**-0.5, bf16)
        for k in range(TOK // part):
            rows = pl.ds(r0 + k * part, part)
            da = nt(dmx[rows, :], vlow)
            p = prob[rows, :]
            t = da * p
            dsb[rows, :] = (t - p * jnp.sum(t, axis=1, keepdims=True)).astype(bf16)
            yield 70
        dv = nn(pb[mine, :].T, dmx[mine, :])
        trip[mine, 512:768] = dv.astype(bf16)
        gv[11] += jnp.sum(dv.reshape(TOK // 8, 8, CH), axis=0)
        yield 128
        dq = nn(dsb[mine, :], ks[mine, :])
        trip[mine, 0:256] = dq.astype(bf16)
        gv[10] += jnp.sum(dq.reshape(TOK // 8, 8, CH), axis=0)
        yield 128
        dk = nn(dsb[mine, :].T, qs[mine, :])
        trip[mine, 256:512] = dk.astype(bf16)
        yield 128
        dys[mine, :] = nn(trip[mine, :], wat[...])
        yield 128 * 3

        def grad_triple(two):
            turned = []
            for k in range(3):

                def job(k=k):
                    if not turned:
                        turned.append(nrm[two, :].T)
                    ga[:, k * 256 : (k + 1) * 256] += nn(turned[0], trip[two, k * 256 : (k + 1) * 256])

                fill.append(job)

        later(grad_triple)

        def plain(r, h):
            dy = dys[at(r, h), :]
            return dy, dy * x2[at(r, h), :]

        s1, s2 = yield from crop_sums(plain)
        sum2, db, dg = backward_tables(2, s1, s2, row(8))
        gv[8] += dg
        gv[9] += db
        sum2 = sum2 + sum3
        gv[7] += sum2
        yield 200
        for r in range(SIDE):
            halves = []
            for h in range(2):
                d = norm_grad(2, r, h, x2) + gtop[at(r, h), :]
                gtop[at(r, h), :] = d
                halves.append(d)
            spread_grad(0, r, jnp.concatenate(halves, axis=0))
            if r % GRAIN == GRAIN - 1:
                yield 18 * GRAIN
        yield from put_us(side[mine, 0:768], wt2)
        weight_grad(gk2, xc2, side, 0, 3)
        s1, s2 = yield from crop_sums(tap_back(sp2, x1))
        sum1, db, dg = backward_tables(1, s1, s2, row(5))
        gv[5] += dg
        gv[6] += db
        gv[4] += sum1
        dtb[pl.ds((base + b) * 8, 8), :] = sum1
        yield 200
        for r in range(SIDE):
            spread_grad(768, r, jnp.concatenate([norm_grad(1, r, h, x1) for h in range(2)], axis=0))
            if r % GRAIN == GRAIN - 1:
                yield 16 * GRAIN
        yield from put_us(side[mine, 768:1536], wt1)
        weight_grad(gk1, xc1, side, 768, 3)
        s1, s2 = yield from crop_sums(tap_back(sp1, x0))
        sum0, db, dg = backward_tables(0, s1, s2, row(2))
        gv[2] += dg
        gv[3] += db
        gv[0] += sum0 + sum2
        yield 200
        for r in range(SIDE):
            halves = [norm_grad(0, r, h, x0) + gtop[at(r, h), :] for h in range(2)]
            dps[at(r, 0, 16), :] = jnp.concatenate(halves, axis=0).astype(bf16)
            if r % GRAIN == GRAIN - 1:
                yield 14 * GRAIN

        def grad_stem(two):
            def job():
                gs[...] += nn(xt_ref[two, :].T, dps[two, :])

            fill.append(job)

        later(grad_stem)

    clocks = {b: float(b * SKEW) for b in range(PAIR)}
    streams = {b: stream(b) for b in range(PAIR)}
    filled = 0.0
    while streams:
        b = min(streams, key=lambda k: clocks[k])
        try:
            clocks[b] += next(streams[b])
        except StopIteration:
            del streams[b]
        now = min([clocks[k] for k in streams], default=1e18)
        while fill and filled < now:
            filled = max(filled, now if now < 1e17 else 0.0) + FILLCOST
            fill.pop(0)()

    @pl.when(step == last)
    def _():
        low = dtb[...].astype(bf16)
        hp = hpre[...]
        sg = jax.nn.sigmoid(hp)
        gp = (nn((hp * sg).astype(bf16).T, low) * 0.5).astype(bf16)
        hg = nt(low, wpj[...]) * (sg * (1.0 + hp * (1.0 - sg)))
        ge = (nn(feat_ref[...].T, hg.astype(bf16)) * 0.5).astype(bf16)
        twice = {10: 1.0, 11: 1.0}
        rows = [jnp.sum(gv[4 if k == 1 else k], axis=0, keepdims=True) * twice.get(k, 0.5) for k in range(15)]
        gnorm = jnp.concatenate(rows + [jnp.zeros((1, 256), f32)], axis=0)
        gstem = gs[...].T
        shared = pltpu.roll(lacc[...], PIX, 1)
        shared = jnp.concatenate([shared, jnp.zeros((AROW - 8, 128), f32)], axis=0)
        gstem = gstem + jnp.concatenate([shared] * VIRT, axis=0)
        for dy in range(3):
            for lo in range(0, 768, 256):
                part = gr[pl.ds(lo, 256), (dy // 2) * 128 : (dy // 2) * 128 + 128]
                if dy == 1:
                    part = pltpu.roll(part, 64, 1)
                grn[pl.ds(dy * 768 + lo, 256), :] = part
        for core in range(2):

            @pl.when(geo_ref[3] == core)
            def _(core=core):
                for f in range(VIRT):
                    out_ref, z = (keep_ref, send_ref)[(f % 2) ^ core], f // 2
                    for dy in range(3):
                        lo, hi = max(f * KROW, dy * 768), min((f + 1) * KROW, (dy + 1) * 768)
                        if lo >= hi:
                            continue
                        src = pl.ds(lo - dy * 768, hi - lo)
                        dst = pl.ds(lo - f * KROW, hi - lo)
                        out_ref[z, dst, 0:256] = gk1[src, dy * 256 : (dy + 1) * 256].astype(bf16)
                        out_ref[z, dst, 256:512] = gk2[src, dy * 256 : (dy + 1) * 256].astype(bf16)
                    k = f * AROW
                    a1, a2, p0 = KROW, KROW + AROW, KROW + 2 * AROW
                    e0 = p0 + PROW
                    out_ref[z, a1:a2, :] = ga[k : k + AROW, 0:512].astype(bf16)
                    out_ref[z, a2:p0, :] = ga[k : k + AROW, 512:1024].astype(bf16)
                    out_ref[z, p0:e0, 0:256] = gp[f * 2 * PROW : f * 2 * PROW + PROW, :]
                    out_ref[z, p0:e0, 256:512] = gp[f * 2 * PROW + PROW : (f + 1) * 2 * PROW, :]
                    out_ref[z, e0:TROW, :] = ge[f * EROW : (f + 1) * EROW, :]
                    back = grn[pl.ds(f * KROW, 384), :].T[:TAIL, :]
                    keep = lax.broadcasted_iota(jnp.int32, (TAIL, 384), 1) < KROW
                    out_ref[z, TROW:PACKED, 0:384] = jnp.where(keep, back, 0.0).astype(bf16)
                    out_ref[z, TROW : TROW + 32, 384:512] = gstem[k : k + AROW, :].astype(bf16)
                    tile = gnorm[:, (f // 4) * 128 : (f // 4) * 128 + 128]
                    tile = pltpu.roll(tile, (128 - (f % 4) * AROW) % 128, 1)
                    keep = lax.broadcasted_iota(jnp.int32, (16, 128), 1) < AROW
                    out_ref[z, TROW + 32 : PACKED, 384:512] = jnp.where(keep, tile, 0.0).astype(bf16)
        loss_ref[...] = lacc[...]


SKEW = 700
FILLCOST = 128
GRAIN = 2


def run_step(packed, quad, geo, scal, feat, cp, tg, inv, cnt):
    canvases = cp.shape[0] // TOK
    whole = pl.BlockSpec(memory_space=pltpu.VMEM)
    smem = pl.BlockSpec(memory_space=pltpu.SMEM)

    def rows(n, lanes):
        return pl.BlockSpec((n, lanes), lambda i, *_: (i, 0))

    items = scratch_list(canvases)
    return pl.pallas_call(
        functools.partial(step_kernel, [name for name, _, _ in items]),
        grid_spec=pltpu.PrefetchScalarGridSpec(
            num_scalar_prefetch=2,
            grid=(canvases // PAIR,),
            in_specs=[
                smem, whole, whole, rows(ROWS, 128), rows(ROWS, 128), rows(8 * PAIR, 256), rows(8 * PAIR, 256),
            ],
            out_specs=[whole, whole, whole],
            scratch_shapes=[pltpu.VMEM(shape, dtype) for _, shape, dtype in items],
        ),
        out_shape=[
            jax.ShapeDtypeStruct((VIRT // 2, PACKED, 512), bf16),
            jax.ShapeDtypeStruct((VIRT // 2, PACKED, 512), bf16),
            jax.ShapeDtypeStruct((8, 128), f32),
        ],
        compiler_params=pltpu.CompilerParams(
            dimension_semantics=("arbitrary",), vmem_limit_bytes=60 * 1024 * 1024
        ),
        name="unet_step",
    )(quad, geo, scal, packed, feat, cp, tg, inv, cnt)


def patch_kernel(clean_ref, noise_ref, cp_ref, np_ref, staged):
    n = clean_ref.shape[0]
    slot = staged.shape[0] // (2 * SIDE)
    for k, ref in enumerate((clean_ref, noise_ref)):
        for r in range(SIDE):
            for c in range(3):
                staged[pl.ds((k * SIDE + r) * slot, n), c * 256 : (c + 1) * 256] = ref[:, c * 4096 + r * 256 : c * 4096 + r * 256 + 256]
    src = lax.broadcasted_iota(jnp.int32, (768, 256), 0)
    place = ((src >> 2) & 15) * 128 + (src >> 8) * 16 + ((src >> 6) & 3) * 4 + (src & 3)
    for j in range(SIDE // 2):
        lane = lax.broadcasted_iota(jnp.int32, (768, 256), 1) + j * 256
        out = nn(staged[...], (place == lane).astype(bf16))
        for k, ref in enumerate((cp_ref, np_ref)):
            for r in range(SIDE):
                row = (k * SIDE + r) * slot
                for i in range(2):
                    ref[pl.ds(r * SIDE + 2 * j + i, n, stride=TOK), :] = out[row : row + n, i * 128 : (i + 1) * 128]


def patches(clean, noise):
    n = clean.shape[0]
    slot = -(-n // 16) * 16
    whole = pl.BlockSpec(memory_space=pltpu.VMEM)
    return pl.pallas_call(
        patch_kernel,
        in_specs=[whole, whole],
        out_specs=[whole, whole],
        out_shape=[jax.ShapeDtypeStruct((n * TOK, 128), f32)] * 2,
        scratch_shapes=[pltpu.VMEM((2 * SIDE * slot, 768), bf16)],
        compiler_params=pltpu.CompilerParams(vmem_limit_bytes=48 * 1024 * 1024),
        name="patches",
    )(clean, noise)


def pack_kernel(stem, kernels, embed, project, attention, readout, norm, out):
    a1, a2, p0 = KROW, KROW + AROW, KROW + 2 * AROW
    e0 = p0 + PROW
    out[0:a1, :] = kernels[...].astype(bf16)
    out[a1:a2, :] = attention[:, 0:512].astype(bf16)
    out[a2:p0, :] = attention[:, 512:1024].astype(bf16)
    out[p0:e0, 0:256] = project[0:PROW, :].astype(bf16)
    out[p0:e0, 256:512] = project[PROW : 2 * PROW, :].astype(bf16)
    out[e0:TROW, :] = embed[...].astype(bf16)
    out[TROW:PACKED, 256:512] = jnp.zeros((TAIL, 256), bf16)
    out[TROW:PACKED, 0:KROW] = readout[...].astype(bf16)
    out[TROW : TROW + 32, 384 : 384 + PIX] = stem[...].astype(bf16)
    out[TROW + 32 : TROW + 47, 384 : 384 + AROW] = norm[...].astype(bf16)


def pack_weights(masters):
    if masters[1].shape[0] != KROW:
        return pack_rows([w.astype(bf16) for w in masters])
    stem, kernels, embed, project, attention, readout, norm = masters
    return pl.pallas_call(
        pack_kernel, out_shape=jax.ShapeDtypeStruct((PACKED, 512), bf16), name="pack_weights"
    )(stem, kernels, embed, project, attention, readout.T, norm.T)


def update_kernel(place, rate, own, first, second, *refs):
    loss_out, total = refs[-2:]
    refs = refs[:-2]
    half, quarter = PACKED // 4, PACKED // 8
    for k in range(2):
        near, far = place[k], place[1 - k]
        at = k * 2 * half
        total[pl.ds(pl.multiple_of(at + near * half + far * quarter, 8), quarter), :] = own[k].astype(f32)
        total[pl.ds(pl.multiple_of(at + near * half + (1 - far) * quarter, 8), quarter), :] = first[k].astype(f32)
        there = at + (1 - near) * half
        total[pl.ds(pl.multiple_of(there + far * quarter, 8), quarter), :] = second[k, 0].astype(f32)
        total[pl.ds(pl.multiple_of(there + (1 - far) * quarter, 8), quarter), :] = second[k, 1].astype(f32)
    shared = total[TROW : TROW + 8, 384:512]
    lane = lax.broadcasted_iota(jnp.int32, (8, 128), 1)
    shared = jnp.where((lane >= PIX) & (lane < 2 * PIX), shared, 0.0)
    loss_out[...] = jnp.sum(shared, axis=(0, 1), keepdims=True) * rate[1]
    a1, a2, p0 = KROW, KROW + AROW, KROW + 2 * AROW
    e0 = p0 + PROW
    everything = slice(None)
    cuts = [
        (0, everything, everything, total[TROW : TROW + 32, 384:512][:, :PIX]),
        (1, everything, everything, total[0:a1, :]),
        (2, everything, everything, total[e0:TROW, :]),
        (3, slice(0, PROW), everything, total[p0:e0, 0:256]),
        (3, slice(PROW, 2 * PROW), everything, total[p0:e0, 256:512]),
        (4, everything, slice(0, 512), total[a1:a2, :]),
        (4, everything, slice(512, 1024), total[a2:p0, :]),
        (5, everything, everything, total[TROW:PACKED, 0:384][:, :KROW]),
        (6, everything, everything, total[TROW + 32 : PACKED, 384:512][:15, :AROW]),
    ]
    for n, rows, lanes, grad in cuts:
        w, m, a, m_out, w_out, a_out = [refs[n + 7 * j] for j in range(6)]
        m_next = momentum_rate * m[rows, lanes] + grad
        w_next = w[rows, lanes] - rate[0] * (grad + momentum_rate * m_next)
        m_out[rows, lanes] = m_next
        w_out[rows, lanes] = w_next
        a_out[rows, lanes] = average_rate * a[rows, lanes] + (1.0 - average_rate) * w_next


def turn(arrays):
    return [x.T if k in (5, 6) else x for k, x in enumerate(arrays)]


def update_fused(place, rate, own, first, second, masters, moments, averages):
    whole = pl.BlockSpec(memory_space=pltpu.VMEM)
    smem = pl.BlockSpec(memory_space=pltpu.SMEM)
    state = turn(masters) + turn(moments) + turn(averages)
    out = pl.pallas_call(
        update_kernel,
        in_specs=[smem, smem] + [whole] * 24,
        out_specs=[whole] * 22,
        out_shape=[jax.ShapeDtypeStruct(x.shape, f32) for x in state] + [jax.ShapeDtypeStruct((1, 1), f32)],
        scratch_shapes=[pltpu.VMEM((PACKED, 512), f32)],
        compiler_params=pltpu.CompilerParams(vmem_limit_bytes=32 * 1024 * 1024),
        name="update",
    )(place, rate, own, first, second, *state)
    return (out[21][0, 0],) + tuple(turn(out[0:7]) + turn(out[7:14]) + turn(out[14:21]))


def signal_table():
    beta = np.linspace(0.0001, 0.02, TSTEPS, dtype=np.float64)
    return np.exp(np.cumsum(np.log(1.0 - beta))).astype(np.float32)


def time_features(time_steps):
    half_width = TEMB // 2
    frequency = jnp.exp(-math.log(10000.0) * jnp.arange(half_width, dtype=f32) / (half_width - 1))
    angles = time_steps.astype(f32)[..., None] * frequency
    return jnp.concatenate([jnp.sin(angles), jnp.cos(angles)], axis=-1)


def prepare(clean, noise, lab, time_steps, count, core):
    canvases = lab.shape[0]
    cut = jnp.sum(jnp.all(lab == lab[:, :, :1], axis=1).astype(jnp.int32), axis=1)
    left = jnp.sum((lab[:, :, 0] == lab[:, :1, 0]).astype(jnp.int32), axis=1)
    right = jnp.sum((lab[:, :, -1] == lab[:, :1, -1]).astype(jnp.int32), axis=1)
    own = jnp.stack([lab[:, 0, 0], lab[:, -1, 0], lab[:, 0, -1], lab[:, -1, -1]], axis=1)
    area = jnp.stack(
        [cut * left, cut * (SIDE - left), (SIDE - cut) * right, (SIDE - cut) * (SIDE - right)], axis=1
    ).astype(f32)
    geo = jnp.stack([cut, left, right] + [jnp.full_like(cut, core)] * 5, axis=1).reshape(-1)
    line = jnp.arange(SIDE, dtype=jnp.int32)
    quad = (line >= left[:, None]).astype(jnp.int32) + 2 * (line >= right[:, None]).astype(jnp.int32)
    quad = quad.reshape(-1)
    hit = own[..., None] == jnp.arange(1, CROPS + 1, dtype=jnp.int32)
    times = jnp.sum(jnp.where(hit, time_steps[:, None, :], 0), axis=-1)
    eight = np.array([0, 0, 2, 2, 1, 1, 3, 3])
    feat = time_features(times[:, eight]).astype(bf16).reshape(-1, TEMB)
    area8 = area[:, eight].reshape(-1, 1)
    picked = times[..., None] == jnp.arange(TSTEPS, dtype=jnp.int32)
    chosen = jnp.sum(jnp.where(picked, jnp.asarray(signal_table()), 0.0), axis=-1)
    inv = jnp.broadcast_to(1.0 / jnp.maximum(area8, 1.0), (8 * canvases, CH))
    cnt = jnp.broadcast_to(area8, (8 * canvases, CH))
    inside = (own > 0).astype(f32)
    levels = [inside, jnp.sqrt(chosen), jnp.sqrt(1.0 - chosen)]
    scal = jnp.concatenate([jnp.full((8,), 2.0 / count, f32)] + [x.reshape(-1) for x in levels])
    cp, tg = patches(clean, noise)
    return quad, geo, scal, feat, cp, tg, inv, cnt


def exchange(value, axis, bit):
    return lax.ppermute(value, axis, [(i, i ^ bit) for i in range(lax.axis_size(axis))])


def sum_over_all(value):
    for axis in ("fsdp", "dp"):
        bit = 1
        while bit < lax.axis_size(axis):
            value = value + exchange(value, axis, bit)
            bit *= 2
    return value


def join(a, b):
    return (a.astype(f32) + b.astype(f32)).astype(bf16)


def halves(value, which):
    n = value.shape[1] // 2
    low, high = value[:, :n], value[:, n:]
    return jnp.where(which == 0, low, high), jnp.where(which == 0, high, low)


def reduce_grads(keep, send):
    total = join(keep, exchange(send, "fsdp", 1))
    near, far = lax.axis_index("dp") % 2, lax.axis_index("dp") // 2
    n = total.shape[1] // 2
    parts = [total[:, :n], total[:, n:]]
    for first, second in (((near, 1), (far, 2)), ((far, 2), (near, 1))):
        split = [halves(parts[0], first[0]), halves(parts[1], second[0])]
        came = [exchange(split[0][1], "dp", first[1]), exchange(split[1][1], "dp", second[1])]
        parts = [join(split[0][0], came[0]), join(split[1][0], came[1])]
    blocks = jnp.stack(parts, axis=1)
    chips, shards = blocks.shape[0], lax.axis_size("fsdp")
    chip = lax.axis_index("fsdp") // 2
    own = lax.dynamic_index_in_dim(blocks, chip, 0, keepdims=False).astype(f32)
    for j in range(1, chips):
        out = lax.dynamic_index_in_dim(blocks, (chip + j) % chips, 0, keepdims=False)
        own = own + lax.ppermute(out, "fsdp", [(i, (i + 2 * j) % shards) for i in range(shards)]).astype(f32)
    own = own.astype(bf16)
    first = jnp.stack([exchange(own[0], "dp", 2), exchange(own[1], "dp", 1)])
    both = jnp.stack([own, first], axis=1)
    second = jnp.stack([exchange(both[0], "dp", 1), exchange(both[1], "dp", 2)])
    return jnp.stack([near, far]).astype(jnp.int32), own, first, second


def assemble(place, own, first, second):
    n = own.shape[1]
    parts = []
    for k in range(2):
        near, far = place[k], place[1 - k]
        mine = jnp.where(far == 0, jnp.concatenate([own[k], first[k]]), jnp.concatenate([first[k], own[k]]))
        s = second[k]
        theirs = jnp.where(far == 0, jnp.concatenate([s[0], s[1]]), jnp.concatenate([s[1], s[0]]))
        parts.append(jnp.where(near == 0, jnp.concatenate([mine, theirs]), jnp.concatenate([theirs, mine])))
    return jnp.concatenate(parts).astype(f32)


def on_device(clean, noise, crop_labels, time_steps, *state):
    masters, moments, averages = state[0:7], state[7:14], state[14:21]
    shards = lax.axis_size("fsdp")
    core = lax.axis_index("fsdp") % 2
    packed = lax.all_gather(pack_weights(masters), "fsdp", axis=0, tiled=False)
    count = sum_over_all(PATCH * PATCH * jnp.sum((crop_labels > 0).astype(f32)).reshape(1, 1))[0, 0]
    direct = shards == VIRT
    inputs = prepare(clean, noise, crop_labels, time_steps, count, core if direct else 0)
    keep, send, loss = run_step(repack(packed, shards, VIRT), *inputs)
    if not direct:
        blocks = jnp.stack([keep, send], axis=1).reshape(VIRT, PACKED, 512)
        blocks = repack(blocks, VIRT, shards)
        blocks = blocks.reshape(shards // 2, 2, *blocks.shape[1:])
        keep = lax.dynamic_index_in_dim(blocks, core, 1, keepdims=False)
        send = lax.dynamic_index_in_dim(blocks, 1 - core, 1, keepdims=False)
    place, own, first, second = reduce_grads(keep, send)
    rate = lr_scale * jnp.sqrt(count)
    if direct:
        rates = jnp.stack([rate, 1.0 / count])
        return update_fused(place, rates, own, first, second, masters, moments, averages)
    total_loss = sum_over_all(jnp.sum(loss).reshape(1, 1))[0, 0]
    cut = [masters[1].shape[0], masters[0].shape[0], masters[3].shape[0], masters[2].shape[0]]
    grads = unpack_rows(assemble(place, own, first, second), *cut)
    moment_next = tuple(momentum_rate * m + g for m, g in zip(moments, grads))
    master_next = tuple(w - rate * (g + momentum_rate * m) for w, g, m in zip(masters, grads, moment_next))
    average_next = tuple(average_rate * a + (1.0 - average_rate) * w for a, w in zip(averages, master_next))
    return (total_loss / count,) + moment_next + master_next + average_next


def solution(mesh):
    split = P(("dp", "fsdp"), None)
    in_specs = (split, split, P(("dp", "fsdp"), None, None), split) + (P("fsdp", None),) * 21
    out_specs = (P(),) + (P("fsdp", None),) * 21
    return jax.shard_map(on_device, mesh=mesh, in_specs=in_specs, out_specs=out_specs, check_vma=False)
```

```python
import functools
import math

import jax
import jax.numpy as jnp
import numpy as np
from jax import lax
from jax.experimental import pallas as pl
from jax.experimental.pallas import tpu as pltpu
from jax.sharding import PartitionSpec as P

GROUPS = 32
TEMB = 128
SIDE = 16
PATCH = 4
CROPS = 4
TSTEPS = 1000
TOK = SIDE * SIDE
CH = 256
PIX = 3 * PATCH * PATCH
PAIR = 4
ROWS = PAIR * TOK
VIRT = 8
TAIL = 48

eps_norm = 1e-05
lr_scale = 0.01
momentum_rate = 0.5
average_rate = 0.5
far_score = -1e30
f32 = jnp.float32
bf16 = jnp.bfloat16


def pad_to(value, rows, lanes):
    return jnp.pad(value, ((0, rows - value.shape[0]), (0, lanes - value.shape[1])))


def pack_rows(parts):
    stem, kernels, embed, project, attention, readout, norm = parts
    half = project.shape[0] // 2
    small = jnp.concatenate([pad_to(stem, 32, 128), pad_to(norm.T, 16, 128)], axis=0)
    tail = jnp.concatenate([pad_to(readout.T, TAIL, 384), small], axis=1)
    rows = [kernels, attention[:, :512], attention[:, 512:]]
    rows += [jnp.concatenate([project[:half], project[half:]], axis=1), embed, tail]
    rows = jnp.concatenate(rows, axis=0)
    return pad_to(rows, -(-rows.shape[0] // 8) * 8, 512)


def unpack_rows(rows, k, a, p, e):
    half = p // 2
    at = [0, k, k + a, k + 2 * a, k + 2 * a + half, k + 2 * a + half + e, k + 2 * a + half + e + TAIL]
    kernels, left, right, halves, embed, tail = [rows[at[i] : at[i + 1]] for i in range(6)]
    project = jnp.concatenate([halves[:, :256], halves[:, 256:]], axis=0)
    stem, norm = tail[:a, 384 : 384 + PIX], tail[32 : 32 + 15, 384 : 384 + a].T
    return stem, kernels, embed, project, jnp.concatenate([left, right], axis=1), tail[:, :k].T, norm


def repack(packed, parts_now, parts_next):
    if parts_now == parts_next:
        return packed
    cut = [n // parts_now for n in (9 * CH, CH, 2 * CH, CH // 2)]
    pieces = jax.vmap(lambda rows: unpack_rows(rows, *cut))(packed)
    whole = [piece.reshape(-1, piece.shape[-1]) for piece in pieces]
    split = [piece.reshape(parts_next, -1, piece.shape[-1]) for piece in whole]
    return jax.vmap(lambda *p: pack_rows(p))(*split)


KROW = 9 * CH // VIRT
AROW = CH // VIRT
PROW = CH // VIRT
EROW = TEMB // VIRT
TROW = KROW + 2 * AROW + PROW + EROW
PACKED = TROW + TAIL
CUT = PACKED // 2
PART = (PACKED - CUT) // 2


def lane_groups(value):
    lane = lax.broadcasted_iota(jnp.int32, (8, 128), 1)
    tiles = []
    for t in range(2):
        x = value[:, t * 128 : (t + 1) * 128]
        for s in (1, 2, 4):
            x = x + jnp.where((lane & s) == 0, pltpu.roll(x, 128 - s, 1), pltpu.roll(x, s, 1))
        tiles.append(x)
    return jnp.concatenate(tiles, axis=1)


def quad_rows(q0, q1, q2, q3):
    sub = lax.broadcasted_iota(jnp.int32, (8, 128), 0)
    tiles = []
    for t in range(2):
        a, b, c, d = [q[:, t * 128 : (t + 1) * 128] for q in (q0, q1, q2, q3)]
        low = sub < 4
        u = jnp.where(low, a, pltpu.roll(b, 4, 0)) + jnp.where(low, pltpu.roll(a, 4, 0), b)
        v = jnp.where(low, c, pltpu.roll(d, 4, 0)) + jnp.where(low, pltpu.roll(c, 4, 0), d)
        even = (sub & 2) == 0
        w = jnp.where(even, u, pltpu.roll(v, 2, 0)) + jnp.where(even, pltpu.roll(u, 6, 0), v)
        w = w + jnp.where((sub & 1) == 0, pltpu.roll(w, 7, 0), pltpu.roll(w, 1, 0))
        tiles.append(w)
    return jnp.concatenate(tiles, axis=1)


QUAD_ROW = (0, 4, 2, 6)


def nt(a, b):
    return lax.dot_general(a, b, (((1,), (1,)), ((), ())), preferred_element_type=f32)


def nn(a, b):
    return lax.dot_general(a, b, (((1,), (0,)), ((), ())), preferred_element_type=f32)


PADROWS = TOK + 16


def scratch_list(canvases):
    n = 8 * canvases
    items = [
        ("wk1", (2304, 256), bf16), ("wk2", (2304, 256), bf16), ("wt1", (768, 768), bf16), ("wt2", (768, 768), bf16),
        ("wr", (768, 256), bf16), ("wrt", (256, 768), bf16), ("wqkv", (256, 768), bf16), ("wat", (768, 256), bf16),
        ("wo", (256, 256), bf16), ("wot", (256, 256), bf16), ("ws", (128, 256), bf16), ("wpj", (512, 256), bf16),
        ("wem", (128, 512), bf16), ("vec", (16, 256), f32), ("tbs", (n, 256), f32), ("hpre", (n, 512), f32),
        ("grn", (2304 + 96, 128), f32), ("low", (4, VIRT, PACKED - CUT, 128), bf16), ("sc", (8, 128), f32),
        ("xt", (ROWS, 128), bf16),
        ("gk1", (768, 768), f32), ("gk2", (768, 768), f32), ("gr", (768, 256), f32), ("ga", (256, 1024), f32),
        ("gs", (128, 256), f32), ("gv", (15, 8, 256), f32), ("dtb", (n, 256), f32), ("lacc", (8, 128), f32),
        ("x0", (ROWS, 256), f32), ("x1", (ROWS, 256), f32), ("x2", (ROWS, 256), f32), ("x3", (ROWS, 256), f32),
        ("sp1", (ROWS, 256), f32), ("sp2", (ROWS, 256), f32), ("sp4", (ROWS, 256), f32),
        ("xs", (PAIR, 2, PADROWS, 128), f32), ("us", (PAIR, 6, PADROWS, 128), f32),
        ("side", (ROWS, 1536), bf16),
        ("xc1", (ROWS, 768), bf16), ("xc2", (ROWS, 768), bf16), ("xc3", (ROWS, 768), bf16),
        ("nrm", (ROWS, 256), bf16), ("qs", (ROWS, 256), bf16), ("ks", (ROWS, 256), bf16), ("vs", (ROWS, 256), bf16),
        ("prob", (ROWS, 256), f32), ("pb", (ROWS, 256), bf16), ("dsb", (ROWS, 256), bf16), ("mix", (ROWS, 256), bf16), ("dmx", (ROWS, 256), bf16), ("dpo", (ROWS, 256), bf16),
        ("gtop", (ROWS, 256), f32), ("dys", (ROWS, 256), f32),
        ("dps", (ROWS, 256), bf16),
        ("dyp", (ROWS, 256), bf16), ("trip", (ROWS, 768), bf16),
        ("mvu", (ROWS, 128), f32), ("mvd", (ROWS, 128), f32), ("mbu", (ROWS, 128), bf16), ("mbd", (ROWS, 128), bf16),
        ("ctab", (PAIR, 4, 4, 8, 256), f32),
    ]
    for b in range(PAIR):
        items += [(f"pref{b}", (2, 2, 17, 8, 256), f32)]
        items += [(f"tab{b}_{slot}", (4, 2, 8, 256), f32) for slot in range(7)]
    return items


def step_kernel(names, *refs):
    quad_ref, geo_ref, scale_ref, up_ref, oa_ref, ob_ref, ca_ref, cb_ref, feat_ref, cp_ref, tg_ref = refs[:11]
    keep_ref, send_ref, loss_ref, total_ref = refs[11:15]
    S = dict(zip(names, refs[15:]))
    wk1, wk2, wt1, wt2, wr, wrt, wqkv, wat, wo, wot = [S[k] for k in ("wk1", "wk2", "wt1", "wt2", "wr", "wrt", "wqkv", "wat", "wo", "wot")]
    ws, wpj, wem, vec, tbs, hpre = [S[k] for k in ("ws", "wpj", "wem", "vec", "tbs", "hpre")]
    gk1, gk2, gr, ga, gs, gv, dtb, lacc = [S[k] for k in ("gk1", "gk2", "gr", "ga", "gs", "gv", "dtb", "lacc")]
    x0, x1, x2, x3, sp1, sp2, sp4, xs, us = [S[k] for k in ("x0", "x1", "x2", "x3", "sp1", "sp2", "sp4", "xs", "us")]
    side, xc1, xc2, xc3, nrm, qs, ks, vs = [S[k] for k in ("side", "xc1", "xc2", "xc3", "nrm", "qs", "ks", "vs")]
    prob, mix, dmx, dpo, gtop, dys = [S[k] for k in ("prob", "mix", "dmx", "dpo", "gtop", "dys")]
    dps, dyp, trip = [S[k] for k in ("dps", "dyp", "trip")]
    mvu, mvd, mbu, mbd, ctab = [S[k] for k in ("mvu", "mvd", "mbu", "mbd", "ctab")]
    grn, xt_ref, pb, dsb, low, sc = S["grn"], S["xt"], S["pb"], S["dsb"], S["low"], S["sc"]
    pref = [S[f"pref{b}"] for b in range(PAIR)]
    tab = [[S[f"tab{b}_{slot}"] for slot in range(7)] for b in range(PAIR)]
    step = pl.program_id(0)
    last = pl.num_programs(0) - 1
    canvases = tbs.shape[0] // 8

    @pl.when(step == 0)
    def _():
        core, chip, copy = geo_ref[3], geo_ref[4], geo_ref[5]
        tokens = jnp.zeros((16, 128), f32)
        for p, (a_ref, b_ref) in enumerate(((oa_ref, ob_ref), (ca_ref, cb_ref))):
            for s in range(4):
                for j in range(4):
                    f = ((chip - j) & 3) * 2 + (core ^ p)
                    low[copy ^ s, f, 0:PART, :] = a_ref[s, j]
                    low[copy ^ ((s >> 1) | ((s & 1) << 1)), f, PART : 2 * PART, :] = b_ref[s, j, 0:PART, :]
                    tokens = tokens + b_ref[s, j, PART : PART + 16, :].astype(f32)
        lanes = lax.broadcasted_iota(jnp.int32, (16, 128), 1)
        tokens = jnp.sum(tokens * jnp.where(lanes == 0, 64.0, 1.0), axis=(0, 1), keepdims=True)
        count = scale_ref[0] + PATCH * PATCH * tokens
        sc[...] = jnp.broadcast_to(2.0 / count, (8, 128))
        total_ref[...] = jnp.broadcast_to(count, (8, 128))

        def lower(f, lo, hi, first, end):
            tiles = [low[q, f, lo - CUT : hi - CUT, :] for q in range(first // 128, end // 128)]
            return tiles[0] if len(tiles) == 1 else jnp.concatenate(tiles, axis=1)

        a1, a2, p0 = KROW, KROW + AROW, KROW + 2 * AROW
        e0 = p0 + PROW
        for f in range(VIRT):
            wk1[pl.ds(f * KROW, CUT), :] = up_ref[f, :, 0:256]
            wk2[pl.ds(f * KROW, CUT), :] = up_ref[f, :, 256:512]
            wk1[pl.ds(f * KROW + CUT, KROW - CUT), :] = lower(f, CUT, KROW, 0, 256)
            wk2[pl.ds(f * KROW + CUT, KROW - CUT), :] = lower(f, CUT, KROW, 256, 512)
            back = lower(f, TROW, PACKED, 0, 384).astype(f32)
            back = jnp.concatenate([back, jnp.zeros((128 - TAIL, 384), f32)], axis=0).T
            grn[pl.ds(f * KROW, KROW), :] = back[:KROW, :]
            wqkv[pl.ds(f * AROW, AROW), 0:512] = lower(f, a1, a2, 0, 512)
            wqkv[pl.ds(f * AROW, AROW), 512:768] = lower(f, a2, p0, 0, 256)
            wo[pl.ds(f * AROW, AROW), :] = lower(f, a2, p0, 256, 512)
            wpj[pl.ds(f * 2 * PROW, PROW), :] = lower(f, p0, e0, 0, 256)
            wpj[pl.ds(f * 2 * PROW + PROW, PROW), :] = lower(f, p0, e0, 256, 512)
            wem[pl.ds(f * EROW, EROW), :] = lower(f, e0, TROW, 0, 512)
        stem = jnp.concatenate([lower(f, TROW, TROW + 32, 384, 512) for f in range(VIRT)], axis=0)
        ws[...] = stem.T
        for t in range(2):
            tile = jnp.zeros((16, 128), f32)
            for j in range(4):
                part = lower(4 * t + j, TROW + 32, PACKED, 384, 512).astype(f32)
                part = jnp.where(lax.broadcasted_iota(jnp.int32, (16, 128), 1) < AROW, part, 0.0)
                tile = tile + (pltpu.roll(part, j * AROW, 1) if j else part)
            vec[:, t * 128 : (t + 1) * 128] = tile
        for dy in range(3):
            for dx in range(3):
                rows = pl.ds((dy * 3 + dx) * 256, 256)
                wt1[pl.ds(dy * 256, 256), dx * 256 : (dx + 1) * 256] = wk1[rows, :].T
                wt2[pl.ds(dy * 256, 256), dx * 256 : (dx + 1) * 256] = wk2[rows, :].T
        for j in range(3):
            wat[pl.ds(j * 256, 256), :] = wqkv[:, j * 256 : (j + 1) * 256].T
        wot[...] = wo[...].T
        for dx in range(3):
            rows = [grn[pl.ds(dy * 768 + dx * 256, 256), :] for dy in range(3)]
            tile0 = (rows[0] + pltpu.roll(rows[1], 64, 1)).astype(bf16)
            tile1 = rows[2].astype(bf16)
            wr[pl.ds(dx * 256, 256), 0:128] = tile0
            wr[pl.ds(dx * 256, 256), 128:256] = tile1
            wrt[0:128, dx * 256 : (dx + 1) * 256] = tile0.T
            wrt[128:256, dx * 256 : (dx + 1) * 256] = tile1.T
        hp = nn(feat_ref[...], wem[...])
        hpre[...] = hp
        tbs[...] = nn(jax.nn.silu(hp).astype(bf16), wpj[...]) + vec[1:2, :]
        grn[pl.ds(2304, 96), :] = jnp.zeros((96, 128), f32)
        for ref in [gk1, gk2, gr, ga, gs, gv, lacc] + pref:
            ref[...] = jnp.zeros_like(ref)

    base = step * PAIR
    cuts = [geo_ref[(base + b) * 8] for b in range(PAIR)]
    lefts = [geo_ref[(base + b) * 8 + 1] for b in range(PAIR)]
    rights = [geo_ref[(base + b) * 8 + 2] for b in range(PAIR)]
    iota8 = lax.broadcasted_iota(jnp.int32, (8, 256), 0)
    iota8n = lax.broadcasted_iota(jnp.int32, (8, 128), 0)
    onleft = [[iota8 < (cuts[b] - 8 * h) for h in range(2)] for b in range(PAIR)]
    onleftn = [[iota8n < (cuts[b] - 8 * h) for h in range(2)] for b in range(PAIR)]
    hasl = [[(iota8n + 8 * h != 0) & (iota8n + 8 * h != cuts[b]) for h in range(2)] for b in range(PAIR)]
    hasr = [[(iota8n + 8 * h != 15) & (iota8n + 8 * h != cuts[b] - 1) for h in range(2)] for b in range(PAIR)]
    lane = lax.broadcasted_iota(jnp.int32, (8, 128), 1)
    fill = []

    def row(k):
        return vec[k : k + 1, :]

    def stream(b):
        r0 = b * TOK
        mine = pl.ds(r0, TOK)
        areas = [scale_ref[8 + 12 * canvases + (base + b) * 4 + q] for q in range(4)]
        sub = lax.broadcasted_iota(jnp.int32, (8, 256), 0)
        cnt = jnp.where(sub < 4, jnp.where(sub < 2, areas[0], areas[2]), jnp.where(sub < 6, areas[1], areas[3]))
        inv = 1.0 / jnp.maximum(cnt, 1.0)

        def at(r, h=0, n=8):
            return pl.ds(r0 + r * 16 + h * 8, n)

        def kind(r):
            return quad_ref[(base + b) * SIDE + r]

        def quads(r):
            t = kind(r)
            return t & 1, 2 + (t >> 1)

        def masks():
            for r in range(SIDE):
                upl = ((lefts[b] != r) & (r > 0)).astype(f32)
                upr = ((rights[b] != r) & (r > 0)).astype(f32)
                dnl = ((lefts[b] != r + 1) & (r < SIDE - 1)).astype(f32)
                dnr = ((rights[b] != r + 1) & (r < SIDE - 1)).astype(f32)
                up = jnp.concatenate([jnp.where(onleftn[b][h], upl, upr) for h in range(2)], axis=0)
                dn = jnp.concatenate([jnp.where(onleftn[b][h], dnl, dnr) for h in range(2)], axis=0)
                mvu[at(r, 0, 16), :] = up
                mvd[at(r, 0, 16), :] = dn
                mbu[at(r, 0, 16), :] = up.astype(bf16)
                mbd[at(r, 0, 16), :] = dn.astype(bf16)
                ql, qr = quads(r)
                level = 8 + 4 * canvases + (base + b) * 4
                al, ar = scale_ref[level + ql], scale_ref[level + qr]
                sl, sr = scale_ref[level + 4 * canvases + ql], scale_ref[level + 4 * canvases + qr]
                mixed = []
                for h in range(2):
                    m = onleftn[b][h]
                    noisy = jnp.where(m, sl, sr) * tg_ref[at(r, h), :]
                    mixed.append(jnp.where(m, al, ar) * cp_ref[at(r, h), :] + noisy)
                xt_ref[at(r, 0, 16), :] = jnp.concatenate(mixed, axis=0).astype(bf16)
            yield 100

        def put_table(slot, table):
            of = [jnp.broadcast_to(table[k : k + 1, :], (8, 256)) for k in QUAD_ROW]
            for t in range(4):
                for h in range(2):
                    tab[b][slot][t, h] = jnp.where(onleft[b][h], of[t & 1], of[2 + (t >> 1)])

        def pick(slot, r, h):
            return tab[b][slot][kind(r), h]

        def crop_sums(values_of):
            total = [None, None]
            left = [None, None]
            p = pref[b]
            for r in range(SIDE):
                halves = [values_of(r, h) for h in range(2)]
                for j in range(2):
                    a0, a1 = halves[0][j], halves[1][j]
                    lp = jnp.where(onleft[b][0], a0, 0.0) + jnp.where(onleft[b][1], a1, 0.0)
                    tp = a0 + a1
                    left[j] = lp if r == 0 else left[j] + lp
                    total[j] = tp if r == 0 else total[j] + tp
                    p[j, 0, r + 1] = left[j]
                    p[j, 1, r + 1] = total[j]
                if r % GRAIN == GRAIN - 1:
                    yield 16 * GRAIN
            got = []
            for j in range(2):
                q0 = p[j, 0, lefts[b]]
                q1 = left[j] - q0
                q2 = p[j, 1, rights[b]] - p[j, 0, rights[b]]
                q3 = (total[j] - left[j]) - q2
                got.append(quad_rows(q0, q1, q2, q3))
            yield 100
            return got

        def forward_tables(n, xref, bias, gain, shift):
            def both(r, h):
                x = xref[at(r, h), :]
                return x, x * x

            s1, s2 = yield from crop_sums(both)
            own = s1 * inv
            mean = lane_groups(own + bias) * 0.125
            apart = own + bias - mean
            var = lane_groups(jnp.maximum(s2 * inv - own * own, 0.0) + apart * apart) * 0.125
            rs = lax.rsqrt(var + eps_norm)
            a = rs * gain
            e = bias - mean
            put_table(n, a)
            put_table(4, e * a + shift)
            ctab[b, n, 0] = a
            ctab[b, n, 1] = rs
            ctab[b, n, 2] = e
            ctab[b, n, 3] = s1
            yield 250

        def backward_tables(n, s1, s2, gain):
            a, rs, e, sx = [ctab[b, n, j] for j in range(4)]
            sn = rs * (s2 + e * s1)
            m1 = lane_groups(gain * s1 * inv) * 0.125
            m2 = lane_groups(gain * sn * inv) * 0.125
            v = rs * rs * m2
            u = rs * m1 + e * v
            put_table(5, v)
            put_table(6, u)
            return a * s1 - v * sx - cnt * u, s1, sn

        def silu_pass(n, xref, spref, xcref, vertical):
            if vertical:
                side[at(0, 0, 16), 0:768] = jnp.zeros((16, 768), bf16)
                side[at(SIDE - 1, 0, 16), 768:1536] = jnp.zeros((16, 768), bf16)
            for r in range(SIDE):
                acts = []
                for h in range(2):
                    x = xref[at(r, h), :]
                    y = x * pick(n, r, h) + pick(4, r, h)
                    hy = 0.5 * y
                    t = jnp.tanh(hy)
                    act = hy * t + hy
                    sig = 0.5 * t + 0.5
                    spref[at(r, h), :] = sig + act - act * sig
                    acts.append(act)
                    for c in range(2):
                        xs[b, c, pl.ds(8 + r * 16 + h * 8, 8), :] = act[:, c * 128 : (c + 1) * 128]
                k0 = 8 + r * 16
                if vertical:
                    below = mbu[at(r + 1, 0, 16), :] if r < SIDE - 1 else None
                    above = mbd[at(r - 1, 0, 16), :] if r > 0 else None
                for c in range(2):
                    taps = []
                    for dx in (-1, 0, 1):
                        pieces = []
                        for h in range(2):
                            if dx == 0:
                                pieces.append(acts[h][:, c * 128 : (c + 1) * 128])
                                continue
                            piece = xs[b, c, pl.ds(k0 + h * 8 + dx, 8), :]
                            if dx == -1:
                                piece = jnp.where(hasl[b][h], piece, 0.0)
                            if dx == 1:
                                piece = jnp.where(hasr[b][h], piece, 0.0)
                            pieces.append(piece)
                        taps.append(jnp.concatenate(pieces, axis=0).astype(bf16))
                    for k, tap in enumerate(taps):
                        lanes = slice(k * 256 + c * 128, k * 256 + c * 128 + 128)
                        low = slice(768 + lanes.start, 768 + lanes.stop)
                        xcref[at(r, 0, 16), lanes] = tap
                        if vertical and r < SIDE - 1:
                            side[at(r + 1, 0, 16), lanes] = tap * below
                        if vertical and r > 0:
                            side[at(r - 1, 0, 16), low] = tap * above
                if r % GRAIN == GRAIN - 1:
                    yield 30 * GRAIN

        def spread_grad(first, r, value):
            low = value.astype(bf16)
            side[at(r, 0, 16), first + 256 : first + 512] = low
            if r == 0:
                side[at(0, 0, 16), first + 512 : first + 768] = jnp.zeros((16, 256), bf16)
            if r == SIDE - 1:
                side[at(r, 0, 16), first : first + 256] = jnp.zeros((16, 256), bf16)
            below = mbu[at(r + 1, 0, 16), :] if r < SIDE - 1 else None
            above = mbd[at(r - 1, 0, 16), :] if r > 0 else None
            for c in range(2):
                part = low[:, c * 128 : (c + 1) * 128]
                if r > 0:
                    side[at(r - 1, 0, 16), first + c * 128 : first + c * 128 + 128] = part * above
                if r < SIDE - 1:
                    side[at(r + 1, 0, 16), first + 512 + c * 128 : first + 640 + c * 128] = part * below

        def tap_back(spref, xref):
            def values(r, h):
                k = 8 + r * 16 + h * 8
                cols = []
                for c in range(2):
                    d = us[b, 2 + c, pl.ds(k, 8), :]
                    d = d + jnp.where(hasr[b][h], us[b, c, pl.ds(k + 1, 8), :], 0.0)
                    d = d + jnp.where(hasl[b][h], us[b, 4 + c, pl.ds(k - 1, 8), :], 0.0)
                    cols.append(d)
                dy = jnp.concatenate(cols, axis=1) * spref[at(r, h), :]
                dys[at(r, h), :] = dy
                return dy, dy * xref[at(r, h), :]

            return values

        def norm_grad(n, r, h, xref):
            return dys[at(r, h), :] * pick(n, r, h) - xref[at(r, h), :] * pick(5, r, h) - pick(6, r, h)

        def nine(xcref):
            return jnp.concatenate([side[mine, 0:768], xcref[mine, :], side[mine, 768:1536]], axis=1)

        def put_us(lhs, rhs_ref):
            for dx in range(3):
                u = nn(lhs, rhs_ref[:, dx * 256 : (dx + 1) * 256])
                for c in range(2):
                    us[b, dx * 2 + c, pl.ds(8, TOK), :] = u[:, c * 128 : (c + 1) * 128]
                yield 64 * (lhs.shape[1] // 256)

        def later(job):
            if b % 2:
                job(pl.ds(r0 - TOK, 2 * TOK))

        def weight_grad(acc, xref, dref, first, width):
            def job(two):
                for dx in range(3):
                    turned = []

                    def one(dy, dx=dx, turned=turned):
                        if not turned:
                            turned.append(xref[two, dx * 256 : (dx + 1) * 256].T)
                        cols = slice(dy * 256, (dy + 1) * 256)
                        grad = dref[two, first + dy * 256 : first + (dy + 1) * 256]
                        acc[pl.ds(dx * 256, 256), cols] += nn(turned[0], grad)

                    for dy in range(width):
                        fill.append(lambda dy=dy, one=one: one(dy))

            later(job)

        yield from masks()
        x0[mine, :] = nn(xt_ref[mine, :], ws[...])
        yield 128
        yield from forward_tables(0, x0, jnp.broadcast_to(row(0), (8, 256)), row(2), row(3))
        yield from silu_pass(0, x0, sp1, xc1, True)
        x1[mine, :] = nn(nine(xc1), wk1[...])
        yield 128 * 9
        bias1 = tbs[pl.ds((base + b) * 8, 8), :] + row(4)
        yield from forward_tables(1, x1, bias1, row(5), row(6))
        yield from silu_pass(1, x1, sp2, xc2, True)
        x2[mine, :] = x0[mine, :] + nn(nine(xc2), wk2[...])
        yield 128 * 9
        yield from forward_tables(2, x2, jnp.broadcast_to(row(0) + row(7), (8, 256)), row(8), row(9))
        for r in range(SIDE):
            halves = [x2[at(r, h), :] * pick(2, r, h) + pick(4, r, h) for h in range(2)]
            nrm[at(r, 0, 16), :] = jnp.concatenate(halves, axis=0).astype(bf16)
            if r % GRAIN == GRAIN - 1:
                yield 10 * GRAIN
        ks[mine, :] = nn(nrm[mine, :], wqkv[:, 256:512]).astype(bf16)
        qs[mine, :] = (nn(nrm[mine, :], wqkv[:, 0:256]) + row(10)).astype(bf16)
        vs[mine, :] = (nn(nrm[mine, :], wqkv[:, 512:768]) + row(11)).astype(bf16)
        yield 128 * 2

        def quadrant(p):
            col, line = p & 15, p >> 4
            left = jnp.where(line < lefts[b], 0, 1)
            right = jnp.where(line < rights[b], 2, 3)
            return jnp.where(col < cuts[b], left, right)

        qq = quadrant(lax.broadcasted_iota(jnp.int32, (1, TOK), 1))
        part = 64
        scores = []
        for k in range(TOK // part):
            scores.append(nt(qs[pl.ds(r0 + k * part, part), :], ks[mine, :]))
        yield 128
        for k in range(TOK // part):
            rows = pl.ds(r0 + k * part, part)
            qp = quadrant(k * part + lax.broadcasted_iota(jnp.int32, (part, 1), 0))
            s = jnp.where(qp == qq, scores[k], far_score)
            top = jnp.max(s, axis=1, keepdims=True)
            ex = jnp.exp((s - top) * (CH**-0.5))
            p = ex * (1.0 / jnp.sum(ex, axis=1, keepdims=True))
            prob[rows, :] = p
            pb[rows, :] = p.astype(bf16)
            yield 60
        mix[mine, :] = nn(pb[mine, :], vs[mine, :]).astype(bf16)
        yield 128
        x3[mine, :] = x2[mine, :] + nn(mix[mine, :], wo[...])
        yield 128
        yield from forward_tables(3, x3, jnp.broadcast_to(row(0) + row(7) + row(12), (8, 256)), row(13), row(14))
        yield from silu_pass(3, x3, sp4, xc3, False)

        z = nn(xc3[mine, :], wr[...])
        us[b, 0, pl.ds(8, TOK), :] = z[:, 0:128]
        us[b, 1, pl.ds(8, TOK), :] = z[:, 128:256]
        yield 128 * 3
        for r in range(SIDE):
            ql, qr = quads(r)
            inl = scale_ref[8 + (base + b) * 4 + ql]
            inr = scale_ref[8 + (base + b) * 4 + qr]
            for h in range(2):
                k = 8 + r * 16 + h * 8
                y = pltpu.roll(us[b, 0, pl.ds(k, 8), :], 64, 1)
                if r > 0:
                    y = y + us[b, 0, pl.ds(k - 16, 8), :] * mvu[at(r, h), :]
                if r < SIDE - 1:
                    y = y + us[b, 1, pl.ds(k + 16, 8), :] * mvd[at(r, h), :]
                inside = jnp.where(onleftn[b][h], inl, inr)
                err = jnp.where(lane < PIX, (y - tg_ref[at(r, h), :]) * inside, 0.0)
                lacc[...] += err * err
                xs[b, 0, pl.ds(k, 8), :] = (err * sc[...]).astype(bf16).astype(f32)
            yield 15
        for r in range(SIDE):
            tile0, tile1 = [], []
            for h in range(2):
                k = 8 + r * 16 + h * 8
                t0 = pltpu.roll(xs[b, 0, pl.ds(k, 8), :], 64, 1)
                if r < SIDE - 1:
                    t0 = t0 + xs[b, 0, pl.ds(k + 16, 8), :] * mvd[at(r, h), :]
                t1 = jnp.zeros((8, 128), f32)
                if r > 0:
                    t1 = xs[b, 0, pl.ds(k - 16, 8), :] * mvu[at(r, h), :]
                tile0.append(t0)
                tile1.append(t1)
            dyp[at(r, 0, 16), 0:128] = jnp.concatenate(tile0, axis=0).astype(bf16)
            dyp[at(r, 0, 16), 128:256] = jnp.concatenate(tile1, axis=0).astype(bf16)
            if r % GRAIN == GRAIN - 1:
                yield 10 * GRAIN

        yield from put_us(dyp[mine, :], wrt)
        weight_grad(gr, xc3, dyp, 0, 1)
        s1, s2 = yield from crop_sums(tap_back(sp4, x3))
        sum3, db, dg = backward_tables(3, s1, s2, row(13))
        gv[13] += dg
        gv[14] += db
        gv[12] += sum3
        yield 200
        for r in range(SIDE):
            halves = []
            for h in range(2):
                d = norm_grad(3, r, h, x3)
                gtop[at(r, h), :] = d
                halves.append(d)
            dpo[at(r, 0, 16), :] = jnp.concatenate(halves, axis=0).astype(bf16)
            if r % GRAIN == GRAIN - 1:
                yield 14 * GRAIN
        dmx[mine, :] = nn(dpo[mine, :], wot[...]).astype(bf16)
        yield 128

        def grad_out(two):
            def job():
                ga[:, 768:1024] += nn(mix[two, :].T, dpo[two, :])

            fill.append(job)

        later(grad_out)
        vlow = vs[mine, :] * jnp.asarray(CH**-0.5, bf16)
        for k in range(TOK // part):
            rows = pl.ds(r0 + k * part, part)
            da = nt(dmx[rows, :], vlow)
            p = prob[rows, :]
            t = da * p
            dsb[rows, :] = (t - p * jnp.sum(t, axis=1, keepdims=True)).astype(bf16)
            yield 70
        dv = nn(pb[mine, :].T, dmx[mine, :])
        trip[mine, 512:768] = dv.astype(bf16)
        gv[11] += jnp.sum(dv.reshape(TOK // 8, 8, CH), axis=0)
        yield 128
        dq = nn(dsb[mine, :], ks[mine, :])
        trip[mine, 0:256] = dq.astype(bf16)
        gv[10] += jnp.sum(dq.reshape(TOK // 8, 8, CH), axis=0)
        yield 128
        dk = nn(dsb[mine, :].T, qs[mine, :])
        trip[mine, 256:512] = dk.astype(bf16)
        yield 128
        dys[mine, :] = nn(trip[mine, :], wat[...])
        yield 128 * 3

        def grad_triple(two):
            turned = []
            for k in range(3):

                def job(k=k):
                    if not turned:
                        turned.append(nrm[two, :].T)
                    ga[:, k * 256 : (k + 1) * 256] += nn(turned[0], trip[two, k * 256 : (k + 1) * 256])

                fill.append(job)

        later(grad_triple)

        def plain(r, h):
            dy = dys[at(r, h), :]
            return dy, dy * x2[at(r, h), :]

        s1, s2 = yield from crop_sums(plain)
        sum2, db, dg = backward_tables(2, s1, s2, row(8))
        gv[8] += dg
        gv[9] += db
        sum2 = sum2 + sum3
        gv[7] += sum2
        yield 200
        for r in range(SIDE):
            halves = []
            for h in range(2):
                d = norm_grad(2, r, h, x2) + gtop[at(r, h), :]
                gtop[at(r, h), :] = d
                halves.append(d)
            spread_grad(0, r, jnp.concatenate(halves, axis=0))
            if r % GRAIN == GRAIN - 1:
                yield 18 * GRAIN
        yield from put_us(side[mine, 0:768], wt2)
        weight_grad(gk2, xc2, side, 0, 3)
        s1, s2 = yield from crop_sums(tap_back(sp2, x1))
        sum1, db, dg = backward_tables(1, s1, s2, row(5))
        gv[5] += dg
        gv[6] += db
        gv[4] += sum1
        dtb[pl.ds((base + b) * 8, 8), :] = sum1
        yield 200
        for r in range(SIDE):
            spread_grad(768, r, jnp.concatenate([norm_grad(1, r, h, x1) for h in range(2)], axis=0))
            if r % GRAIN == GRAIN - 1:
                yield 16 * GRAIN
        yield from put_us(side[mine, 768:1536], wt1)
        weight_grad(gk1, xc1, side, 768, 3)
        s1, s2 = yield from crop_sums(tap_back(sp1, x0))
        sum0, db, dg = backward_tables(0, s1, s2, row(2))
        gv[2] += dg
        gv[3] += db
        gv[0] += sum0 + sum2
        yield 200
        for r in range(SIDE):
            halves = [norm_grad(0, r, h, x0) + gtop[at(r, h), :] for h in range(2)]
            dps[at(r, 0, 16), :] = jnp.concatenate(halves, axis=0).astype(bf16)
            if r % GRAIN == GRAIN - 1:
                yield 14 * GRAIN

        def grad_stem(two):
            def job():
                gs[...] += nn(xt_ref[two, :].T, dps[two, :])

            fill.append(job)

        later(grad_stem)

    clocks = {b: float(b * SKEW) for b in range(PAIR)}
    streams = {b: stream(b) for b in range(PAIR)}
    filled = 0.0
    while streams:
        b = min(streams, key=lambda k: clocks[k])
        try:
            clocks[b] += next(streams[b])
        except StopIteration:
            del streams[b]
        now = min([clocks[k] for k in streams], default=1e18)
        while fill and filled < now:
            filled = max(filled, now if now < 1e17 else 0.0) + FILLCOST
            fill.pop(0)()

    @pl.when(step == last)
    def _():
        low = dtb[...].astype(bf16)
        hp = hpre[...]
        sg = jax.nn.sigmoid(hp)
        gp = (nn((hp * sg).astype(bf16).T, low) * 0.5).astype(bf16)
        hg = nt(low, wpj[...]) * (sg * (1.0 + hp * (1.0 - sg)))
        ge = (nn(feat_ref[...].T, hg.astype(bf16)) * 0.5).astype(bf16)
        twice = {10: 1.0, 11: 1.0}
        rows = [jnp.sum(gv[4 if k == 1 else k], axis=0, keepdims=True) * twice.get(k, 0.5) for k in range(15)]
        gnorm = jnp.concatenate(rows + [jnp.zeros((1, 256), f32)], axis=0)
        gstem = gs[...].T
        shared = pltpu.roll(lacc[...], PIX, 1)
        shared = jnp.concatenate([shared, jnp.zeros((AROW - 8, 128), f32)], axis=0)
        gstem = gstem + jnp.concatenate([shared] * VIRT, axis=0)
        for dy in range(3):
            for lo in range(0, 768, 256):
                part = gr[pl.ds(lo, 256), (dy // 2) * 128 : (dy // 2) * 128 + 128]
                if dy == 1:
                    part = pltpu.roll(part, 64, 1)
                grn[pl.ds(dy * 768 + lo, 256), :] = part
        for core in range(2):

            @pl.when(geo_ref[3] == core)
            def _(core=core):
                for f in range(VIRT):
                    out_ref, z = (keep_ref, send_ref)[(f % 2) ^ core], f // 2
                    for dy in range(3):
                        lo, hi = max(f * KROW, dy * 768), min((f + 1) * KROW, (dy + 1) * 768)
                        if lo >= hi:
                            continue
                        src = pl.ds(lo - dy * 768, hi - lo)
                        dst = pl.ds(lo - f * KROW, hi - lo)
                        out_ref[z, dst, 0:256] = gk1[src, dy * 256 : (dy + 1) * 256].astype(bf16)
                        out_ref[z, dst, 256:512] = gk2[src, dy * 256 : (dy + 1) * 256].astype(bf16)
                    k = f * AROW
                    a1, a2, p0 = KROW, KROW + AROW, KROW + 2 * AROW
                    e0 = p0 + PROW
                    out_ref[z, a1:a2, :] = ga[k : k + AROW, 0:512].astype(bf16)
                    out_ref[z, a2:p0, :] = ga[k : k + AROW, 512:1024].astype(bf16)
                    out_ref[z, p0:e0, 0:256] = gp[f * 2 * PROW : f * 2 * PROW + PROW, :]
                    out_ref[z, p0:e0, 256:512] = gp[f * 2 * PROW + PROW : (f + 1) * 2 * PROW, :]
                    out_ref[z, e0:TROW, :] = ge[f * EROW : (f + 1) * EROW, :]
                    back = grn[pl.ds(f * KROW, 384), :].T[:TAIL, :]
                    keep = lax.broadcasted_iota(jnp.int32, (TAIL, 384), 1) < KROW
                    out_ref[z, TROW:PACKED, 0:384] = jnp.where(keep, back, 0.0).astype(bf16)
                    out_ref[z, TROW : TROW + 32, 384:512] = gstem[k : k + AROW, :].astype(bf16)
                    tile = gnorm[:, (f // 4) * 128 : (f // 4) * 128 + 128]
                    tile = pltpu.roll(tile, (128 - (f % 4) * AROW) % 128, 1)
                    keep = lax.broadcasted_iota(jnp.int32, (16, 128), 1) < AROW
                    out_ref[z, TROW + 32 : PACKED, 384:512] = jnp.where(keep, tile, 0.0).astype(bf16)
        loss_ref[...] = lacc[...]


SKEW = 700
FILLCOST = 128
GRAIN = 2


def run_step(packed, quad, geo, scal, feat, cp, tg):
    canvases = cp.shape[0] // TOK
    whole = pl.BlockSpec(memory_space=pltpu.VMEM)
    smem = pl.BlockSpec(memory_space=pltpu.SMEM)

    def rows(n, lanes):
        return pl.BlockSpec((n, lanes), lambda i, *_: (i, 0))

    items = scratch_list(canvases)
    return pl.pallas_call(
        functools.partial(step_kernel, [name for name, _, _ in items]),
        grid_spec=pltpu.PrefetchScalarGridSpec(
            num_scalar_prefetch=2,
            grid=(canvases // PAIR,),
            in_specs=[
                smem, whole, whole, whole, whole, whole, whole, rows(ROWS, 128), rows(ROWS, 128),
            ],
            out_specs=[whole] * 4,
            scratch_shapes=[pltpu.VMEM(shape, dtype) for _, shape, dtype in items],
        ),
        out_shape=[
            jax.ShapeDtypeStruct((VIRT // 2, PACKED, 512), bf16),
            jax.ShapeDtypeStruct((VIRT // 2, PACKED, 512), bf16),
            jax.ShapeDtypeStruct((8, 128), f32),
            jax.ShapeDtypeStruct((8, 128), f32),
        ],
        compiler_params=pltpu.CompilerParams(
            dimension_semantics=("arbitrary",), vmem_limit_bytes=60 * 1024 * 1024
        ),
        name="unet_step",
    )(quad, geo, scal, *packed, feat, cp, tg)


def patch_kernel(clean_ref, noise_ref, cp_ref, np_ref, staged):
    n = clean_ref.shape[0]
    slot = staged.shape[0] // (2 * SIDE)
    for k, ref in enumerate((clean_ref, noise_ref)):
        for r in range(SIDE):
            for c in range(3):
                staged[pl.ds((k * SIDE + r) * slot, n), c * 256 : (c + 1) * 256] = ref[:, c * 4096 + r * 256 : c * 4096 + r * 256 + 256]
    src = lax.broadcasted_iota(jnp.int32, (768, 256), 0)
    place = ((src >> 2) & 15) * 128 + (src >> 8) * 16 + ((src >> 6) & 3) * 4 + (src & 3)
    for j in range(SIDE // 2):
        lane = lax.broadcasted_iota(jnp.int32, (768, 256), 1) + j * 256
        out = nn(staged[...], (place == lane).astype(bf16))
        for k, ref in enumerate((cp_ref, np_ref)):
            for r in range(SIDE):
                row = (k * SIDE + r) * slot
                for i in range(2):
                    ref[pl.ds(r * SIDE + 2 * j + i, n, stride=TOK), :] = out[row : row + n, i * 128 : (i + 1) * 128]


def patches(clean, noise):
    n = clean.shape[0]
    slot = -(-n // 16) * 16
    whole = pl.BlockSpec(memory_space=pltpu.VMEM)
    return pl.pallas_call(
        patch_kernel,
        in_specs=[whole, whole],
        out_specs=[whole, whole],
        out_shape=[jax.ShapeDtypeStruct((n * TOK, 128), f32)] * 2,
        scratch_shapes=[pltpu.VMEM((2 * SIDE * slot, 768), bf16)],
        compiler_params=pltpu.CompilerParams(vmem_limit_bytes=48 * 1024 * 1024),
        cost_estimate=pl.CostEstimate(flops=2 * 64 * n * 768 * 2048, bytes_accessed=8 * n * TOK * 128, transcendentals=0),
        name="patches",
    )(clean, noise)


def upper_kernel(kernels, upper):
    upper[...] = kernels[0:CUT, :].astype(bf16)


def pack_kernel(copy, tokens, upper, stem, kernels, embed, project, attention, readout, norm, mine, block):
    a1, a2, p0 = KROW - CUT, KROW + AROW - CUT, KROW + 2 * AROW - CUT
    e0, tail, end = p0 + PROW, TROW - CUT, PACKED - CUT

    def put(lo, hi, value):
        for q in range(value.shape[1] // 128):
            block[q, lo:hi, :] = value[:, q * 128 : (q + 1) * 128].astype(bf16)

    put(0, a1, kernels[CUT:KROW, :])
    put(a1, a2, attention[:, 0:512])
    put(a2, p0, attention[:, 512:1024])
    put(p0, e0, jnp.concatenate([project[0:PROW, :], project[PROW : 2 * PROW, :]], axis=1))
    put(e0, tail, embed[...])
    for q in range(2, 4):
        block[q, tail:end, :] = jnp.zeros((TAIL, 128), bf16)
    put(tail, end, readout[:, 0:256])
    block[2, tail:end, 0 : KROW - 256] = readout[:, 256:KROW].astype(bf16)
    block[3, tail : tail + 32, 0:PIX] = stem[...].astype(bf16)
    block[3, tail + 32 : tail + 47, 0:AROW] = norm[...].astype(bf16)
    mine[0:end, :] = block[copy[0]]
    row = lax.broadcasted_iota(jnp.int32, (16, 128), 0)
    lane = lax.broadcasted_iota(jnp.int32, (16, 128), 1)
    tokens = tokens[0]
    limbs = jnp.where(lane == 0, tokens >> 6, jnp.where(lane == 1, tokens & 63, 0))
    mine[end : end + 16, :] = jnp.where(row == 0, limbs, 0).astype(f32).astype(bf16)


def pack_weights(masters, copy, tokens):
    stem, kernels, embed, project, attention, readout, norm = masters
    whole, smem = pl.BlockSpec(memory_space=pltpu.VMEM), pl.BlockSpec(memory_space=pltpu.SMEM)
    rest = PACKED - CUT
    upper = pl.pallas_call(
        upper_kernel,
        grid=(1,),
        in_specs=[pl.BlockSpec((CUT, 512), lambda i: (0, 0))],
        out_specs=pl.BlockSpec((CUT, 512), lambda i: (0, 0)),
        out_shape=jax.ShapeDtypeStruct((CUT, 512), bf16),
        name="pack_upper",
    )(kernels)
    mine = pl.pallas_call(
        pack_kernel,
        in_specs=[smem, smem, pl.BlockSpec(memory_space=pl.ANY)] + [whole] * 7,
        out_specs=whole,
        out_shape=jax.ShapeDtypeStruct((rest + 16, 128), bf16),
        scratch_shapes=[pltpu.VMEM((4, rest, 128), bf16)],
        name="pack_rest",
    )(copy.reshape(1), tokens.reshape(1), upper, stem, kernels, embed, project, attention, readout.T, norm.T)
    return upper, mine


def gather_weights(upper, mine):
    shards = lax.axis_size("fsdp")
    upper = lax.all_gather(upper, "fsdp", axis=0, tiled=False)
    got = [lax.ppermute(mine, "fsdp", [(i, (i + 2 * j) % shards) for i in range(shards)]) for j in range(1, 4)]
    both = jnp.stack([mine] + got)
    a, b = both[:, :PART], both[:, PART:]
    ga, gb = exchange(a, "dp", 1), exchange(b, "dp", 2)
    a, b = jnp.stack([a, ga]), jnp.stack([b, gb])
    ga, gb = exchange(a, "dp", 2), exchange(b, "dp", 1)
    a, b = jnp.concatenate([a, ga]), jnp.concatenate([b, gb])
    return upper, a, b, exchange(a, "fsdp", 1), exchange(b, "fsdp", 1)


def slots_of(packed):
    rest = packed[:, CUT:].reshape(4, 2, PACKED - CUT, 4, 128)
    rest = jnp.stack([rest[z] for z in (0, 3, 2, 1)]).transpose(1, 3, 0, 2, 4)
    a, b = rest[..., :PART, :], jnp.stack([rest[:, q, :, PART:, :] for q in (0, 2, 1, 3)], axis=1)
    b = jnp.pad(b, ((0, 0), (0, 0), (0, 0), (0, 16), (0, 0)))
    return packed[:, :CUT], a[0], b[0], a[1], b[1]


def update_kernel(place, count, own, first, second, *refs):
    loss_out, total = refs[-2:]
    refs = refs[:-2]
    half, quarter = PACKED // 4, PACKED // 8
    for k in range(2):
        near, far = place[k], place[1 - k]
        at = k * 2 * half
        total[pl.ds(pl.multiple_of(at + near * half + far * quarter, 8), quarter), :] = own[k].astype(f32)
        total[pl.ds(pl.multiple_of(at + near * half + (1 - far) * quarter, 8), quarter), :] = first[k].astype(f32)
        there = at + (1 - near) * half
        total[pl.ds(pl.multiple_of(there + far * quarter, 8), quarter), :] = second[k, 0].astype(f32)
        total[pl.ds(pl.multiple_of(there + (1 - far) * quarter, 8), quarter), :] = second[k, 1].astype(f32)
    shared = total[TROW : TROW + 8, 384:512]
    lane = lax.broadcasted_iota(jnp.int32, (8, 128), 1)
    shared = jnp.where((lane >= PIX) & (lane < 2 * PIX), shared, 0.0)
    count = count[0:1, 0:1]
    loss_out[...] = jnp.sum(shared, axis=(0, 1), keepdims=True) / count
    rate = lr_scale * jnp.sqrt(count)
    a1, a2, p0 = KROW, KROW + AROW, KROW + 2 * AROW
    e0 = p0 + PROW
    everything = slice(None)
    cuts = [
        (0, everything, everything, total[TROW : TROW + 32, 384:512][:, :PIX]),
        (1, everything, everything, total[0:a1, :]),
        (2, everything, everything, total[e0:TROW, :]),
        (3, slice(0, PROW), everything, total[p0:e0, 0:256]),
        (3, slice(PROW, 2 * PROW), everything, total[p0:e0, 256:512]),
        (4, everything, slice(0, 512), total[a1:a2, :]),
        (4, everything, slice(512, 1024), total[a2:p0, :]),
        (5, everything, everything, total[TROW:PACKED, 0:384][:, :KROW]),
        (6, everything, everything, total[TROW + 32 : PACKED, 384:512][:15, :AROW]),
    ]
    for n, rows, lanes, grad in cuts:
        w, m, a, m_out, w_out, a_out = [refs[n + 7 * j] for j in range(6)]
        m_next = momentum_rate * m[rows, lanes] + grad
        w_next = w[rows, lanes] - rate * (grad + momentum_rate * m_next)
        m_out[rows, lanes] = m_next
        w_out[rows, lanes] = w_next
        a_out[rows, lanes] = average_rate * a[rows, lanes] + (1.0 - average_rate) * w_next


def turn(arrays):
    return [x.T if k in (5, 6) else x for k, x in enumerate(arrays)]


def update_fused(place, count, own, first, second, masters, moments, averages):
    whole = pl.BlockSpec(memory_space=pltpu.VMEM)
    smem = pl.BlockSpec(memory_space=pltpu.SMEM)
    state = turn(masters) + turn(moments) + turn(averages)
    out = pl.pallas_call(
        update_kernel,
        in_specs=[smem] + [whole] * 25,
        out_specs=[whole] * 22,
        out_shape=[jax.ShapeDtypeStruct(x.shape, f32) for x in state] + [jax.ShapeDtypeStruct((1, 1), f32)],
        scratch_shapes=[pltpu.VMEM((PACKED, 512), f32)],
        compiler_params=pltpu.CompilerParams(vmem_limit_bytes=32 * 1024 * 1024),
        name="update",
    )(place, count, own, first, second, *state)
    return (out[21][0, 0],) + tuple(turn(out[0:7]) + turn(out[7:14]) + turn(out[14:21]))


def signal_table():
    beta = np.linspace(0.0001, 0.02, TSTEPS, dtype=np.float64)
    return np.exp(np.cumsum(np.log(1.0 - beta))).astype(np.float32)


def time_features(time_steps):
    half_width = TEMB // 2
    frequency = jnp.exp(-math.log(10000.0) * jnp.arange(half_width, dtype=f32) / (half_width - 1))
    angles = time_steps.astype(f32)[..., None] * frequency
    return jnp.concatenate([jnp.sin(angles), jnp.cos(angles)], axis=-1)


def prepare(clean, noise, lab, time_steps, count, place):
    canvases = lab.shape[0]
    cut = jnp.sum(jnp.all(lab == lab[:, :, :1], axis=1).astype(jnp.int32), axis=1)
    left = jnp.sum((lab[:, :, 0] == lab[:, :1, 0]).astype(jnp.int32), axis=1)
    right = jnp.sum((lab[:, :, -1] == lab[:, :1, -1]).astype(jnp.int32), axis=1)
    own = jnp.stack([lab[:, 0, 0], lab[:, -1, 0], lab[:, 0, -1], lab[:, -1, -1]], axis=1)
    area = jnp.stack(
        [cut * left, cut * (SIDE - left), (SIDE - cut) * right, (SIDE - cut) * (SIDE - right)], axis=1
    ).astype(f32)
    here = [jnp.full_like(cut, x) for x in place]
    geo = jnp.stack([cut, left, right] + here + here[:2], axis=1).reshape(-1)
    line = jnp.arange(SIDE, dtype=jnp.int32)
    quad = (line >= left[:, None]).astype(jnp.int32) + 2 * (line >= right[:, None]).astype(jnp.int32)
    quad = quad.reshape(-1)
    hit = own[..., None] == jnp.arange(1, CROPS + 1, dtype=jnp.int32)
    times = jnp.sum(jnp.where(hit, time_steps[:, None, :], 0), axis=-1)
    eight = np.array([0, 0, 2, 2, 1, 1, 3, 3])
    feat = time_features(times[:, eight]).astype(bf16).reshape(-1, TEMB)
    picked = times[..., None] == jnp.arange(TSTEPS, dtype=jnp.int32)
    chosen = jnp.sum(jnp.where(picked, jnp.asarray(signal_table()), 0.0), axis=-1)
    inside = (own > 0).astype(f32)
    levels = [inside, jnp.sqrt(chosen), jnp.sqrt(1.0 - chosen), area]
    scal = jnp.concatenate([jnp.full((8,), count, f32)] + [x.reshape(-1) for x in levels])
    cp, tg = patches(clean, noise)
    return quad, geo, scal, feat, cp, tg


def exchange(value, axis, bit):
    return lax.ppermute(value, axis, [(i, i ^ bit) for i in range(lax.axis_size(axis))])


def sum_over_all(value):
    for axis in ("fsdp", "dp"):
        bit = 1
        while bit < lax.axis_size(axis):
            value = value + exchange(value, axis, bit)
            bit *= 2
    return value


def join(a, b):
    return (a.astype(f32) + b.astype(f32)).astype(bf16)


def halves(value, which):
    n = value.shape[1] // 2
    low, high = value[:, :n], value[:, n:]
    return jnp.where(which == 0, low, high), jnp.where(which == 0, high, low)


def reduce_grads(keep, send):
    total = join(keep, exchange(send, "fsdp", 1))
    near, far = lax.axis_index("dp") % 2, lax.axis_index("dp") // 2
    n = total.shape[1] // 2
    parts = [total[:, :n], total[:, n:]]
    for first, second in (((near, 1), (far, 2)), ((far, 2), (near, 1))):
        split = [halves(parts[0], first[0]), halves(parts[1], second[0])]
        came = [exchange(split[0][1], "dp", first[1]), exchange(split[1][1], "dp", second[1])]
        parts = [join(split[0][0], came[0]), join(split[1][0], came[1])]
    blocks = jnp.stack(parts, axis=1)
    chips, shards = blocks.shape[0], lax.axis_size("fsdp")
    chip = lax.axis_index("fsdp") // 2
    own = lax.dynamic_index_in_dim(blocks, chip, 0, keepdims=False).astype(f32)
    for j in range(1, chips):
        out = lax.dynamic_index_in_dim(blocks, (chip + j) % chips, 0, keepdims=False)
        own = own + lax.ppermute(out, "fsdp", [(i, (i + 2 * j) % shards) for i in range(shards)]).astype(f32)
    own = own.astype(bf16)
    first = jnp.stack([exchange(own[0], "dp", 2), exchange(own[1], "dp", 1)])
    both = jnp.stack([own, first], axis=1)
    second = jnp.stack([exchange(both[0], "dp", 1), exchange(both[1], "dp", 2)])
    return jnp.stack([near, far]).astype(jnp.int32), own, first, second


def assemble(place, own, first, second):
    n = own.shape[1]
    parts = []
    for k in range(2):
        near, far = place[k], place[1 - k]
        mine = jnp.where(far == 0, jnp.concatenate([own[k], first[k]]), jnp.concatenate([first[k], own[k]]))
        s = second[k]
        theirs = jnp.where(far == 0, jnp.concatenate([s[0], s[1]]), jnp.concatenate([s[1], s[0]]))
        parts.append(jnp.where(near == 0, jnp.concatenate([mine, theirs]), jnp.concatenate([theirs, mine])))
    return jnp.concatenate(parts).astype(f32)


def on_device(clean, noise, crop_labels, time_steps, *state):
    masters, moments, averages = state[0:7], state[7:14], state[14:21]
    shards = lax.axis_size("fsdp")
    index, copy = lax.axis_index("fsdp"), lax.axis_index("dp")
    tokens = jnp.sum((crop_labels > 0).astype(jnp.int32))
    direct = shards == VIRT and lax.axis_size("dp") == 4
    if direct:
        packed = gather_weights(*pack_weights(masters, copy, tokens))
        inputs = prepare(clean, noise, crop_labels, time_steps, 0.0, (index % 2, index // 2, copy))
    else:
        own = lax.all_gather(pack_rows([w.astype(bf16) for w in masters]), "fsdp", axis=0, tiled=False)
        packed = slots_of(repack(own, shards, VIRT))
        count = sum_over_all(PATCH * PATCH * tokens.astype(f32).reshape(1, 1))[0, 0]
        inputs = prepare(clean, noise, crop_labels, time_steps, count, (0, 0, 0))
    keep, send, loss, total = run_step(packed, *inputs)
    if not direct:
        core = index % 2
        blocks = jnp.stack([keep, send], axis=1).reshape(VIRT, PACKED, 512)
        blocks = repack(blocks, VIRT, shards)
        blocks = blocks.reshape(shards // 2, 2, *blocks.shape[1:])
        keep = lax.dynamic_index_in_dim(blocks, core, 1, keepdims=False)
        send = lax.dynamic_index_in_dim(blocks, 1 - core, 1, keepdims=False)
    place, own, first, second = reduce_grads(keep, send)
    if direct:
        return update_fused(place, total, own, first, second, masters, moments, averages)
    rate = lr_scale * jnp.sqrt(count)
    total_loss = sum_over_all(jnp.sum(loss).reshape(1, 1))[0, 0]
    cut = [masters[1].shape[0], masters[0].shape[0], masters[3].shape[0], masters[2].shape[0]]
    grads = unpack_rows(assemble(place, own, first, second), *cut)
    moment_next = tuple(momentum_rate * m + g for m, g in zip(moments, grads))
    master_next = tuple(w - rate * (g + momentum_rate * m) for w, g, m in zip(masters, grads, moment_next))
    average_next = tuple(average_rate * a + (1.0 - average_rate) * w for a, w in zip(averages, master_next))
    return (total_loss / count,) + moment_next + master_next + average_next


def solution(mesh):
    split = P(("dp", "fsdp"), None)
    in_specs = (split, split, P(("dp", "fsdp"), None, None), split) + (P("fsdp", None),) * 21
    out_specs = (P(),) + (P("fsdp", None),) * 21
    return jax.shard_map(on_device, mesh=mesh, in_specs=in_specs, out_specs=out_specs, check_vma=False)
```

```python
import functools
import math

import jax
import jax.numpy as jnp
import numpy as np
from jax import lax
from jax.experimental import pallas as pl
from jax.experimental.pallas import tpu as pltpu
from jax.sharding import PartitionSpec as P

GROUPS = 32
TEMB = 128
SIDE = 16
PATCH = 4
CROPS = 4
TSTEPS = 1000
TOK = SIDE * SIDE
CH = 256
PIX = 3 * PATCH * PATCH
PAIR = 4
ROWS = PAIR * TOK
VIRT = 8
TAIL = 48

eps_norm = 1e-05
lr_scale = 0.01
momentum_rate = 0.5
average_rate = 0.5
far_score = -1e30
f32 = jnp.float32
bf16 = jnp.bfloat16


def pad_to(value, rows, lanes):
    return jnp.pad(value, ((0, rows - value.shape[0]), (0, lanes - value.shape[1])))


def pack_rows(parts):
    stem, kernels, embed, project, attention, readout, norm = parts
    half = project.shape[0] // 2
    small = jnp.concatenate([pad_to(stem, 32, 128), pad_to(norm.T, 16, 128)], axis=0)
    tail = jnp.concatenate([pad_to(readout.T, TAIL, 384), small], axis=1)
    rows = [kernels, attention[:, :512], attention[:, 512:]]
    rows += [jnp.concatenate([project[:half], project[half:]], axis=1), embed, tail]
    rows = jnp.concatenate(rows, axis=0)
    return pad_to(rows, -(-rows.shape[0] // 8) * 8, 512)


def unpack_rows(rows, k, a, p, e):
    half = p // 2
    at = [0, k, k + a, k + 2 * a, k + 2 * a + half, k + 2 * a + half + e, k + 2 * a + half + e + TAIL]
    kernels, left, right, halves, embed, tail = [rows[at[i] : at[i + 1]] for i in range(6)]
    project = jnp.concatenate([halves[:, :256], halves[:, 256:]], axis=0)
    stem, norm = tail[:a, 384 : 384 + PIX], tail[32 : 32 + 15, 384 : 384 + a].T
    return stem, kernels, embed, project, jnp.concatenate([left, right], axis=1), tail[:, :k].T, norm


def repack(packed, parts_now, parts_next):
    if parts_now == parts_next:
        return packed
    cut = [n // parts_now for n in (9 * CH, CH, 2 * CH, CH // 2)]
    pieces = jax.vmap(lambda rows: unpack_rows(rows, *cut))(packed)
    whole = [piece.reshape(-1, piece.shape[-1]) for piece in pieces]
    split = [piece.reshape(parts_next, -1, piece.shape[-1]) for piece in whole]
    return jax.vmap(lambda *p: pack_rows(p))(*split)


KROW = 9 * CH // VIRT
AROW = CH // VIRT
PROW = CH // VIRT
EROW = TEMB // VIRT
TROW = KROW + 2 * AROW + PROW + EROW
PACKED = TROW + TAIL
CUT = PACKED // 2
PART = (PACKED - CUT) // 2


def lane_groups(value):
    lane = lax.broadcasted_iota(jnp.int32, (8, 128), 1)
    tiles = []
    for t in range(2):
        x = value[:, t * 128 : (t + 1) * 128]
        for s in (1, 2, 4):
            x = x + jnp.where((lane & s) == 0, pltpu.roll(x, 128 - s, 1), pltpu.roll(x, s, 1))
        tiles.append(x)
    return jnp.concatenate(tiles, axis=1)


def quad_rows(q0, q1, q2, q3):
    sub = lax.broadcasted_iota(jnp.int32, (8, 128), 0)
    tiles = []
    for t in range(2):
        a, b, c, d = [q[:, t * 128 : (t + 1) * 128] for q in (q0, q1, q2, q3)]
        low = sub < 4
        u = jnp.where(low, a, pltpu.roll(b, 4, 0)) + jnp.where(low, pltpu.roll(a, 4, 0), b)
        v = jnp.where(low, c, pltpu.roll(d, 4, 0)) + jnp.where(low, pltpu.roll(c, 4, 0), d)
        even = (sub & 2) == 0
        w = jnp.where(even, u, pltpu.roll(v, 2, 0)) + jnp.where(even, pltpu.roll(u, 6, 0), v)
        w = w + jnp.where((sub & 1) == 0, pltpu.roll(w, 7, 0), pltpu.roll(w, 1, 0))
        tiles.append(w)
    return jnp.concatenate(tiles, axis=1)


QUAD_ROW = (0, 4, 2, 6)


def nt(a, b):
    return lax.dot_general(a, b, (((1,), (1,)), ((), ())), preferred_element_type=f32)


def nn(a, b):
    return lax.dot_general(a, b, (((1,), (0,)), ((), ())), preferred_element_type=f32)


PADROWS = TOK + 16


def scratch_list(canvases):
    n = 8 * canvases
    items = [
        ("wk1", (2304, 256), bf16), ("wk2", (2304, 256), bf16), ("wt1", (768, 768), bf16), ("wt2", (768, 768), bf16),
        ("wr", (768, 256), bf16), ("wrt", (256, 768), bf16), ("wqkv", (256, 768), bf16), ("wat", (768, 256), bf16),
        ("wo", (256, 256), bf16), ("wot", (256, 256), bf16), ("ws", (128, 256), bf16), ("wpj", (512, 256), bf16),
        ("wem", (128, 512), bf16), ("vec", (16, 256), f32), ("tbs", (n, 256), f32), ("hpre", (n, 512), f32),
        ("grn", (2304 + 96, 128), f32), ("low", (4, VIRT, PACKED - CUT, 128), bf16), ("sc", (8, 128), f32),
        ("xt", (ROWS, 128), bf16),
        ("gk1", (768, 768), f32), ("gk2", (768, 768), f32), ("gr", (768, 256), f32), ("ga", (256, 1024), f32),
        ("gs", (128, 256), f32), ("gv", (15, 8, 256), f32), ("dtb", (n, 256), f32), ("lacc", (8, 128), f32),
        ("x0", (ROWS, 256), f32), ("x1", (ROWS, 256), f32), ("x2", (ROWS, 256), f32), ("x3", (ROWS, 256), f32),
        ("sp1", (ROWS, 256), f32), ("sp2", (ROWS, 256), f32), ("sp4", (ROWS, 256), f32),
        ("xs", (PAIR, 2, PADROWS, 128), f32), ("us", (PAIR, 6, PADROWS, 128), f32),
        ("side", (ROWS, 1536), bf16),
        ("xc1", (ROWS, 768), bf16), ("xc2", (ROWS, 768), bf16), ("xc3", (ROWS, 768), bf16),
        ("nrm", (ROWS, 256), bf16), ("qs", (ROWS, 256), bf16), ("ks", (ROWS, 256), bf16), ("vs", (ROWS, 256), bf16),
        ("prob", (ROWS, 256), f32), ("pb", (ROWS, 256), bf16), ("dsb", (ROWS, 256), bf16), ("mix", (ROWS, 256), bf16), ("dmx", (ROWS, 256), bf16), ("dpo", (ROWS, 256), bf16),
        ("gtop", (ROWS, 256), f32), ("dys", (ROWS, 256), f32),
        ("dps", (ROWS, 256), bf16),
        ("dyp", (ROWS, 256), bf16), ("trip", (ROWS, 768), bf16),
        ("mvu", (ROWS, 128), f32), ("mvd", (ROWS, 128), f32), ("mbu", (ROWS, 128), bf16), ("mbd", (ROWS, 128), bf16),
        ("ctab", (PAIR, 4, 4, 8, 256), f32),
    ]
    for b in range(PAIR):
        items += [(f"pref{b}", (2, 2, 17, 8, 256), f32)]
        items += [(f"tab{b}_{slot}", (4, 2, 8, 256), f32) for slot in range(7)]
    return items


def step_kernel(names, *refs):
    quad_ref, geo_ref, scale_ref, up_ref, oa_ref, ob_ref, ca_ref, cb_ref, feat_ref, cp_ref, tg_ref = refs[:11]
    halves_ref, (loss_ref, total_ref) = refs[11:15], refs[15:17]
    S = dict(zip(names, refs[17:]))
    wk1, wk2, wt1, wt2, wr, wrt, wqkv, wat, wo, wot = [S[k] for k in ("wk1", "wk2", "wt1", "wt2", "wr", "wrt", "wqkv", "wat", "wo", "wot")]
    ws, wpj, wem, vec, tbs, hpre = [S[k] for k in ("ws", "wpj", "wem", "vec", "tbs", "hpre")]
    gk1, gk2, gr, ga, gs, gv, dtb, lacc = [S[k] for k in ("gk1", "gk2", "gr", "ga", "gs", "gv", "dtb", "lacc")]
    x0, x1, x2, x3, sp1, sp2, sp4, xs, us = [S[k] for k in ("x0", "x1", "x2", "x3", "sp1", "sp2", "sp4", "xs", "us")]
    side, xc1, xc2, xc3, nrm, qs, ks, vs = [S[k] for k in ("side", "xc1", "xc2", "xc3", "nrm", "qs", "ks", "vs")]
    prob, mix, dmx, dpo, gtop, dys = [S[k] for k in ("prob", "mix", "dmx", "dpo", "gtop", "dys")]
    dps, dyp, trip = [S[k] for k in ("dps", "dyp", "trip")]
    mvu, mvd, mbu, mbd, ctab = [S[k] for k in ("mvu", "mvd", "mbu", "mbd", "ctab")]
    grn, xt_ref, pb, dsb, low, sc = S["grn"], S["xt"], S["pb"], S["dsb"], S["low"], S["sc"]
    pref = [S[f"pref{b}"] for b in range(PAIR)]
    tab = [[S[f"tab{b}_{slot}"] for slot in range(7)] for b in range(PAIR)]
    step = pl.program_id(0)
    last = pl.num_programs(0) - 1
    canvases = tbs.shape[0] // 8

    @pl.when(step == 0)
    def _():
        core, chip, copy = geo_ref[3], geo_ref[4], geo_ref[5]
        tokens = jnp.zeros((16, 128), f32)
        for p, (a_ref, b_ref) in enumerate(((oa_ref, ob_ref), (ca_ref, cb_ref))):
            for s in range(4):
                for j in range(4):
                    f = ((chip - j) & 3) * 2 + (core ^ p)
                    low[copy ^ s, f, 0:PART, :] = a_ref[s, j]
                    low[copy ^ ((s >> 1) | ((s & 1) << 1)), f, PART : 2 * PART, :] = b_ref[s, j, 0:PART, :]
                    tokens = tokens + b_ref[s, j, PART : PART + 16, :].astype(f32)
        lanes = lax.broadcasted_iota(jnp.int32, (16, 128), 1)
        tokens = jnp.sum(tokens * jnp.where(lanes == 0, 64.0, 1.0), axis=(0, 1), keepdims=True)
        count = scale_ref[0] + PATCH * PATCH * tokens
        sc[...] = jnp.broadcast_to(2.0 / count, (8, 128))
        total_ref[...] = jnp.broadcast_to(count, (8, 128))

        def lower(f, lo, hi, first, end):
            tiles = [low[q, f, lo - CUT : hi - CUT, :] for q in range(first // 128, end // 128)]
            return tiles[0] if len(tiles) == 1 else jnp.concatenate(tiles, axis=1)

        a1, a2, p0 = KROW, KROW + AROW, KROW + 2 * AROW
        e0 = p0 + PROW
        for f in range(VIRT):
            wk1[pl.ds(f * KROW, CUT), :] = up_ref[f, :, 0:256]
            wk2[pl.ds(f * KROW, CUT), :] = up_ref[f, :, 256:512]
            wk1[pl.ds(f * KROW + CUT, KROW - CUT), :] = lower(f, CUT, KROW, 0, 256)
            wk2[pl.ds(f * KROW + CUT, KROW - CUT), :] = lower(f, CUT, KROW, 256, 512)
            back = lower(f, TROW, PACKED, 0, 384).astype(f32)
            back = jnp.concatenate([back, jnp.zeros((128 - TAIL, 384), f32)], axis=0).T
            grn[pl.ds(f * KROW, KROW), :] = back[:KROW, :]
            wqkv[pl.ds(f * AROW, AROW), 0:512] = lower(f, a1, a2, 0, 512)
            wqkv[pl.ds(f * AROW, AROW), 512:768] = lower(f, a2, p0, 0, 256)
            wo[pl.ds(f * AROW, AROW), :] = lower(f, a2, p0, 256, 512)
            wpj[pl.ds(f * 2 * PROW, PROW), :] = lower(f, p0, e0, 0, 256)
            wpj[pl.ds(f * 2 * PROW + PROW, PROW), :] = lower(f, p0, e0, 256, 512)
            wem[pl.ds(f * EROW, EROW), :] = lower(f, e0, TROW, 0, 512)
        stem = jnp.concatenate([lower(f, TROW, TROW + 32, 384, 512) for f in range(VIRT)], axis=0)
        ws[...] = stem.T
        for t in range(2):
            tile = jnp.zeros((16, 128), f32)
            for j in range(4):
                part = lower(4 * t + j, TROW + 32, PACKED, 384, 512).astype(f32)
                part = jnp.where(lax.broadcasted_iota(jnp.int32, (16, 128), 1) < AROW, part, 0.0)
                tile = tile + (pltpu.roll(part, j * AROW, 1) if j else part)
            vec[:, t * 128 : (t + 1) * 128] = tile
        for dy in range(3):
            for dx in range(3):
                rows = pl.ds((dy * 3 + dx) * 256, 256)
                wt1[pl.ds(dy * 256, 256), dx * 256 : (dx + 1) * 256] = wk1[rows, :].T
                wt2[pl.ds(dy * 256, 256), dx * 256 : (dx + 1) * 256] = wk2[rows, :].T
        for j in range(3):
            wat[pl.ds(j * 256, 256), :] = wqkv[:, j * 256 : (j + 1) * 256].T
        wot[...] = wo[...].T
        for dx in range(3):
            rows = [grn[pl.ds(dy * 768 + dx * 256, 256), :] for dy in range(3)]
            tile0 = (rows[0] + pltpu.roll(rows[1], 64, 1)).astype(bf16)
            tile1 = rows[2].astype(bf16)
            wr[pl.ds(dx * 256, 256), 0:128] = tile0
            wr[pl.ds(dx * 256, 256), 128:256] = tile1
            wrt[0:128, dx * 256 : (dx + 1) * 256] = tile0.T
            wrt[128:256, dx * 256 : (dx + 1) * 256] = tile1.T
        hp = nn(feat_ref[...], wem[...])
        hpre[...] = hp
        tbs[...] = nn(jax.nn.silu(hp).astype(bf16), wpj[...]) + vec[1:2, :]
        grn[pl.ds(2304, 96), :] = jnp.zeros((96, 128), f32)
        for ref in [gk1, gk2, gr, ga, gs, gv, lacc] + pref:
            ref[...] = jnp.zeros_like(ref)

    base = step * PAIR
    cuts = [geo_ref[(base + b) * 8] for b in range(PAIR)]
    lefts = [geo_ref[(base + b) * 8 + 1] for b in range(PAIR)]
    rights = [geo_ref[(base + b) * 8 + 2] for b in range(PAIR)]
    iota8 = lax.broadcasted_iota(jnp.int32, (8, 256), 0)
    iota8n = lax.broadcasted_iota(jnp.int32, (8, 128), 0)
    onleft = [[iota8 < (cuts[b] - 8 * h) for h in range(2)] for b in range(PAIR)]
    onleftn = [[iota8n < (cuts[b] - 8 * h) for h in range(2)] for b in range(PAIR)]
    hasl = [[(iota8n + 8 * h != 0) & (iota8n + 8 * h != cuts[b]) for h in range(2)] for b in range(PAIR)]
    hasr = [[(iota8n + 8 * h != 15) & (iota8n + 8 * h != cuts[b] - 1) for h in range(2)] for b in range(PAIR)]
    lane = lax.broadcasted_iota(jnp.int32, (8, 128), 1)
    fill = []

    def row(k):
        return vec[k : k + 1, :]

    def stream(b):
        r0 = b * TOK
        mine = pl.ds(r0, TOK)
        areas = [scale_ref[8 + 12 * canvases + (base + b) * 4 + q] for q in range(4)]
        sub = lax.broadcasted_iota(jnp.int32, (8, 256), 0)
        cnt = jnp.where(sub < 4, jnp.where(sub < 2, areas[0], areas[2]), jnp.where(sub < 6, areas[1], areas[3]))
        inv = 1.0 / jnp.maximum(cnt, 1.0)

        def at(r, h=0, n=8):
            return pl.ds(r0 + r * 16 + h * 8, n)

        def kind(r):
            return quad_ref[(base + b) * SIDE + r]

        def quads(r):
            t = kind(r)
            return t & 1, 2 + (t >> 1)

        def masks():
            for r in range(SIDE):
                upl = ((lefts[b] != r) & (r > 0)).astype(f32)
                upr = ((rights[b] != r) & (r > 0)).astype(f32)
                dnl = ((lefts[b] != r + 1) & (r < SIDE - 1)).astype(f32)
                dnr = ((rights[b] != r + 1) & (r < SIDE - 1)).astype(f32)
                up = jnp.concatenate([jnp.where(onleftn[b][h], upl, upr) for h in range(2)], axis=0)
                dn = jnp.concatenate([jnp.where(onleftn[b][h], dnl, dnr) for h in range(2)], axis=0)
                mvu[at(r, 0, 16), :] = up
                mvd[at(r, 0, 16), :] = dn
                mbu[at(r, 0, 16), :] = up.astype(bf16)
                mbd[at(r, 0, 16), :] = dn.astype(bf16)
                ql, qr = quads(r)
                level = 8 + 4 * canvases + (base + b) * 4
                al, ar = scale_ref[level + ql], scale_ref[level + qr]
                sl, sr = scale_ref[level + 4 * canvases + ql], scale_ref[level + 4 * canvases + qr]
                mixed = []
                for h in range(2):
                    m = onleftn[b][h]
                    noisy = jnp.where(m, sl, sr) * tg_ref[at(r, h), :]
                    mixed.append(jnp.where(m, al, ar) * cp_ref[at(r, h), :] + noisy)
                xt_ref[at(r, 0, 16), :] = jnp.concatenate(mixed, axis=0).astype(bf16)
            yield 100

        def put_table(slot, table):
            of = [jnp.broadcast_to(table[k : k + 1, :], (8, 256)) for k in QUAD_ROW]
            for t in range(4):
                for h in range(2):
                    tab[b][slot][t, h] = jnp.where(onleft[b][h], of[t & 1], of[2 + (t >> 1)])

        def pick(slot, r, h):
            return tab[b][slot][kind(r), h]

        def crop_sums(values_of):
            total = [None, None]
            left = [None, None]
            p = pref[b]
            for r in range(SIDE):
                halves = [values_of(r, h) for h in range(2)]
                for j in range(2):
                    a0, a1 = halves[0][j], halves[1][j]
                    lp = jnp.where(onleft[b][0], a0, 0.0) + jnp.where(onleft[b][1], a1, 0.0)
                    tp = a0 + a1
                    left[j] = lp if r == 0 else left[j] + lp
                    total[j] = tp if r == 0 else total[j] + tp
                    p[j, 0, r + 1] = left[j]
                    p[j, 1, r + 1] = total[j]
                if r % GRAIN == GRAIN - 1:
                    yield 16 * GRAIN
            got = []
            for j in range(2):
                q0 = p[j, 0, lefts[b]]
                q1 = left[j] - q0
                q2 = p[j, 1, rights[b]] - p[j, 0, rights[b]]
                q3 = (total[j] - left[j]) - q2
                got.append(quad_rows(q0, q1, q2, q3))
            yield 100
            return got

        def forward_tables(n, xref, bias, gain, shift):
            def both(r, h):
                x = xref[at(r, h), :]
                return x, x * x

            s1, s2 = yield from crop_sums(both)
            own = s1 * inv
            mean = lane_groups(own + bias) * 0.125
            apart = own + bias - mean
            var = lane_groups(jnp.maximum(s2 * inv - own * own, 0.0) + apart * apart) * 0.125
            rs = lax.rsqrt(var + eps_norm)
            a = rs * gain
            e = bias - mean
            put_table(n, a)
            put_table(4, e * a + shift)
            ctab[b, n, 0] = a
            ctab[b, n, 1] = rs
            ctab[b, n, 2] = e
            ctab[b, n, 3] = s1
            yield 250

        def backward_tables(n, s1, s2, gain):
            a, rs, e, sx = [ctab[b, n, j] for j in range(4)]
            sn = rs * (s2 + e * s1)
            m1 = lane_groups(gain * s1 * inv) * 0.125
            m2 = lane_groups(gain * sn * inv) * 0.125
            v = rs * rs * m2
            u = rs * m1 + e * v
            put_table(5, v)
            put_table(6, u)
            return a * s1 - v * sx - cnt * u, s1, sn

        def silu_pass(n, xref, spref, xcref, vertical):
            if vertical:
                side[at(0, 0, 16), 0:768] = jnp.zeros((16, 768), bf16)
                side[at(SIDE - 1, 0, 16), 768:1536] = jnp.zeros((16, 768), bf16)
            for r in range(SIDE):
                acts = []
                for h in range(2):
                    x = xref[at(r, h), :]
                    y = x * pick(n, r, h) + pick(4, r, h)
                    hy = 0.5 * y
                    t = jnp.tanh(hy)
                    act = hy * t + hy
                    sig = 0.5 * t + 0.5
                    spref[at(r, h), :] = sig + act - act * sig
                    acts.append(act)
                    for c in range(2):
                        xs[b, c, pl.ds(8 + r * 16 + h * 8, 8), :] = act[:, c * 128 : (c + 1) * 128]
                k0 = 8 + r * 16
                if vertical:
                    below = mbu[at(r + 1, 0, 16), :] if r < SIDE - 1 else None
                    above = mbd[at(r - 1, 0, 16), :] if r > 0 else None
                for c in range(2):
                    taps = []
                    for dx in (-1, 0, 1):
                        pieces = []
                        for h in range(2):
                            if dx == 0:
                                pieces.append(acts[h][:, c * 128 : (c + 1) * 128])
                                continue
                            piece = xs[b, c, pl.ds(k0 + h * 8 + dx, 8), :]
                            if dx == -1:
                                piece = jnp.where(hasl[b][h], piece, 0.0)
                            if dx == 1:
                                piece = jnp.where(hasr[b][h], piece, 0.0)
                            pieces.append(piece)
                        taps.append(jnp.concatenate(pieces, axis=0).astype(bf16))
                    for k, tap in enumerate(taps):
                        lanes = slice(k * 256 + c * 128, k * 256 + c * 128 + 128)
                        low = slice(768 + lanes.start, 768 + lanes.stop)
                        xcref[at(r, 0, 16), lanes] = tap
                        if vertical and r < SIDE - 1:
                            side[at(r + 1, 0, 16), lanes] = tap * below
                        if vertical and r > 0:
                            side[at(r - 1, 0, 16), low] = tap * above
                if r % GRAIN == GRAIN - 1:
                    yield 30 * GRAIN

        def spread_grad(first, r, value):
            low = value.astype(bf16)
            side[at(r, 0, 16), first + 256 : first + 512] = low
            if r == 0:
                side[at(0, 0, 16), first + 512 : first + 768] = jnp.zeros((16, 256), bf16)
            if r == SIDE - 1:
                side[at(r, 0, 16), first : first + 256] = jnp.zeros((16, 256), bf16)
            below = mbu[at(r + 1, 0, 16), :] if r < SIDE - 1 else None
            above = mbd[at(r - 1, 0, 16), :] if r > 0 else None
            for c in range(2):
                part = low[:, c * 128 : (c + 1) * 128]
                if r > 0:
                    side[at(r - 1, 0, 16), first + c * 128 : first + c * 128 + 128] = part * above
                if r < SIDE - 1:
                    side[at(r + 1, 0, 16), first + 512 + c * 128 : first + 640 + c * 128] = part * below

        def tap_back(spref, xref):
            def values(r, h):
                k = 8 + r * 16 + h * 8
                cols = []
                for c in range(2):
                    d = us[b, 2 + c, pl.ds(k, 8), :]
                    d = d + jnp.where(hasr[b][h], us[b, c, pl.ds(k + 1, 8), :], 0.0)
                    d = d + jnp.where(hasl[b][h], us[b, 4 + c, pl.ds(k - 1, 8), :], 0.0)
                    cols.append(d)
                dy = jnp.concatenate(cols, axis=1) * spref[at(r, h), :]
                dys[at(r, h), :] = dy
                return dy, dy * xref[at(r, h), :]

            return values

        def norm_grad(n, r, h, xref):
            return dys[at(r, h), :] * pick(n, r, h) - xref[at(r, h), :] * pick(5, r, h) - pick(6, r, h)

        def nine(xcref):
            return jnp.concatenate([side[mine, 0:768], xcref[mine, :], side[mine, 768:1536]], axis=1)

        def put_us(lhs, rhs_ref):
            for dx in range(3):
                u = nn(lhs, rhs_ref[:, dx * 256 : (dx + 1) * 256])
                for c in range(2):
                    us[b, dx * 2 + c, pl.ds(8, TOK), :] = u[:, c * 128 : (c + 1) * 128]
                yield 64 * (lhs.shape[1] // 256)

        def later(job):
            if b % 2:
                job(pl.ds(r0 - TOK, 2 * TOK))

        def weight_grad(acc, xref, dref, first, width):
            def job(two):
                for dx in range(3):
                    turned = []

                    def one(dy, dx=dx, turned=turned):
                        if not turned:
                            turned.append(xref[two, dx * 256 : (dx + 1) * 256].T)
                        cols = slice(dy * 256, (dy + 1) * 256)
                        grad = dref[two, first + dy * 256 : first + (dy + 1) * 256]
                        acc[pl.ds(dx * 256, 256), cols] += nn(turned[0], grad)

                    for dy in range(width):
                        fill.append(lambda dy=dy, one=one: one(dy))

            later(job)

        yield from masks()
        x0[mine, :] = nn(xt_ref[mine, :], ws[...])
        yield 128
        yield from forward_tables(0, x0, jnp.broadcast_to(row(0), (8, 256)), row(2), row(3))
        yield from silu_pass(0, x0, sp1, xc1, True)
        x1[mine, :] = nn(nine(xc1), wk1[...])
        yield 128 * 9
        bias1 = tbs[pl.ds((base + b) * 8, 8), :] + row(4)
        yield from forward_tables(1, x1, bias1, row(5), row(6))
        yield from silu_pass(1, x1, sp2, xc2, True)
        x2[mine, :] = x0[mine, :] + nn(nine(xc2), wk2[...])
        yield 128 * 9
        yield from forward_tables(2, x2, jnp.broadcast_to(row(0) + row(7), (8, 256)), row(8), row(9))
        for r in range(SIDE):
            halves = [x2[at(r, h), :] * pick(2, r, h) + pick(4, r, h) for h in range(2)]
            nrm[at(r, 0, 16), :] = jnp.concatenate(halves, axis=0).astype(bf16)
            if r % GRAIN == GRAIN - 1:
                yield 10 * GRAIN
        ks[mine, :] = nn(nrm[mine, :], wqkv[:, 256:512]).astype(bf16)
        qs[mine, :] = (nn(nrm[mine, :], wqkv[:, 0:256]) + row(10)).astype(bf16)
        vs[mine, :] = (nn(nrm[mine, :], wqkv[:, 512:768]) + row(11)).astype(bf16)
        yield 128 * 2

        def quadrant(p):
            col, line = p & 15, p >> 4
            left = jnp.where(line < lefts[b], 0, 1)
            right = jnp.where(line < rights[b], 2, 3)
            return jnp.where(col < cuts[b], left, right)

        qq = quadrant(lax.broadcasted_iota(jnp.int32, (1, TOK), 1))
        part = 64
        scores = []
        for k in range(TOK // part):
            scores.append(nt(qs[pl.ds(r0 + k * part, part), :], ks[mine, :]))
        yield 128
        for k in range(TOK // part):
            rows = pl.ds(r0 + k * part, part)
            qp = quadrant(k * part + lax.broadcasted_iota(jnp.int32, (part, 1), 0))
            s = jnp.where(qp == qq, scores[k], far_score)
            top = jnp.max(s, axis=1, keepdims=True)
            ex = jnp.exp((s - top) * (CH**-0.5))
            p = ex * (1.0 / jnp.sum(ex, axis=1, keepdims=True))
            prob[rows, :] = p
            pb[rows, :] = p.astype(bf16)
            yield 60
        mix[mine, :] = nn(pb[mine, :], vs[mine, :]).astype(bf16)
        yield 128
        x3[mine, :] = x2[mine, :] + nn(mix[mine, :], wo[...])
        yield 128
        yield from forward_tables(3, x3, jnp.broadcast_to(row(0) + row(7) + row(12), (8, 256)), row(13), row(14))
        yield from silu_pass(3, x3, sp4, xc3, False)

        z = nn(xc3[mine, :], wr[...])
        us[b, 0, pl.ds(8, TOK), :] = z[:, 0:128]
        us[b, 1, pl.ds(8, TOK), :] = z[:, 128:256]
        yield 128 * 3
        for r in range(SIDE):
            ql, qr = quads(r)
            inl = scale_ref[8 + (base + b) * 4 + ql]
            inr = scale_ref[8 + (base + b) * 4 + qr]
            for h in range(2):
                k = 8 + r * 16 + h * 8
                y = pltpu.roll(us[b, 0, pl.ds(k, 8), :], 64, 1)
                if r > 0:
                    y = y + us[b, 0, pl.ds(k - 16, 8), :] * mvu[at(r, h), :]
                if r < SIDE - 1:
                    y = y + us[b, 1, pl.ds(k + 16, 8), :] * mvd[at(r, h), :]
                inside = jnp.where(onleftn[b][h], inl, inr)
                err = jnp.where(lane < PIX, (y - tg_ref[at(r, h), :]) * inside, 0.0)
                lacc[...] += err * err
                xs[b, 0, pl.ds(k, 8), :] = (err * sc[...]).astype(bf16).astype(f32)
            yield 15
        for r in range(SIDE):
            tile0, tile1 = [], []
            for h in range(2):
                k = 8 + r * 16 + h * 8
                t0 = pltpu.roll(xs[b, 0, pl.ds(k, 8), :], 64, 1)
                if r < SIDE - 1:
                    t0 = t0 + xs[b, 0, pl.ds(k + 16, 8), :] * mvd[at(r, h), :]
                t1 = jnp.zeros((8, 128), f32)
                if r > 0:
                    t1 = xs[b, 0, pl.ds(k - 16, 8), :] * mvu[at(r, h), :]
                tile0.append(t0)
                tile1.append(t1)
            dyp[at(r, 0, 16), 0:128] = jnp.concatenate(tile0, axis=0).astype(bf16)
            dyp[at(r, 0, 16), 128:256] = jnp.concatenate(tile1, axis=0).astype(bf16)
            if r % GRAIN == GRAIN - 1:
                yield 10 * GRAIN

        yield from put_us(dyp[mine, :], wrt)
        weight_grad(gr, xc3, dyp, 0, 1)
        s1, s2 = yield from crop_sums(tap_back(sp4, x3))
        sum3, db, dg = backward_tables(3, s1, s2, row(13))
        gv[13] += dg
        gv[14] += db
        gv[12] += sum3
        yield 200
        for r in range(SIDE):
            halves = []
            for h in range(2):
                d = norm_grad(3, r, h, x3)
                gtop[at(r, h), :] = d
                halves.append(d)
            dpo[at(r, 0, 16), :] = jnp.concatenate(halves, axis=0).astype(bf16)
            if r % GRAIN == GRAIN - 1:
                yield 14 * GRAIN
        dmx[mine, :] = nn(dpo[mine, :], wot[...]).astype(bf16)
        yield 128

        def grad_out(two):
            def job():
                ga[:, 768:1024] += nn(mix[two, :].T, dpo[two, :])

            fill.append(job)

        later(grad_out)
        vlow = vs[mine, :] * jnp.asarray(CH**-0.5, bf16)
        for k in range(TOK // part):
            rows = pl.ds(r0 + k * part, part)
            da = nt(dmx[rows, :], vlow)
            p = prob[rows, :]
            t = da * p
            dsb[rows, :] = (t - p * jnp.sum(t, axis=1, keepdims=True)).astype(bf16)
            yield 70
        dv = nn(pb[mine, :].T, dmx[mine, :])
        trip[mine, 512:768] = dv.astype(bf16)
        gv[11] += jnp.sum(dv.reshape(TOK // 8, 8, CH), axis=0)
        yield 128
        dq = nn(dsb[mine, :], ks[mine, :])
        trip[mine, 0:256] = dq.astype(bf16)
        gv[10] += jnp.sum(dq.reshape(TOK // 8, 8, CH), axis=0)
        yield 128
        dk = nn(dsb[mine, :].T, qs[mine, :])
        trip[mine, 256:512] = dk.astype(bf16)
        yield 128
        dys[mine, :] = nn(trip[mine, :], wat[...])
        yield 128 * 3

        def grad_triple(two):
            turned = []
            for k in range(3):

                def job(k=k):
                    if not turned:
                        turned.append(nrm[two, :].T)
                    ga[:, k * 256 : (k + 1) * 256] += nn(turned[0], trip[two, k * 256 : (k + 1) * 256])

                fill.append(job)

        later(grad_triple)

        def plain(r, h):
            dy = dys[at(r, h), :]
            return dy, dy * x2[at(r, h), :]

        s1, s2 = yield from crop_sums(plain)
        sum2, db, dg = backward_tables(2, s1, s2, row(8))
        gv[8] += dg
        gv[9] += db
        sum2 = sum2 + sum3
        gv[7] += sum2
        yield 200
        for r in range(SIDE):
            halves = []
            for h in range(2):
                d = norm_grad(2, r, h, x2) + gtop[at(r, h), :]
                gtop[at(r, h), :] = d
                halves.append(d)
            spread_grad(0, r, jnp.concatenate(halves, axis=0))
            if r % GRAIN == GRAIN - 1:
                yield 18 * GRAIN
        yield from put_us(side[mine, 0:768], wt2)
        weight_grad(gk2, xc2, side, 0, 3)
        s1, s2 = yield from crop_sums(tap_back(sp2, x1))
        sum1, db, dg = backward_tables(1, s1, s2, row(5))
        gv[5] += dg
        gv[6] += db
        gv[4] += sum1
        dtb[pl.ds((base + b) * 8, 8), :] = sum1
        yield 200
        for r in range(SIDE):
            spread_grad(768, r, jnp.concatenate([norm_grad(1, r, h, x1) for h in range(2)], axis=0))
            if r % GRAIN == GRAIN - 1:
                yield 16 * GRAIN
        yield from put_us(side[mine, 768:1536], wt1)
        weight_grad(gk1, xc1, side, 768, 3)
        s1, s2 = yield from crop_sums(tap_back(sp1, x0))
        sum0, db, dg = backward_tables(0, s1, s2, row(2))
        gv[2] += dg
        gv[3] += db
        gv[0] += sum0 + sum2
        yield 200
        for r in range(SIDE):
            halves = [norm_grad(0, r, h, x0) + gtop[at(r, h), :] for h in range(2)]
            dps[at(r, 0, 16), :] = jnp.concatenate(halves, axis=0).astype(bf16)
            if r % GRAIN == GRAIN - 1:
                yield 14 * GRAIN

        def grad_stem(two):
            def job():
                gs[...] += nn(xt_ref[two, :].T, dps[two, :])

            fill.append(job)

        later(grad_stem)

    clocks = {b: float(b * SKEW) for b in range(PAIR)}
    streams = {b: stream(b) for b in range(PAIR)}
    filled = 0.0
    while streams:
        b = min(streams, key=lambda k: clocks[k])
        try:
            clocks[b] += next(streams[b])
        except StopIteration:
            del streams[b]
        now = min([clocks[k] for k in streams], default=1e18)
        while fill and filled < now:
            filled = max(filled, now if now < 1e17 else 0.0) + FILLCOST
            fill.pop(0)()

    @pl.when(step == last)
    def _():
        low = dtb[...].astype(bf16)
        hp = hpre[...]
        sg = jax.nn.sigmoid(hp)
        gp = (nn((hp * sg).astype(bf16).T, low) * 0.5).astype(bf16)
        hg = nt(low, wpj[...]) * (sg * (1.0 + hp * (1.0 - sg)))
        ge = (nn(feat_ref[...].T, hg.astype(bf16)) * 0.5).astype(bf16)
        twice = {10: 1.0, 11: 1.0}
        rows = [jnp.sum(gv[4 if k == 1 else k], axis=0, keepdims=True) * twice.get(k, 0.5) for k in range(15)]
        gnorm = jnp.concatenate(rows + [jnp.zeros((1, 256), f32)], axis=0)
        gstem = gs[...].T
        shared = pltpu.roll(lacc[...], PIX, 1)
        shared = jnp.concatenate([shared, jnp.zeros((AROW - 8, 128), f32)], axis=0)
        gstem = gstem + jnp.concatenate([shared] * VIRT, axis=0)
        for dy in range(3):
            for lo in range(0, 768, 256):
                part = gr[pl.ds(lo, 256), (dy // 2) * 128 : (dy // 2) * 128 + 128]
                if dy == 1:
                    part = pltpu.roll(part, 64, 1)
                grn[pl.ds(dy * 768 + lo, 256), :] = part
        for core in range(2):

            @pl.when(geo_ref[3] == core)
            def _(core=core):
                for f in range(VIRT):
                    z = f // 2
                    pair = [halves_ref[2 * part + ((f % 2) ^ core)] for part in range(2)]

                    def put(lo, hi, lanes, value, pair=pair, z=z):
                        for ref, first, end in zip(pair, (0, CUT), (CUT, PACKED)):
                            s, e = max(lo, first), min(hi, end)
                            if s < e:
                                ref[z, s - first : e - first, lanes] = value[s - lo : e - lo]

                    for dy in range(3):
                        lo, hi = max(f * KROW, dy * 768), min((f + 1) * KROW, (dy + 1) * 768)
                        if lo >= hi:
                            continue
                        src = pl.ds(lo - dy * 768, hi - lo)
                        d0, d1 = lo - f * KROW, hi - f * KROW
                        put(d0, d1, slice(0, 256), gk1[src, dy * 256 : (dy + 1) * 256].astype(bf16))
                        put(d0, d1, slice(256, 512), gk2[src, dy * 256 : (dy + 1) * 256].astype(bf16))
                    k = f * AROW
                    a1, a2, p0 = KROW, KROW + AROW, KROW + 2 * AROW
                    e0 = p0 + PROW
                    put(a1, a2, slice(0, 512), ga[k : k + AROW, 0:512].astype(bf16))
                    put(a2, p0, slice(0, 512), ga[k : k + AROW, 512:1024].astype(bf16))
                    put(p0, e0, slice(0, 256), gp[f * 2 * PROW : f * 2 * PROW + PROW, :])
                    put(p0, e0, slice(256, 512), gp[f * 2 * PROW + PROW : (f + 1) * 2 * PROW, :])
                    put(e0, TROW, slice(0, 512), ge[f * EROW : (f + 1) * EROW, :])
                    back = grn[pl.ds(f * KROW, 384), :].T[:TAIL, :]
                    keep = lax.broadcasted_iota(jnp.int32, (TAIL, 384), 1) < KROW
                    put(TROW, PACKED, slice(0, 384), jnp.where(keep, back, 0.0).astype(bf16))
                    put(TROW, TROW + 32, slice(384, 512), gstem[k : k + AROW, :].astype(bf16))
                    tile = gnorm[:, (f // 4) * 128 : (f // 4) * 128 + 128]
                    tile = pltpu.roll(tile, (128 - (f % 4) * AROW) % 128, 1)
                    keep = lax.broadcasted_iota(jnp.int32, (16, 128), 1) < AROW
                    put(TROW + 32, PACKED, slice(384, 512), jnp.where(keep, tile, 0.0).astype(bf16))
        loss_ref[...] = lacc[...]


SKEW = 700
FILLCOST = 128
GRAIN = 2


def run_step(packed, quad, geo, scal, feat, cp, tg):
    canvases = cp.shape[0] // TOK
    whole = pl.BlockSpec(memory_space=pltpu.VMEM)
    smem = pl.BlockSpec(memory_space=pltpu.SMEM)

    def rows(n, lanes):
        return pl.BlockSpec((n, lanes), lambda i, *_: (i, 0))

    items = scratch_list(canvases)
    return pl.pallas_call(
        functools.partial(step_kernel, [name for name, _, _ in items]),
        grid_spec=pltpu.PrefetchScalarGridSpec(
            num_scalar_prefetch=2,
            grid=(canvases // PAIR,),
            in_specs=[
                smem, whole, whole, whole, whole, whole, whole, rows(ROWS, 128), rows(ROWS, 128),
            ],
            out_specs=[whole] * 6,
            scratch_shapes=[pltpu.VMEM(shape, dtype) for _, shape, dtype in items],
        ),
        out_shape=[
            *[jax.ShapeDtypeStruct((VIRT // 2, CUT, 512), bf16)] * 4,
            jax.ShapeDtypeStruct((8, 128), f32),
            jax.ShapeDtypeStruct((8, 128), f32),
        ],
        compiler_params=pltpu.CompilerParams(
            dimension_semantics=("arbitrary",), vmem_limit_bytes=60 * 1024 * 1024
        ),
        name="unet_step",
    )(quad, geo, scal, *packed, feat, cp, tg)


def patch_kernel(image_ref, out_ref, staged):
    n = image_ref.shape[0]
    slot = staged.shape[0] // SIDE
    for r in range(SIDE):
        for c in range(3):
            staged[pl.ds(r * slot, n), c * 256 : (c + 1) * 256] = image_ref[:, c * 4096 + r * 256 : c * 4096 + r * 256 + 256]
    src = lax.broadcasted_iota(jnp.int32, (768, 256), 0)
    place = ((src >> 2) & 15) * 128 + (src >> 8) * 16 + ((src >> 6) & 3) * 4 + (src & 3)
    for j in range(SIDE // 2):
        lane = lax.broadcasted_iota(jnp.int32, (768, 256), 1) + j * 256
        out = nn(staged[...], (place == lane).astype(bf16))
        for r in range(SIDE):
            for i in range(2):
                rows = pl.ds(r * SIDE + 2 * j + i, n, stride=TOK)
                out_ref[rows, :] = out[r * slot : r * slot + n, i * 128 : (i + 1) * 128]


def patches(image):
    n = image.shape[0]
    slot = -(-n // 16) * 16
    whole = pl.BlockSpec(memory_space=pltpu.VMEM)
    return pl.pallas_call(
        patch_kernel,
        in_specs=[whole],
        out_specs=whole,
        out_shape=jax.ShapeDtypeStruct((n * TOK, 128), f32),
        scratch_shapes=[pltpu.VMEM((SIDE * slot, 768), bf16)],
        compiler_params=pltpu.CompilerParams(vmem_limit_bytes=48 * 1024 * 1024),
        cost_estimate=pl.CostEstimate(flops=2 * 32 * n * 768 * 2048, bytes_accessed=4 * n * TOK * 128, transcendentals=0),
        name="patches",
    )(image)


def upper_kernel(kernels, upper):
    upper[...] = kernels[0:CUT, :].astype(bf16)


def pack_kernel(copy, tokens, upper, stem, kernels, embed, project, attention, readout, norm, mine, block):
    a1, a2, p0 = KROW - CUT, KROW + AROW - CUT, KROW + 2 * AROW - CUT
    e0, tail, end = p0 + PROW, TROW - CUT, PACKED - CUT

    def put(lo, hi, value):
        for q in range(value.shape[1] // 128):
            block[q, lo:hi, :] = value[:, q * 128 : (q + 1) * 128].astype(bf16)

    put(0, a1, kernels[CUT:KROW, :])
    put(a1, a2, attention[:, 0:512])
    put(a2, p0, attention[:, 512:1024])
    put(p0, e0, jnp.concatenate([project[0:PROW, :], project[PROW : 2 * PROW, :]], axis=1))
    put(e0, tail, embed[...])
    for q in range(2, 4):
        block[q, tail:end, :] = jnp.zeros((TAIL, 128), bf16)
    put(tail, end, readout[:, 0:256])
    block[2, tail:end, 0 : KROW - 256] = readout[:, 256:KROW].astype(bf16)
    block[3, tail : tail + 32, 0:PIX] = stem[...].astype(bf16)
    block[3, tail + 32 : tail + 47, 0:AROW] = norm[...].astype(bf16)
    mine[0:end, :] = block[copy[0]]
    row = lax.broadcasted_iota(jnp.int32, (16, 128), 0)
    lane = lax.broadcasted_iota(jnp.int32, (16, 128), 1)
    tokens = tokens[0]
    limbs = jnp.where(lane == 0, tokens >> 6, jnp.where(lane == 1, tokens & 63, 0))
    mine[end : end + 16, :] = jnp.where(row == 0, limbs, 0).astype(f32).astype(bf16)


def pack_weights(masters, copy, tokens):
    stem, kernels, embed, project, attention, readout, norm = masters
    whole, smem = pl.BlockSpec(memory_space=pltpu.VMEM), pl.BlockSpec(memory_space=pltpu.SMEM)
    rest = PACKED - CUT
    upper = pl.pallas_call(
        upper_kernel,
        grid=(1,),
        in_specs=[pl.BlockSpec((CUT, 512), lambda i: (0, 0))],
        out_specs=pl.BlockSpec((CUT, 512), lambda i: (0, 0)),
        out_shape=jax.ShapeDtypeStruct((CUT, 512), bf16),
        name="pack_upper",
    )(kernels)
    mine = pl.pallas_call(
        pack_kernel,
        in_specs=[smem, smem, pl.BlockSpec(memory_space=pl.ANY)] + [whole] * 7,
        out_specs=whole,
        out_shape=jax.ShapeDtypeStruct((rest + 16, 128), bf16),
        scratch_shapes=[pltpu.VMEM((4, rest, 128), bf16)],
        name="pack_rest",
    )(copy.reshape(1), tokens.reshape(1), upper, stem, kernels, embed, project, attention, readout.T, norm.T)
    return upper, mine


def gather_weights(upper, mine, cp, tg):
    shards = lax.axis_size("fsdp")
    upper = lax.all_gather(upper, "fsdp", axis=0, tiled=False)
    got = [lax.ppermute(mine, "fsdp", [(i, (i + 2 * j) % shards) for i in range(shards)]) for j in range(1, 4)]
    both = jnp.stack([mine] + got)
    a, b = both[:, :PART], both[:, PART:]
    ga, gb = exchange(a, "dp", 1), exchange(b, "dp", 2)
    a, b, cp = lax.optimization_barrier((jnp.stack([a, ga]), jnp.stack([b, gb]), cp))
    ga, gb = exchange(a, "dp", 2), exchange(b, "dp", 1)
    a, b, tg = lax.optimization_barrier((jnp.concatenate([a, ga]), jnp.concatenate([b, gb]), tg))
    return (upper, a, b, exchange(a, "fsdp", 1), exchange(b, "fsdp", 1)), cp, tg


def slots_of(packed):
    rest = packed[:, CUT:].reshape(4, 2, PACKED - CUT, 4, 128)
    rest = jnp.stack([rest[z] for z in (0, 3, 2, 1)]).transpose(1, 3, 0, 2, 4)
    a, b = rest[..., :PART, :], jnp.stack([rest[:, q, :, PART:, :] for q in (0, 2, 1, 3)], axis=1)
    b = jnp.pad(b, ((0, 0), (0, 0), (0, 0), (0, 16), (0, 0)))
    return packed[:, :CUT], a[0], b[0], a[1], b[1]


def update_kernel(place, count, own, first, second, *refs):
    loss_out, total = refs[-2:]
    refs = refs[:-2]
    half, quarter = PACKED // 4, PACKED // 8
    for k in range(2):
        near, far = place[k], place[1 - k]
        at = k * 2 * half
        total[pl.ds(pl.multiple_of(at + near * half + far * quarter, 8), quarter), :] = own[k].astype(f32)
        total[pl.ds(pl.multiple_of(at + near * half + (1 - far) * quarter, 8), quarter), :] = first[k].astype(f32)
        there = at + (1 - near) * half
        total[pl.ds(pl.multiple_of(there + far * quarter, 8), quarter), :] = second[k, 0].astype(f32)
        total[pl.ds(pl.multiple_of(there + (1 - far) * quarter, 8), quarter), :] = second[k, 1].astype(f32)
    shared = total[TROW : TROW + 8, 384:512]
    lane = lax.broadcasted_iota(jnp.int32, (8, 128), 1)
    shared = jnp.where((lane >= PIX) & (lane < 2 * PIX), shared, 0.0)
    count = count[0:1, 0:1]
    loss_out[...] = jnp.sum(shared, axis=(0, 1), keepdims=True) / count
    rate = lr_scale * jnp.sqrt(count)
    a1, a2, p0 = KROW, KROW + AROW, KROW + 2 * AROW
    e0 = p0 + PROW
    everything = slice(None)
    cuts = [
        (0, everything, everything, total[TROW : TROW + 32, 384:512][:, :PIX]),
        (1, everything, everything, total[0:a1, :]),
        (2, everything, everything, total[e0:TROW, :]),
        (3, slice(0, PROW), everything, total[p0:e0, 0:256]),
        (3, slice(PROW, 2 * PROW), everything, total[p0:e0, 256:512]),
        (4, everything, slice(0, 512), total[a1:a2, :]),
        (4, everything, slice(512, 1024), total[a2:p0, :]),
        (5, everything, everything, total[TROW:PACKED, 0:384][:, :KROW]),
        (6, everything, everything, total[TROW + 32 : PACKED, 384:512][:15, :AROW]),
    ]
    for n, rows, lanes, grad in cuts:
        w, m, a, m_out, w_out, a_out = [refs[n + 7 * j] for j in range(6)]
        m_next = momentum_rate * m[rows, lanes] + grad
        w_next = w[rows, lanes] - rate * (grad + momentum_rate * m_next)
        m_out[rows, lanes] = m_next
        w_out[rows, lanes] = w_next
        a_out[rows, lanes] = average_rate * a[rows, lanes] + (1.0 - average_rate) * w_next


def turn(arrays):
    return [x.T if k in (5, 6) else x for k, x in enumerate(arrays)]


def update_fused(place, count, own, first, second, masters, moments, averages):
    whole = pl.BlockSpec(memory_space=pltpu.VMEM)
    smem = pl.BlockSpec(memory_space=pltpu.SMEM)
    state = turn(masters) + turn(moments) + turn(averages)
    out = pl.pallas_call(
        update_kernel,
        in_specs=[smem] + [whole] * 25,
        out_specs=[whole] * 22,
        out_shape=[jax.ShapeDtypeStruct(x.shape, f32) for x in state] + [jax.ShapeDtypeStruct((1, 1), f32)],
        scratch_shapes=[pltpu.VMEM((PACKED, 512), f32)],
        compiler_params=pltpu.CompilerParams(vmem_limit_bytes=32 * 1024 * 1024),
        name="update",
    )(place, count, own, first, second, *state)
    return (out[21][0, 0],) + tuple(turn(out[0:7]) + turn(out[7:14]) + turn(out[14:21]))


def signal_table():
    beta = np.linspace(0.0001, 0.02, TSTEPS, dtype=np.float64)
    return np.exp(np.cumsum(np.log(1.0 - beta))).astype(np.float32)


def time_features(time_steps):
    half_width = TEMB // 2
    frequency = jnp.exp(-math.log(10000.0) * jnp.arange(half_width, dtype=f32) / (half_width - 1))
    angles = time_steps.astype(f32)[..., None] * frequency
    return jnp.concatenate([jnp.sin(angles), jnp.cos(angles)], axis=-1)


def prepare(lab, time_steps, count, place):
    canvases = lab.shape[0]
    cut = jnp.sum(jnp.all(lab == lab[:, :, :1], axis=1).astype(jnp.int32), axis=1)
    left = jnp.sum((lab[:, :, 0] == lab[:, :1, 0]).astype(jnp.int32), axis=1)
    right = jnp.sum((lab[:, :, -1] == lab[:, :1, -1]).astype(jnp.int32), axis=1)
    own = jnp.stack([lab[:, 0, 0], lab[:, -1, 0], lab[:, 0, -1], lab[:, -1, -1]], axis=1)
    area = jnp.stack(
        [cut * left, cut * (SIDE - left), (SIDE - cut) * right, (SIDE - cut) * (SIDE - right)], axis=1
    ).astype(f32)
    here = [jnp.full_like(cut, x) for x in place]
    geo = jnp.stack([cut, left, right] + here + here[:2], axis=1).reshape(-1)
    line = jnp.arange(SIDE, dtype=jnp.int32)
    quad = (line >= left[:, None]).astype(jnp.int32) + 2 * (line >= right[:, None]).astype(jnp.int32)
    quad = quad.reshape(-1)
    hit = own[..., None] == jnp.arange(1, CROPS + 1, dtype=jnp.int32)
    times = jnp.sum(jnp.where(hit, time_steps[:, None, :], 0), axis=-1)
    eight = np.array([0, 0, 2, 2, 1, 1, 3, 3])
    feat = time_features(times[:, eight]).astype(bf16).reshape(-1, TEMB)
    picked = times[..., None] == jnp.arange(TSTEPS, dtype=jnp.int32)
    chosen = jnp.sum(jnp.where(picked, jnp.asarray(signal_table()), 0.0), axis=-1)
    inside = (own > 0).astype(f32)
    levels = [inside, jnp.sqrt(chosen), jnp.sqrt(1.0 - chosen), area]
    scal = jnp.concatenate([jnp.full((8,), count, f32)] + [x.reshape(-1) for x in levels])
    return quad, geo, scal, feat


def exchange(value, axis, bit):
    return lax.ppermute(value, axis, [(i, i ^ bit) for i in range(lax.axis_size(axis))])


def sum_over_all(value):
    for axis in ("fsdp", "dp"):
        bit = 1
        while bit < lax.axis_size(axis):
            value = value + exchange(value, axis, bit)
            bit *= 2
    return value


def join(a, b):
    return (a.astype(f32) + b.astype(f32)).astype(bf16)


def halves(value, which):
    n = value.shape[1] // 2
    low, high = value[:, :n], value[:, n:]
    return jnp.where(which == 0, low, high), jnp.where(which == 0, high, low)


def reduce_grads(keep, send):
    parts = [join(own, exchange(other, "fsdp", 1)) for own, other in zip(keep, send)]
    near, far = lax.axis_index("dp") % 2, lax.axis_index("dp") // 2
    for first, second in (((near, 1), (far, 2)), ((far, 2), (near, 1))):
        split = [halves(parts[0], first[0]), halves(parts[1], second[0])]
        came = [exchange(split[0][1], "dp", first[1]), exchange(split[1][1], "dp", second[1])]
        parts = [join(split[0][0], came[0]), join(split[1][0], came[1])]
    blocks = jnp.stack(parts, axis=1)
    chips, shards = blocks.shape[0], lax.axis_size("fsdp")
    chip = lax.axis_index("fsdp") // 2
    own = lax.dynamic_index_in_dim(blocks, chip, 0, keepdims=False).astype(f32)
    for j in range(1, chips):
        out = lax.dynamic_index_in_dim(blocks, (chip + j) % chips, 0, keepdims=False)
        own = own + lax.ppermute(out, "fsdp", [(i, (i + 2 * j) % shards) for i in range(shards)]).astype(f32)
    own = own.astype(bf16)
    first = jnp.stack([exchange(own[0], "dp", 2), exchange(own[1], "dp", 1)])
    both = jnp.stack([own, first], axis=1)
    second = jnp.stack([exchange(both[0], "dp", 1), exchange(both[1], "dp", 2)])
    return jnp.stack([near, far]).astype(jnp.int32), own, first, second


def assemble(place, own, first, second):
    n = own.shape[1]
    parts = []
    for k in range(2):
        near, far = place[k], place[1 - k]
        mine = jnp.where(far == 0, jnp.concatenate([own[k], first[k]]), jnp.concatenate([first[k], own[k]]))
        s = second[k]
        theirs = jnp.where(far == 0, jnp.concatenate([s[0], s[1]]), jnp.concatenate([s[1], s[0]]))
        parts.append(jnp.where(near == 0, jnp.concatenate([mine, theirs]), jnp.concatenate([theirs, mine])))
    return jnp.concatenate(parts).astype(f32)


def on_device(clean, noise, crop_labels, time_steps, *state):
    masters, moments, averages = state[0:7], state[7:14], state[14:21]
    shards = lax.axis_size("fsdp")
    index, copy = lax.axis_index("fsdp"), lax.axis_index("dp")
    tokens = jnp.sum((crop_labels > 0).astype(jnp.int32))
    direct = shards == VIRT and lax.axis_size("dp") == 4
    cp, tg = patches(clean), patches(noise)
    if direct:
        packed, cp, tg = gather_weights(*pack_weights(masters, copy, tokens), cp, tg)
        inputs = prepare(crop_labels, time_steps, 0.0, (index % 2, index // 2, copy))
    else:
        own = lax.all_gather(pack_rows([w.astype(bf16) for w in masters]), "fsdp", axis=0, tiled=False)
        packed = slots_of(repack(own, shards, VIRT))
        count = sum_over_all(PATCH * PATCH * tokens.astype(f32).reshape(1, 1))[0, 0]
        inputs = prepare(crop_labels, time_steps, count, (0, 0, 0))
    *grads, loss, total = run_step(packed, *inputs, cp, tg)
    keep, send = grads[0::2], grads[1::2]
    if not direct:
        core = index % 2
        keep, send = jnp.concatenate(keep, axis=1), jnp.concatenate(send, axis=1)
        blocks = jnp.stack([keep, send], axis=1).reshape(VIRT, PACKED, 512)
        blocks = repack(blocks, VIRT, shards)
        blocks = blocks.reshape(shards // 2, 2, *blocks.shape[1:])
        keep = lax.dynamic_index_in_dim(blocks, core, 1, keepdims=False)
        send = lax.dynamic_index_in_dim(blocks, 1 - core, 1, keepdims=False)
        n = keep.shape[1] // 2
        keep, send = [keep[:, :n], keep[:, n:]], [send[:, :n], send[:, n:]]
    place, own, first, second = reduce_grads(keep, send)
    if direct:
        return update_fused(place, total, own, first, second, masters, moments, averages)
    rate = lr_scale * jnp.sqrt(count)
    total_loss = sum_over_all(jnp.sum(loss).reshape(1, 1))[0, 0]
    cut = [masters[1].shape[0], masters[0].shape[0], masters[3].shape[0], masters[2].shape[0]]
    grads = unpack_rows(assemble(place, own, first, second), *cut)
    moment_next = tuple(momentum_rate * m + g for m, g in zip(moments, grads))
    master_next = tuple(w - rate * (g + momentum_rate * m) for w, g, m in zip(masters, grads, moment_next))
    average_next = tuple(average_rate * a + (1.0 - average_rate) * w for a, w in zip(averages, master_next))
    return (total_loss / count,) + moment_next + master_next + average_next


def solution(mesh):
    split = P(("dp", "fsdp"), None)
    in_specs = (split, split, P(("dp", "fsdp"), None, None), split) + (P("fsdp", None),) * 21
    out_specs = (P(),) + (P("fsdp", None),) * 21
    return jax.shard_map(on_device, mesh=mesh, in_specs=in_specs, out_specs=out_specs, check_vma=False)
```

```python
import functools
import math

import jax
import jax.numpy as jnp
import numpy as np
from jax import lax
from jax.experimental import pallas as pl
from jax.experimental.pallas import tpu as pltpu
from jax.sharding import PartitionSpec as P

GROUPS = 32
TEMB = 128
SIDE = 16
PATCH = 4
CROPS = 4
TSTEPS = 1000
TOK = SIDE * SIDE
CH = 256
PIX = 3 * PATCH * PATCH
PAIR = 4
ROWS = PAIR * TOK
VIRT = 8
TAIL = 48

eps_norm = 1e-05
lr_scale = 0.01
momentum_rate = 0.5
average_rate = 0.5
far_score = -1e30
f32 = jnp.float32
bf16 = jnp.bfloat16


def pad_to(value, rows, lanes):
    return jnp.pad(value, ((0, rows - value.shape[0]), (0, lanes - value.shape[1])))


def pack_rows(parts):
    stem, kernels, embed, project, attention, readout, norm = parts
    half = project.shape[0] // 2
    small = jnp.concatenate([pad_to(stem, 32, 128), pad_to(norm.T, 16, 128)], axis=0)
    tail = jnp.concatenate([pad_to(readout.T, TAIL, 384), small], axis=1)
    rows = [kernels, attention[:, :512], attention[:, 512:]]
    rows += [jnp.concatenate([project[:half], project[half:]], axis=1), embed, tail]
    rows = jnp.concatenate(rows, axis=0)
    return pad_to(rows, -(-rows.shape[0] // 8) * 8, 512)


def unpack_rows(rows, k, a, p, e):
    half = p // 2
    at = [0, k, k + a, k + 2 * a, k + 2 * a + half, k + 2 * a + half + e, k + 2 * a + half + e + TAIL]
    kernels, left, right, halves, embed, tail = [rows[at[i] : at[i + 1]] for i in range(6)]
    project = jnp.concatenate([halves[:, :256], halves[:, 256:]], axis=0)
    stem, norm = tail[:a, 384 : 384 + PIX], tail[32 : 32 + 15, 384 : 384 + a].T
    return stem, kernels, embed, project, jnp.concatenate([left, right], axis=1), tail[:, :k].T, norm


def repack(packed, parts_now, parts_next):
    if parts_now == parts_next:
        return packed
    cut = [n // parts_now for n in (9 * CH, CH, 2 * CH, CH // 2)]
    pieces = jax.vmap(lambda rows: unpack_rows(rows, *cut))(packed)
    whole = [piece.reshape(-1, piece.shape[-1]) for piece in pieces]
    split = [piece.reshape(parts_next, -1, piece.shape[-1]) for piece in whole]
    return jax.vmap(lambda *p: pack_rows(p))(*split)


KROW = 9 * CH // VIRT
AROW = CH // VIRT
PROW = CH // VIRT
EROW = TEMB // VIRT
TROW = KROW + 2 * AROW + PROW + EROW
PACKED = TROW + TAIL
CUT = PACKED // 2
PART = (PACKED - CUT) // 2


def lane_groups(value):
    lane = lax.broadcasted_iota(jnp.int32, (8, 128), 1)
    tiles = []
    for t in range(2):
        x = value[:, t * 128 : (t + 1) * 128]
        for s in (1, 2, 4):
            x = x + jnp.where((lane & s) == 0, pltpu.roll(x, 128 - s, 1), pltpu.roll(x, s, 1))
        tiles.append(x)
    return jnp.concatenate(tiles, axis=1)


def quad_rows(q0, q1, q2, q3):
    sub = lax.broadcasted_iota(jnp.int32, (8, 128), 0)
    tiles = []
    for t in range(2):
        a, b, c, d = [q[:, t * 128 : (t + 1) * 128] for q in (q0, q1, q2, q3)]
        low = sub < 4
        u = jnp.where(low, a, pltpu.roll(b, 4, 0)) + jnp.where(low, pltpu.roll(a, 4, 0), b)
        v = jnp.where(low, c, pltpu.roll(d, 4, 0)) + jnp.where(low, pltpu.roll(c, 4, 0), d)
        even = (sub & 2) == 0
        w = jnp.where(even, u, pltpu.roll(v, 2, 0)) + jnp.where(even, pltpu.roll(u, 6, 0), v)
        w = w + jnp.where((sub & 1) == 0, pltpu.roll(w, 7, 0), pltpu.roll(w, 1, 0))
        tiles.append(w)
    return jnp.concatenate(tiles, axis=1)


QUAD_ROW = (0, 4, 2, 6)


def nt(a, b):
    return lax.dot_general(a, b, (((1,), (1,)), ((), ())), preferred_element_type=f32)


def nn(a, b):
    return lax.dot_general(a, b, (((1,), (0,)), ((), ())), preferred_element_type=f32)


PADROWS = TOK + 16


def scratch_list(canvases):
    n = 8 * canvases
    items = [
        ("wk1", (2304, 256), bf16), ("wk2", (2304, 256), bf16), ("wt1", (768, 768), bf16), ("wt2", (768, 768), bf16),
        ("wr", (768, 256), bf16), ("wrt", (256, 768), bf16), ("wqkv", (256, 768), bf16), ("wat", (768, 256), bf16),
        ("wo", (256, 256), bf16), ("wot", (256, 256), bf16), ("ws", (128, 256), bf16), ("wpj", (512, 256), bf16),
        ("wem", (128, 512), bf16), ("vec", (16, 256), f32), ("tbs", (n, 256), f32), ("hpre", (n, 512), f32),
        ("grn", (2304 + 96, 128), f32), ("low", (4, VIRT, PACKED - CUT, 128), bf16), ("sc", (8, 128), f32),
        ("xt", (ROWS, 128), bf16),
        ("gk1", (768, 768), f32), ("gk2", (768, 768), f32), ("gr", (768, 256), f32), ("ga", (256, 1024), f32),
        ("gs", (128, 256), f32), ("gv", (15, 8, 256), f32), ("dtb", (n, 256), f32), ("lacc", (8, 128), f32),
        ("x0", (ROWS, 256), f32), ("x1", (ROWS, 256), f32), ("x2", (ROWS, 256), f32), ("x3", (ROWS, 256), f32),
        ("sp1", (ROWS, 256), f32), ("sp2", (ROWS, 256), f32), ("sp4", (ROWS, 256), f32),
        ("xs", (PAIR, 2, PADROWS, 128), f32), ("us", (PAIR, 6, PADROWS, 128), f32),
        ("side", (ROWS, 1536), bf16),
        ("xc1", (ROWS, 768), bf16), ("xc2", (ROWS, 768), bf16), ("xc3", (ROWS, 768), bf16),
        ("nrm", (ROWS, 256), bf16), ("qs", (ROWS, 256), bf16), ("ks", (ROWS, 256), bf16), ("vs", (ROWS, 256), bf16),
        ("prob", (ROWS, 256), f32), ("pb", (ROWS, 256), bf16), ("dsb", (ROWS, 256), bf16), ("mix", (ROWS, 256), bf16), ("dmx", (ROWS, 256), bf16), ("dpo", (ROWS, 256), bf16),
        ("gtop", (ROWS, 256), f32), ("dys", (ROWS, 256), f32),
        ("dps", (ROWS, 256), bf16),
        ("dyp", (ROWS, 256), bf16), ("trip", (ROWS, 768), bf16),
        ("mvu", (ROWS, 128), f32), ("mvd", (ROWS, 128), f32), ("mbu", (ROWS, 128), bf16), ("mbd", (ROWS, 128), bf16),
        ("ctab", (PAIR, 4, 4, 8, 256), f32),
    ]
    for b in range(PAIR):
        items += [(f"pref{b}", (2, 2, 17, 8, 256), f32)]
        items += [(f"tab{b}_{slot}", (4, 2, 8, 256), f32) for slot in range(7)]
    return items


def step_kernel(names, *refs):
    quad_ref, geo_ref, scale_ref, up_ref, oa_ref, ob_ref, ca_ref, cb_ref, feat_ref, cp_ref, tg_ref = refs[:11]
    halves_ref, (loss_ref, total_ref) = refs[11:15], refs[15:17]
    S = dict(zip(names, refs[17:]))
    wk1, wk2, wt1, wt2, wr, wrt, wqkv, wat, wo, wot = [S[k] for k in ("wk1", "wk2", "wt1", "wt2", "wr", "wrt", "wqkv", "wat", "wo", "wot")]
    ws, wpj, wem, vec, tbs, hpre = [S[k] for k in ("ws", "wpj", "wem", "vec", "tbs", "hpre")]
    gk1, gk2, gr, ga, gs, gv, dtb, lacc = [S[k] for k in ("gk1", "gk2", "gr", "ga", "gs", "gv", "dtb", "lacc")]
    x0, x1, x2, x3, sp1, sp2, sp4, xs, us = [S[k] for k in ("x0", "x1", "x2", "x3", "sp1", "sp2", "sp4", "xs", "us")]
    side, xc1, xc2, xc3, nrm, qs, ks, vs = [S[k] for k in ("side", "xc1", "xc2", "xc3", "nrm", "qs", "ks", "vs")]
    prob, mix, dmx, dpo, gtop, dys = [S[k] for k in ("prob", "mix", "dmx", "dpo", "gtop", "dys")]
    dps, dyp, trip = [S[k] for k in ("dps", "dyp", "trip")]
    mvu, mvd, mbu, mbd, ctab = [S[k] for k in ("mvu", "mvd", "mbu", "mbd", "ctab")]
    grn, xt_ref, pb, dsb, low, sc = S["grn"], S["xt"], S["pb"], S["dsb"], S["low"], S["sc"]
    pref = [S[f"pref{b}"] for b in range(PAIR)]
    tab = [[S[f"tab{b}_{slot}"] for slot in range(7)] for b in range(PAIR)]
    step = pl.program_id(0)
    last = pl.num_programs(0) - 1
    canvases = tbs.shape[0] // 8

    @pl.when(step == 0)
    def _():
        core, chip, copy = geo_ref[3], geo_ref[4], geo_ref[5]
        tokens = jnp.zeros((16, 128), f32)
        for p, (a_ref, b_ref) in enumerate(((oa_ref, ob_ref), (ca_ref, cb_ref))):
            for s in range(4):
                for j in range(4):
                    f = ((chip - j) & 3) * 2 + (core ^ p)
                    low[copy ^ s, f, 0:PART, :] = a_ref[s, j]
                    low[copy ^ ((s >> 1) | ((s & 1) << 1)), f, PART : 2 * PART, :] = b_ref[s, j, 0:PART, :]
                    tokens = tokens + b_ref[s, j, PART : PART + 16, :].astype(f32)
        lanes = lax.broadcasted_iota(jnp.int32, (16, 128), 1)
        tokens = jnp.sum(tokens * jnp.where(lanes == 0, 64.0, 1.0), axis=(0, 1), keepdims=True)
        count = scale_ref[0] + PATCH * PATCH * tokens
        sc[...] = jnp.broadcast_to(2.0 / count, (8, 128))
        total_ref[...] = jnp.broadcast_to(count, (8, 128))

        def lower(f, lo, hi, first, end):
            tiles = [low[q, f, lo - CUT : hi - CUT, :] for q in range(first // 128, end // 128)]
            return tiles[0] if len(tiles) == 1 else jnp.concatenate(tiles, axis=1)

        a1, a2, p0 = KROW, KROW + AROW, KROW + 2 * AROW
        e0 = p0 + PROW
        for f in range(VIRT):
            wk1[pl.ds(f * KROW, CUT), :] = up_ref[f, :, 0:256]
            wk2[pl.ds(f * KROW, CUT), :] = up_ref[f, :, 256:512]
            wk1[pl.ds(f * KROW + CUT, KROW - CUT), :] = lower(f, CUT, KROW, 0, 256)
            wk2[pl.ds(f * KROW + CUT, KROW - CUT), :] = lower(f, CUT, KROW, 256, 512)
            back = lower(f, TROW, PACKED, 0, 384).astype(f32)
            back = jnp.concatenate([back, jnp.zeros((128 - TAIL, 384), f32)], axis=0).T
            grn[pl.ds(f * KROW, KROW), :] = back[:KROW, :]
            wqkv[pl.ds(f * AROW, AROW), 0:512] = lower(f, a1, a2, 0, 512)
            wqkv[pl.ds(f * AROW, AROW), 512:768] = lower(f, a2, p0, 0, 256)
            wo[pl.ds(f * AROW, AROW), :] = lower(f, a2, p0, 256, 512)
            wpj[pl.ds(f * 2 * PROW, PROW), :] = lower(f, p0, e0, 0, 256)
            wpj[pl.ds(f * 2 * PROW + PROW, PROW), :] = lower(f, p0, e0, 256, 512)
            wem[pl.ds(f * EROW, EROW), :] = lower(f, e0, TROW, 0, 512)
        stem = jnp.concatenate([lower(f, TROW, TROW + 32, 384, 512) for f in range(VIRT)], axis=0)
        ws[...] = stem.T
        for t in range(2):
            tile = jnp.zeros((16, 128), f32)
            for j in range(4):
                part = lower(4 * t + j, TROW + 32, PACKED, 384, 512).astype(f32)
                part = jnp.where(lax.broadcasted_iota(jnp.int32, (16, 128), 1) < AROW, part, 0.0)
                tile = tile + (pltpu.roll(part, j * AROW, 1) if j else part)
            vec[:, t * 128 : (t + 1) * 128] = tile
        for dy in range(3):
            for dx in range(3):
                rows = pl.ds((dy * 3 + dx) * 256, 256)
                wt1[pl.ds(dy * 256, 256), dx * 256 : (dx + 1) * 256] = wk1[rows, :].T
                wt2[pl.ds(dy * 256, 256), dx * 256 : (dx + 1) * 256] = wk2[rows, :].T
        for j in range(3):
            wat[pl.ds(j * 256, 256), :] = wqkv[:, j * 256 : (j + 1) * 256].T
        wot[...] = wo[...].T
        for dx in range(3):
            rows = [grn[pl.ds(dy * 768 + dx * 256, 256), :] for dy in range(3)]
            tile0 = (rows[0] + pltpu.roll(rows[1], 64, 1)).astype(bf16)
            tile1 = rows[2].astype(bf16)
            wr[pl.ds(dx * 256, 256), 0:128] = tile0
            wr[pl.ds(dx * 256, 256), 128:256] = tile1
            wrt[0:128, dx * 256 : (dx + 1) * 256] = tile0.T
            wrt[128:256, dx * 256 : (dx + 1) * 256] = tile1.T
        hp = nn(feat_ref[...], wem[...])
        hpre[...] = hp
        tbs[...] = nn(jax.nn.silu(hp).astype(bf16), wpj[...]) + vec[1:2, :]
        grn[pl.ds(2304, 96), :] = jnp.zeros((96, 128), f32)
        for ref in [gk1, gk2, gr, ga, gs, gv, lacc] + pref:
            ref[...] = jnp.zeros_like(ref)

    base = step * PAIR
    cuts = [geo_ref[(base + b) * 8] for b in range(PAIR)]
    lefts = [geo_ref[(base + b) * 8 + 1] for b in range(PAIR)]
    rights = [geo_ref[(base + b) * 8 + 2] for b in range(PAIR)]
    iota8 = lax.broadcasted_iota(jnp.int32, (8, 256), 0)
    iota8n = lax.broadcasted_iota(jnp.int32, (8, 128), 0)
    onleft = [[iota8 < (cuts[b] - 8 * h) for h in range(2)] for b in range(PAIR)]
    onleftn = [[iota8n < (cuts[b] - 8 * h) for h in range(2)] for b in range(PAIR)]
    hasl = [[(iota8n + 8 * h != 0) & (iota8n + 8 * h != cuts[b]) for h in range(2)] for b in range(PAIR)]
    hasr = [[(iota8n + 8 * h != 15) & (iota8n + 8 * h != cuts[b] - 1) for h in range(2)] for b in range(PAIR)]
    lane = lax.broadcasted_iota(jnp.int32, (8, 128), 1)
    fill = []

    def row(k):
        return vec[k : k + 1, :]

    def stream(b):
        r0 = b * TOK
        mine = pl.ds(r0, TOK)
        areas = [scale_ref[8 + 12 * canvases + (base + b) * 4 + q] for q in range(4)]
        sub = lax.broadcasted_iota(jnp.int32, (8, 256), 0)
        cnt = jnp.where(sub < 4, jnp.where(sub < 2, areas[0], areas[2]), jnp.where(sub < 6, areas[1], areas[3]))
        inv = 1.0 / jnp.maximum(cnt, 1.0)

        def at(r, h=0, n=8):
            return pl.ds(r0 + r * 16 + h * 8, n)

        def kind(r):
            return quad_ref[(base + b) * SIDE + r]

        def quads(r):
            t = kind(r)
            return t & 1, 2 + (t >> 1)

        def masks():
            for r in range(SIDE):
                upl = ((lefts[b] != r) & (r > 0)).astype(f32)
                upr = ((rights[b] != r) & (r > 0)).astype(f32)
                dnl = ((lefts[b] != r + 1) & (r < SIDE - 1)).astype(f32)
                dnr = ((rights[b] != r + 1) & (r < SIDE - 1)).astype(f32)
                up = jnp.concatenate([jnp.where(onleftn[b][h], upl, upr) for h in range(2)], axis=0)
                dn = jnp.concatenate([jnp.where(onleftn[b][h], dnl, dnr) for h in range(2)], axis=0)
                mvu[at(r, 0, 16), :] = up
                mvd[at(r, 0, 16), :] = dn
                mbu[at(r, 0, 16), :] = up.astype(bf16)
                mbd[at(r, 0, 16), :] = dn.astype(bf16)
                ql, qr = quads(r)
                level = 8 + 4 * canvases + (base + b) * 4
                al, ar = scale_ref[level + ql], scale_ref[level + qr]
                sl, sr = scale_ref[level + 4 * canvases + ql], scale_ref[level + 4 * canvases + qr]
                mixed = []
                for h in range(2):
                    m = onleftn[b][h]
                    noisy = jnp.where(m, sl, sr) * tg_ref[at(r, h), :]
                    mixed.append(jnp.where(m, al, ar) * cp_ref[at(r, h), :] + noisy)
                xt_ref[at(r, 0, 16), :] = jnp.concatenate(mixed, axis=0).astype(bf16)
            yield 100

        def put_table(slot, table):
            of = [jnp.broadcast_to(table[k : k + 1, :], (8, 256)) for k in QUAD_ROW]
            for t in range(4):
                for h in range(2):
                    tab[b][slot][t, h] = jnp.where(onleft[b][h], of[t & 1], of[2 + (t >> 1)])

        def pick(slot, r, h):
            return tab[b][slot][kind(r), h]

        def crop_sums(values_of):
            total = [None, None]
            left = [None, None]
            p = pref[b]
            for r in range(SIDE):
                halves = [values_of(r, h) for h in range(2)]
                for j in range(2):
                    a0, a1 = halves[0][j], halves[1][j]
                    lp = jnp.where(onleft[b][0], a0, 0.0) + jnp.where(onleft[b][1], a1, 0.0)
                    tp = a0 + a1
                    left[j] = lp if r == 0 else left[j] + lp
                    total[j] = tp if r == 0 else total[j] + tp
                    p[j, 0, r + 1] = left[j]
                    p[j, 1, r + 1] = total[j]
                if r % GRAIN == GRAIN - 1:
                    yield 16 * GRAIN
            got = []
            for j in range(2):
                q0 = p[j, 0, lefts[b]]
                q1 = left[j] - q0
                q2 = p[j, 1, rights[b]] - p[j, 0, rights[b]]
                q3 = (total[j] - left[j]) - q2
                got.append(quad_rows(q0, q1, q2, q3))
            yield 100
            return got

        def forward_tables(n, xref, bias, gain, shift):
            def both(r, h):
                x = xref[at(r, h), :]
                return x, x * x

            s1, s2 = yield from crop_sums(both)
            own = s1 * inv
            mean = lane_groups(own + bias) * 0.125
            apart = own + bias - mean
            var = lane_groups(jnp.maximum(s2 * inv - own * own, 0.0) + apart * apart) * 0.125
            rs = lax.rsqrt(var + eps_norm)
            a = rs * gain
            e = bias - mean
            put_table(n, a)
            put_table(4, e * a + shift)
            ctab[b, n, 0] = a
            ctab[b, n, 1] = rs
            ctab[b, n, 2] = e
            ctab[b, n, 3] = s1
            yield 250

        def backward_tables(n, s1, s2, gain):
            a, rs, e, sx = [ctab[b, n, j] for j in range(4)]
            sn = rs * (s2 + e * s1)
            m1 = lane_groups(gain * s1 * inv) * 0.125
            m2 = lane_groups(gain * sn * inv) * 0.125
            v = rs * rs * m2
            u = rs * m1 + e * v
            put_table(5, v)
            put_table(6, u)
            return a * s1 - v * sx - cnt * u, s1, sn

        def silu_pass(n, xref, spref, xcref, vertical):
            if vertical:
                side[at(0, 0, 16), 0:768] = jnp.zeros((16, 768), bf16)
                side[at(SIDE - 1, 0, 16), 768:1536] = jnp.zeros((16, 768), bf16)
            for r in range(SIDE):
                acts = []
                for h in range(2):
                    x = xref[at(r, h), :]
                    y = x * pick(n, r, h) + pick(4, r, h)
                    hy = 0.5 * y
                    t = jnp.tanh(hy)
                    act = hy * t + hy
                    sig = 0.5 * t + 0.5
                    spref[at(r, h), :] = sig + act - act * sig
                    acts.append(act)
                    for c in range(2):
                        xs[b, c, pl.ds(8 + r * 16 + h * 8, 8), :] = act[:, c * 128 : (c + 1) * 128]
                k0 = 8 + r * 16
                if vertical:
                    below = mbu[at(r + 1, 0, 16), :] if r < SIDE - 1 else None
                    above = mbd[at(r - 1, 0, 16), :] if r > 0 else None
                for c in range(2):
                    taps = []
                    for dx in (-1, 0, 1):
                        pieces = []
                        for h in range(2):
                            if dx == 0:
                                pieces.append(acts[h][:, c * 128 : (c + 1) * 128])
                                continue
                            piece = xs[b, c, pl.ds(k0 + h * 8 + dx, 8), :]
                            if dx == -1:
                                piece = jnp.where(hasl[b][h], piece, 0.0)
                            if dx == 1:
                                piece = jnp.where(hasr[b][h], piece, 0.0)
                            pieces.append(piece)
                        taps.append(jnp.concatenate(pieces, axis=0).astype(bf16))
                    for k, tap in enumerate(taps):
                        lanes = slice(k * 256 + c * 128, k * 256 + c * 128 + 128)
                        low = slice(768 + lanes.start, 768 + lanes.stop)
                        xcref[at(r, 0, 16), lanes] = tap
                        if vertical and r < SIDE - 1:
                            side[at(r + 1, 0, 16), lanes] = tap * below
                        if vertical and r > 0:
                            side[at(r - 1, 0, 16), low] = tap * above
                if r % GRAIN == GRAIN - 1:
                    yield 30 * GRAIN

        def spread_grad(first, r, value):
            low = value.astype(bf16)
            side[at(r, 0, 16), first + 256 : first + 512] = low
            if r == 0:
                side[at(0, 0, 16), first + 512 : first + 768] = jnp.zeros((16, 256), bf16)
            if r == SIDE - 1:
                side[at(r, 0, 16), first : first + 256] = jnp.zeros((16, 256), bf16)
            below = mbu[at(r + 1, 0, 16), :] if r < SIDE - 1 else None
            above = mbd[at(r - 1, 0, 16), :] if r > 0 else None
            for c in range(2):
                part = low[:, c * 128 : (c + 1) * 128]
                if r > 0:
                    side[at(r - 1, 0, 16), first + c * 128 : first + c * 128 + 128] = part * above
                if r < SIDE - 1:
                    side[at(r + 1, 0, 16), first + 512 + c * 128 : first + 640 + c * 128] = part * below

        def tap_back(spref, xref):
            def values(r, h):
                k = 8 + r * 16 + h * 8
                cols = []
                for c in range(2):
                    d = us[b, 2 + c, pl.ds(k, 8), :]
                    d = d + jnp.where(hasr[b][h], us[b, c, pl.ds(k + 1, 8), :], 0.0)
                    d = d + jnp.where(hasl[b][h], us[b, 4 + c, pl.ds(k - 1, 8), :], 0.0)
                    cols.append(d)
                dy = jnp.concatenate(cols, axis=1) * spref[at(r, h), :]
                dys[at(r, h), :] = dy
                return dy, dy * xref[at(r, h), :]

            return values

        def norm_grad(n, r, h, xref):
            return dys[at(r, h), :] * pick(n, r, h) - xref[at(r, h), :] * pick(5, r, h) - pick(6, r, h)

        def nine(xcref):
            return jnp.concatenate([side[mine, 0:768], xcref[mine, :], side[mine, 768:1536]], axis=1)

        def put_us(lhs, rhs_ref):
            for dx in range(3):
                u = nn(lhs, rhs_ref[:, dx * 256 : (dx + 1) * 256])
                for c in range(2):
                    us[b, dx * 2 + c, pl.ds(8, TOK), :] = u[:, c * 128 : (c + 1) * 128]
                yield 64 * (lhs.shape[1] // 256)

        def later(job):
            if b % 2:
                job(pl.ds(r0 - TOK, 2 * TOK))

        def weight_grad(acc, xref, dref, first, width):
            def job(two):
                for dx in range(3):
                    turned = []

                    def one(dy, dx=dx, turned=turned):
                        if not turned:
                            turned.append(xref[two, dx * 256 : (dx + 1) * 256].T)
                        cols = slice(dy * 256, (dy + 1) * 256)
                        grad = dref[two, first + dy * 256 : first + (dy + 1) * 256]
                        acc[pl.ds(dx * 256, 256), cols] += nn(turned[0], grad)

                    for dy in range(width):
                        fill.append(lambda dy=dy, one=one: one(dy))

            later(job)

        yield from masks()
        x0[mine, :] = nn(xt_ref[mine, :], ws[...])
        yield 128
        yield from forward_tables(0, x0, jnp.broadcast_to(row(0), (8, 256)), row(2), row(3))
        yield from silu_pass(0, x0, sp1, xc1, True)
        x1[mine, :] = nn(nine(xc1), wk1[...])
        yield 128 * 9
        bias1 = tbs[pl.ds((base + b) * 8, 8), :] + row(4)
        yield from forward_tables(1, x1, bias1, row(5), row(6))
        yield from silu_pass(1, x1, sp2, xc2, True)
        x2[mine, :] = x0[mine, :] + nn(nine(xc2), wk2[...])
        yield 128 * 9
        yield from forward_tables(2, x2, jnp.broadcast_to(row(0) + row(7), (8, 256)), row(8), row(9))
        for r in range(SIDE):
            halves = [x2[at(r, h), :] * pick(2, r, h) + pick(4, r, h) for h in range(2)]
            nrm[at(r, 0, 16), :] = jnp.concatenate(halves, axis=0).astype(bf16)
            if r % GRAIN == GRAIN - 1:
                yield 10 * GRAIN
        ks[mine, :] = nn(nrm[mine, :], wqkv[:, 256:512]).astype(bf16)
        qs[mine, :] = (nn(nrm[mine, :], wqkv[:, 0:256]) + row(10)).astype(bf16)
        vs[mine, :] = (nn(nrm[mine, :], wqkv[:, 512:768]) + row(11)).astype(bf16)
        yield 128 * 2

        def quadrant(p):
            col, line = p & 15, p >> 4
            left = jnp.where(line < lefts[b], 0, 1)
            right = jnp.where(line < rights[b], 2, 3)
            return jnp.where(col < cuts[b], left, right)

        qq = quadrant(lax.broadcasted_iota(jnp.int32, (1, TOK), 1))
        part = 64
        scores = []
        for k in range(TOK // part):
            scores.append(nt(qs[pl.ds(r0 + k * part, part), :], ks[mine, :]))
        yield 128
        for k in range(TOK // part):
            rows = pl.ds(r0 + k * part, part)
            qp = quadrant(k * part + lax.broadcasted_iota(jnp.int32, (part, 1), 0))
            s = jnp.where(qp == qq, scores[k], far_score)
            top = jnp.max(s, axis=1, keepdims=True)
            ex = jnp.exp((s - top) * (CH**-0.5))
            p = ex * (1.0 / jnp.sum(ex, axis=1, keepdims=True))
            prob[rows, :] = p
            pb[rows, :] = p.astype(bf16)
            yield 60
        mix[mine, :] = nn(pb[mine, :], vs[mine, :]).astype(bf16)
        yield 128
        x3[mine, :] = x2[mine, :] + nn(mix[mine, :], wo[...])
        yield 128
        yield from forward_tables(3, x3, jnp.broadcast_to(row(0) + row(7) + row(12), (8, 256)), row(13), row(14))
        yield from silu_pass(3, x3, sp4, xc3, False)

        z = nn(xc3[mine, :], wr[...])
        us[b, 0, pl.ds(8, TOK), :] = z[:, 0:128]
        us[b, 1, pl.ds(8, TOK), :] = z[:, 128:256]
        yield 128 * 3
        for r in range(SIDE):
            ql, qr = quads(r)
            inl = scale_ref[8 + (base + b) * 4 + ql]
            inr = scale_ref[8 + (base + b) * 4 + qr]
            for h in range(2):
                k = 8 + r * 16 + h * 8
                y = pltpu.roll(us[b, 0, pl.ds(k, 8), :], 64, 1)
                if r > 0:
                    y = y + us[b, 0, pl.ds(k - 16, 8), :] * mvu[at(r, h), :]
                if r < SIDE - 1:
                    y = y + us[b, 1, pl.ds(k + 16, 8), :] * mvd[at(r, h), :]
                inside = jnp.where(onleftn[b][h], inl, inr)
                err = jnp.where(lane < PIX, (y - tg_ref[at(r, h), :]) * inside, 0.0)
                lacc[...] += err * err
                xs[b, 0, pl.ds(k, 8), :] = (err * sc[...]).astype(bf16).astype(f32)
            yield 15
        for r in range(SIDE):
            tile0, tile1 = [], []
            for h in range(2):
                k = 8 + r * 16 + h * 8
                t0 = pltpu.roll(xs[b, 0, pl.ds(k, 8), :], 64, 1)
                if r < SIDE - 1:
                    t0 = t0 + xs[b, 0, pl.ds(k + 16, 8), :] * mvd[at(r, h), :]
                t1 = jnp.zeros((8, 128), f32)
                if r > 0:
                    t1 = xs[b, 0, pl.ds(k - 16, 8), :] * mvu[at(r, h), :]
                tile0.append(t0)
                tile1.append(t1)
            dyp[at(r, 0, 16), 0:128] = jnp.concatenate(tile0, axis=0).astype(bf16)
            dyp[at(r, 0, 16), 128:256] = jnp.concatenate(tile1, axis=0).astype(bf16)
            if r % GRAIN == GRAIN - 1:
                yield 10 * GRAIN

        yield from put_us(dyp[mine, :], wrt)
        weight_grad(gr, xc3, dyp, 0, 1)
        s1, s2 = yield from crop_sums(tap_back(sp4, x3))
        sum3, db, dg = backward_tables(3, s1, s2, row(13))
        gv[13] += dg
        gv[14] += db
        gv[12] += sum3
        yield 200
        for r in range(SIDE):
            halves = []
            for h in range(2):
                d = norm_grad(3, r, h, x3)
                gtop[at(r, h), :] = d
                halves.append(d)
            dpo[at(r, 0, 16), :] = jnp.concatenate(halves, axis=0).astype(bf16)
            if r % GRAIN == GRAIN - 1:
                yield 14 * GRAIN
        dmx[mine, :] = nn(dpo[mine, :], wot[...]).astype(bf16)
        yield 128

        def grad_out(two):
            def job():
                ga[:, 768:1024] += nn(mix[two, :].T, dpo[two, :])

            fill.append(job)

        later(grad_out)
        vlow = vs[mine, :] * jnp.asarray(CH**-0.5, bf16)
        for k in range(TOK // part):
            rows = pl.ds(r0 + k * part, part)
            da = nt(dmx[rows, :], vlow)
            p = prob[rows, :]
            t = da * p
            dsb[rows, :] = (t - p * jnp.sum(t, axis=1, keepdims=True)).astype(bf16)
            yield 70
        dv = nn(pb[mine, :].T, dmx[mine, :])
        trip[mine, 512:768] = dv.astype(bf16)
        gv[11] += jnp.sum(dv.reshape(TOK // 8, 8, CH), axis=0)
        yield 128
        dq = nn(dsb[mine, :], ks[mine, :])
        trip[mine, 0:256] = dq.astype(bf16)
        gv[10] += jnp.sum(dq.reshape(TOK // 8, 8, CH), axis=0)
        yield 128
        dk = nn(dsb[mine, :].T, qs[mine, :])
        trip[mine, 256:512] = dk.astype(bf16)
        yield 128
        dys[mine, :] = nn(trip[mine, :], wat[...])
        yield 128 * 3

        def grad_triple(two):
            turned = []
            for k in range(3):

                def job(k=k):
                    if not turned:
                        turned.append(nrm[two, :].T)
                    ga[:, k * 256 : (k + 1) * 256] += nn(turned[0], trip[two, k * 256 : (k + 1) * 256])

                fill.append(job)

        later(grad_triple)

        def plain(r, h):
            dy = dys[at(r, h), :]
            return dy, dy * x2[at(r, h), :]

        s1, s2 = yield from crop_sums(plain)
        sum2, db, dg = backward_tables(2, s1, s2, row(8))
        gv[8] += dg
        gv[9] += db
        sum2 = sum2 + sum3
        gv[7] += sum2
        yield 200
        for r in range(SIDE):
            halves = []
            for h in range(2):
                d = norm_grad(2, r, h, x2) + gtop[at(r, h), :]
                gtop[at(r, h), :] = d
                halves.append(d)
            spread_grad(0, r, jnp.concatenate(halves, axis=0))
            if r % GRAIN == GRAIN - 1:
                yield 18 * GRAIN
        yield from put_us(side[mine, 0:768], wt2)
        weight_grad(gk2, xc2, side, 0, 3)
        s1, s2 = yield from crop_sums(tap_back(sp2, x1))
        sum1, db, dg = backward_tables(1, s1, s2, row(5))
        gv[5] += dg
        gv[6] += db
        gv[4] += sum1
        dtb[pl.ds((base + b) * 8, 8), :] = sum1
        yield 200
        for r in range(SIDE):
            spread_grad(768, r, jnp.concatenate([norm_grad(1, r, h, x1) for h in range(2)], axis=0))
            if r % GRAIN == GRAIN - 1:
                yield 16 * GRAIN
        yield from put_us(side[mine, 768:1536], wt1)
        weight_grad(gk1, xc1, side, 768, 3)
        s1, s2 = yield from crop_sums(tap_back(sp1, x0))
        sum0, db, dg = backward_tables(0, s1, s2, row(2))
        gv[2] += dg
        gv[3] += db
        gv[0] += sum0 + sum2
        yield 200
        for r in range(SIDE):
            halves = [norm_grad(0, r, h, x0) + gtop[at(r, h), :] for h in range(2)]
            dps[at(r, 0, 16), :] = jnp.concatenate(halves, axis=0).astype(bf16)
            if r % GRAIN == GRAIN - 1:
                yield 14 * GRAIN

        def grad_stem(two):
            def job():
                gs[...] += nn(xt_ref[two, :].T, dps[two, :])

            fill.append(job)

        later(grad_stem)

    clocks = {b: float(b * SKEW) for b in range(PAIR)}
    streams = {b: stream(b) for b in range(PAIR)}
    filled = 0.0
    while streams:
        b = min(streams, key=lambda k: clocks[k])
        try:
            clocks[b] += next(streams[b])
        except StopIteration:
            del streams[b]
        now = min([clocks[k] for k in streams], default=1e18)
        while fill and filled < now:
            filled = max(filled, now if now < 1e17 else 0.0) + FILLCOST
            fill.pop(0)()

    @pl.when(step == last)
    def _():
        low = dtb[...].astype(bf16)
        hp = hpre[...]
        sg = jax.nn.sigmoid(hp)
        gp = (nn((hp * sg).astype(bf16).T, low) * 0.5).astype(bf16)
        hg = nt(low, wpj[...]) * (sg * (1.0 + hp * (1.0 - sg)))
        ge = (nn(feat_ref[...].T, hg.astype(bf16)) * 0.5).astype(bf16)
        twice = {10: 1.0, 11: 1.0}
        rows = [jnp.sum(gv[4 if k == 1 else k], axis=0, keepdims=True) * twice.get(k, 0.5) for k in range(15)]
        gnorm = jnp.concatenate(rows + [jnp.zeros((1, 256), f32)], axis=0)
        gstem = gs[...].T
        shared = pltpu.roll(lacc[...], PIX, 1)
        shared = jnp.concatenate([shared, jnp.zeros((AROW - 8, 128), f32)], axis=0)
        gstem = gstem + jnp.concatenate([shared] * VIRT, axis=0)
        for dy in range(3):
            for lo in range(0, 768, 256):
                part = gr[pl.ds(lo, 256), (dy // 2) * 128 : (dy // 2) * 128 + 128]
                if dy == 1:
                    part = pltpu.roll(part, 64, 1)
                grn[pl.ds(dy * 768 + lo, 256), :] = part
        for core in range(2):

            @pl.when(geo_ref[3] == core)
            def _(core=core):
                for f in range(VIRT):
                    z = f // 2
                    pair = [halves_ref[2 * part + ((f % 2) ^ core)] for part in range(2)]

                    def put(lo, hi, lanes, value, pair=pair, z=z):
                        for ref, first, end in zip(pair, (0, CUT), (CUT, PACKED)):
                            s, e = max(lo, first), min(hi, end)
                            if s < e:
                                ref[z, s - first : e - first, lanes] = value[s - lo : e - lo]

                    for dy in range(3):
                        lo, hi = max(f * KROW, dy * 768), min((f + 1) * KROW, (dy + 1) * 768)
                        if lo >= hi:
                            continue
                        src = pl.ds(lo - dy * 768, hi - lo)
                        d0, d1 = lo - f * KROW, hi - f * KROW
                        put(d0, d1, slice(0, 256), gk1[src, dy * 256 : (dy + 1) * 256].astype(bf16))
                        put(d0, d1, slice(256, 512), gk2[src, dy * 256 : (dy + 1) * 256].astype(bf16))
                    k = f * AROW
                    a1, a2, p0 = KROW, KROW + AROW, KROW + 2 * AROW
                    e0 = p0 + PROW
                    put(a1, a2, slice(0, 512), ga[k : k + AROW, 0:512].astype(bf16))
                    put(a2, p0, slice(0, 512), ga[k : k + AROW, 512:1024].astype(bf16))
                    put(p0, e0, slice(0, 256), gp[f * 2 * PROW : f * 2 * PROW + PROW, :])
                    put(p0, e0, slice(256, 512), gp[f * 2 * PROW + PROW : (f + 1) * 2 * PROW, :])
                    put(e0, TROW, slice(0, 512), ge[f * EROW : (f + 1) * EROW, :])
                    back = grn[pl.ds(f * KROW, 384), :].T[:TAIL, :]
                    keep = lax.broadcasted_iota(jnp.int32, (TAIL, 384), 1) < KROW
                    put(TROW, PACKED, slice(0, 384), jnp.where(keep, back, 0.0).astype(bf16))
                    put(TROW, TROW + 32, slice(384, 512), gstem[k : k + AROW, :].astype(bf16))
                    tile = gnorm[:, (f // 4) * 128 : (f // 4) * 128 + 128]
                    tile = pltpu.roll(tile, (128 - (f % 4) * AROW) % 128, 1)
                    keep = lax.broadcasted_iota(jnp.int32, (16, 128), 1) < AROW
                    put(TROW + 32, PACKED, slice(384, 512), jnp.where(keep, tile, 0.0).astype(bf16))
        loss_ref[...] = lacc[...]


SKEW = 450
FILLCOST = 128
GRAIN = 2


def run_step(packed, quad, geo, scal, feat, cp, tg):
    canvases = cp.shape[0] // TOK
    whole = pl.BlockSpec(memory_space=pltpu.VMEM)
    smem = pl.BlockSpec(memory_space=pltpu.SMEM)

    def rows(n, lanes):
        return pl.BlockSpec((n, lanes), lambda i, *_: (i, 0))

    items = scratch_list(canvases)
    return pl.pallas_call(
        functools.partial(step_kernel, [name for name, _, _ in items]),
        grid_spec=pltpu.PrefetchScalarGridSpec(
            num_scalar_prefetch=2,
            grid=(canvases // PAIR,),
            in_specs=[
                smem, whole, whole, whole, whole, whole, whole, rows(ROWS, 128), rows(ROWS, 128),
            ],
            out_specs=[whole] * 6,
            scratch_shapes=[pltpu.VMEM(shape, dtype) for _, shape, dtype in items],
        ),
        out_shape=[
            *[jax.ShapeDtypeStruct((VIRT // 2, CUT, 512), bf16)] * 4,
            jax.ShapeDtypeStruct((8, 128), f32),
            jax.ShapeDtypeStruct((8, 128), f32),
        ],
        compiler_params=pltpu.CompilerParams(
            dimension_semantics=("arbitrary",), vmem_limit_bytes=60 * 1024 * 1024
        ),
        name="unet_step",
    )(quad, geo, scal, *packed, feat, cp, tg)


def patch_kernel(image_ref, out_ref, staged):
    n = image_ref.shape[0]
    slot = staged.shape[0] // SIDE
    for r in range(SIDE):
        for c in range(3):
            staged[pl.ds(r * slot, n), c * 256 : (c + 1) * 256] = image_ref[:, c * 4096 + r * 256 : c * 4096 + r * 256 + 256]
    src = lax.broadcasted_iota(jnp.int32, (768, 256), 0)
    place = ((src >> 2) & 15) * 128 + (src >> 8) * 16 + ((src >> 6) & 3) * 4 + (src & 3)
    for j in range(SIDE // 2):
        lane = lax.broadcasted_iota(jnp.int32, (768, 256), 1) + j * 256
        out = nn(staged[...], (place == lane).astype(bf16))
        for r in range(SIDE):
            for i in range(2):
                rows = pl.ds(r * SIDE + 2 * j + i, n, stride=TOK)
                out_ref[rows, :] = out[r * slot : r * slot + n, i * 128 : (i + 1) * 128]


def patches(image):
    n = image.shape[0]
    slot = -(-n // 16) * 16
    whole = pl.BlockSpec(memory_space=pltpu.VMEM)
    return pl.pallas_call(
        patch_kernel,
        in_specs=[whole],
        out_specs=whole,
        out_shape=jax.ShapeDtypeStruct((n * TOK, 128), f32),
        scratch_shapes=[pltpu.VMEM((SIDE * slot, 768), bf16)],
        compiler_params=pltpu.CompilerParams(vmem_limit_bytes=48 * 1024 * 1024),
        cost_estimate=pl.CostEstimate(flops=2 * 32 * n * 768 * 2048, bytes_accessed=4 * n * TOK * 128, transcendentals=0),
        name="patches",
    )(image)


def upper_kernel(kernels, upper):
    upper[...] = kernels[0:CUT, :].astype(bf16)


def pack_kernel(copy, tokens, upper, stem, kernels, embed, project, attention, readout, norm, mine, block):
    a1, a2, p0 = KROW - CUT, KROW + AROW - CUT, KROW + 2 * AROW - CUT
    e0, tail, end = p0 + PROW, TROW - CUT, PACKED - CUT

    def put(lo, hi, value):
        for q in range(value.shape[1] // 128):
            block[q, lo:hi, :] = value[:, q * 128 : (q + 1) * 128].astype(bf16)

    put(0, a1, kernels[CUT:KROW, :])
    put(a1, a2, attention[:, 0:512])
    put(a2, p0, attention[:, 512:1024])
    put(p0, e0, jnp.concatenate([project[0:PROW, :], project[PROW : 2 * PROW, :]], axis=1))
    put(e0, tail, embed[...])
    for q in range(2, 4):
        block[q, tail:end, :] = jnp.zeros((TAIL, 128), bf16)
    put(tail, end, readout[:, 0:256])
    block[2, tail:end, 0 : KROW - 256] = readout[:, 256:KROW].astype(bf16)
    block[3, tail : tail + 32, 0:PIX] = stem[...].astype(bf16)
    block[3, tail + 32 : tail + 47, 0:AROW] = norm[...].astype(bf16)
    mine[0:end, :] = block[copy[0]]
    row = lax.broadcasted_iota(jnp.int32, (16, 128), 0)
    lane = lax.broadcasted_iota(jnp.int32, (16, 128), 1)
    tokens = tokens[0]
    limbs = jnp.where(lane == 0, tokens >> 6, jnp.where(lane == 1, tokens & 63, 0))
    mine[end : end + 16, :] = jnp.where(row == 0, limbs, 0).astype(f32).astype(bf16)


def pack_weights(masters, copy, tokens):
    stem, kernels, embed, project, attention, readout, norm = masters
    whole, smem = pl.BlockSpec(memory_space=pltpu.VMEM), pl.BlockSpec(memory_space=pltpu.SMEM)
    rest = PACKED - CUT
    upper = pl.pallas_call(
        upper_kernel,
        grid=(1,),
        in_specs=[pl.BlockSpec((CUT, 512), lambda i: (0, 0))],
        out_specs=pl.BlockSpec((CUT, 512), lambda i: (0, 0)),
        out_shape=jax.ShapeDtypeStruct((CUT, 512), bf16),
        name="pack_upper",
    )(kernels)
    mine = pl.pallas_call(
        pack_kernel,
        in_specs=[smem, smem, pl.BlockSpec(memory_space=pl.ANY)] + [whole] * 7,
        out_specs=whole,
        out_shape=jax.ShapeDtypeStruct((rest + 16, 128), bf16),
        scratch_shapes=[pltpu.VMEM((4, rest, 128), bf16)],
        name="pack_rest",
    )(copy.reshape(1), tokens.reshape(1), upper, stem, kernels, embed, project, attention, readout.T, norm.T)
    return upper, mine


def gather_weights(upper, mine, cp, tg):
    shards = lax.axis_size("fsdp")
    upper = lax.all_gather(upper, "fsdp", axis=0, tiled=False)
    got = [lax.ppermute(mine, "fsdp", [(i, (i + 2 * j) % shards) for i in range(shards)]) for j in range(1, 4)]
    both = jnp.stack([mine] + got)
    a, b = both[:, :PART], both[:, PART:]
    ga, gb = exchange(a, "dp", 1), exchange(b, "dp", 2)
    a, b, cp = lax.optimization_barrier((jnp.stack([a, ga]), jnp.stack([b, gb]), cp))
    ga, gb = exchange(a, "dp", 2), exchange(b, "dp", 1)
    a, b, tg = lax.optimization_barrier((jnp.concatenate([a, ga]), jnp.concatenate([b, gb]), tg))
    return (upper, a, b, exchange(a, "fsdp", 1), exchange(b, "fsdp", 1)), cp, tg


def slots_of(packed):
    rest = packed[:, CUT:].reshape(4, 2, PACKED - CUT, 4, 128)
    rest = jnp.stack([rest[z] for z in (0, 3, 2, 1)]).transpose(1, 3, 0, 2, 4)
    a, b = rest[..., :PART, :], jnp.stack([rest[:, q, :, PART:, :] for q in (0, 2, 1, 3)], axis=1)
    b = jnp.pad(b, ((0, 0), (0, 0), (0, 0), (0, 16), (0, 0)))
    return packed[:, :CUT], a[0], b[0], a[1], b[1]


def update_kernel(place, count, own, first, second, *refs):
    loss_out, total = refs[-2:]
    refs = refs[:-2]
    half, quarter = PACKED // 4, PACKED // 8
    for k in range(2):
        near, far = place[k], place[1 - k]
        at = k * 2 * half
        total[pl.ds(pl.multiple_of(at + near * half + far * quarter, 8), quarter), :] = own[k].astype(f32)
        total[pl.ds(pl.multiple_of(at + near * half + (1 - far) * quarter, 8), quarter), :] = first[k].astype(f32)
        there = at + (1 - near) * half
        total[pl.ds(pl.multiple_of(there + far * quarter, 8), quarter), :] = second[k, 0].astype(f32)
        total[pl.ds(pl.multiple_of(there + (1 - far) * quarter, 8), quarter), :] = second[k, 1].astype(f32)
    shared = total[TROW : TROW + 8, 384:512]
    lane = lax.broadcasted_iota(jnp.int32, (8, 128), 1)
    shared = jnp.where((lane >= PIX) & (lane < 2 * PIX), shared, 0.0)
    count = count[0:1, 0:1]
    loss_out[...] = jnp.sum(shared, axis=(0, 1), keepdims=True) / count
    rate = lr_scale * jnp.sqrt(count)
    a1, a2, p0 = KROW, KROW + AROW, KROW + 2 * AROW
    e0 = p0 + PROW
    everything = slice(None)
    cuts = [
        (0, everything, everything, total[TROW : TROW + 32, 384:512][:, :PIX]),
        (1, everything, everything, total[0:a1, :]),
        (2, everything, everything, total[e0:TROW, :]),
        (3, slice(0, PROW), everything, total[p0:e0, 0:256]),
        (3, slice(PROW, 2 * PROW), everything, total[p0:e0, 256:512]),
        (4, everything, slice(0, 512), total[a1:a2, :]),
        (4, everything, slice(512, 1024), total[a2:p0, :]),
        (5, everything, everything, total[TROW:PACKED, 0:384][:, :KROW]),
        (6, everything, everything, total[TROW + 32 : PACKED, 384:512][:15, :AROW]),
    ]
    for n, rows, lanes, grad in cuts:
        w, m, a, m_out, w_out, a_out = [refs[n + 7 * j] for j in range(6)]
        m_next = momentum_rate * m[rows, lanes] + grad
        w_next = w[rows, lanes] - rate * (grad + momentum_rate * m_next)
        m_out[rows, lanes] = m_next
        w_out[rows, lanes] = w_next
        a_out[rows, lanes] = average_rate * a[rows, lanes] + (1.0 - average_rate) * w_next


def turn(arrays):
    return [x.T if k in (5, 6) else x for k, x in enumerate(arrays)]


def update_fused(place, count, own, first, second, masters, moments, averages):
    whole = pl.BlockSpec(memory_space=pltpu.VMEM)
    smem = pl.BlockSpec(memory_space=pltpu.SMEM)
    state = turn(masters) + turn(moments) + turn(averages)
    out = pl.pallas_call(
        update_kernel,
        in_specs=[smem] + [whole] * 25,
        out_specs=[whole] * 22,
        out_shape=[jax.ShapeDtypeStruct(x.shape, f32) for x in state] + [jax.ShapeDtypeStruct((1, 1), f32)],
        scratch_shapes=[pltpu.VMEM((PACKED, 512), f32)],
        compiler_params=pltpu.CompilerParams(vmem_limit_bytes=32 * 1024 * 1024),
        name="update",
    )(place, count, own, first, second, *state)
    return (out[21][0, 0],) + tuple(turn(out[0:7]) + turn(out[7:14]) + turn(out[14:21]))


def signal_table():
    beta = np.linspace(0.0001, 0.02, TSTEPS, dtype=np.float64)
    return np.exp(np.cumsum(np.log(1.0 - beta))).astype(np.float32)


def time_features(time_steps):
    half_width = TEMB // 2
    frequency = jnp.exp(-math.log(10000.0) * jnp.arange(half_width, dtype=f32) / (half_width - 1))
    angles = time_steps.astype(f32)[..., None] * frequency
    return jnp.concatenate([jnp.sin(angles), jnp.cos(angles)], axis=-1)


def prepare(lab, time_steps, count, place):
    canvases = lab.shape[0]
    cut = jnp.sum(jnp.all(lab == lab[:, :, :1], axis=1).astype(jnp.int32), axis=1)
    left = jnp.sum((lab[:, :, 0] == lab[:, :1, 0]).astype(jnp.int32), axis=1)
    right = jnp.sum((lab[:, :, -1] == lab[:, :1, -1]).astype(jnp.int32), axis=1)
    own = jnp.stack([lab[:, 0, 0], lab[:, -1, 0], lab[:, 0, -1], lab[:, -1, -1]], axis=1)
    area = jnp.stack(
        [cut * left, cut * (SIDE - left), (SIDE - cut) * right, (SIDE - cut) * (SIDE - right)], axis=1
    ).astype(f32)
    here = [jnp.full_like(cut, x) for x in place]
    geo = jnp.stack([cut, left, right] + here + here[:2], axis=1).reshape(-1)
    line = jnp.arange(SIDE, dtype=jnp.int32)
    quad = (line >= left[:, None]).astype(jnp.int32) + 2 * (line >= right[:, None]).astype(jnp.int32)
    quad = quad.reshape(-1)
    hit = own[..., None] == jnp.arange(1, CROPS + 1, dtype=jnp.int32)
    times = jnp.sum(jnp.where(hit, time_steps[:, None, :], 0), axis=-1)
    eight = np.array([0, 0, 2, 2, 1, 1, 3, 3])
    feat = time_features(times[:, eight]).astype(bf16).reshape(-1, TEMB)
    picked = times[..., None] == jnp.arange(TSTEPS, dtype=jnp.int32)
    chosen = jnp.sum(jnp.where(picked, jnp.asarray(signal_table()), 0.0), axis=-1)
    inside = (own > 0).astype(f32)
    levels = [inside, jnp.sqrt(chosen), jnp.sqrt(1.0 - chosen), area]
    scal = jnp.concatenate([jnp.full((8,), count, f32)] + [x.reshape(-1) for x in levels])
    return quad, geo, scal, feat


def exchange(value, axis, bit):
    return lax.ppermute(value, axis, [(i, i ^ bit) for i in range(lax.axis_size(axis))])


def sum_over_all(value):
    for axis in ("fsdp", "dp"):
        bit = 1
        while bit < lax.axis_size(axis):
            value = value + exchange(value, axis, bit)
            bit *= 2
    return value


def join(a, b):
    return (a.astype(f32) + b.astype(f32)).astype(bf16)


def halves(value, which):
    n = value.shape[1] // 2
    low, high = value[:, :n], value[:, n:]
    return jnp.where(which == 0, low, high), jnp.where(which == 0, high, low)


def reduce_grads(keep, send):
    parts = [join(own, exchange(other, "fsdp", 1)) for own, other in zip(keep, send)]
    near, far = lax.axis_index("dp") % 2, lax.axis_index("dp") // 2
    for first, second in (((near, 1), (far, 2)), ((far, 2), (near, 1))):
        split = [halves(parts[0], first[0]), halves(parts[1], second[0])]
        came = [exchange(split[0][1], "dp", first[1]), exchange(split[1][1], "dp", second[1])]
        parts = [join(split[0][0], came[0]), join(split[1][0], came[1])]
    blocks = jnp.stack(parts, axis=1)
    chips, shards = blocks.shape[0], lax.axis_size("fsdp")
    chip = lax.axis_index("fsdp") // 2
    own = lax.dynamic_index_in_dim(blocks, chip, 0, keepdims=False).astype(f32)
    for j in range(1, chips):
        out = lax.dynamic_index_in_dim(blocks, (chip + j) % chips, 0, keepdims=False)
        own = own + lax.ppermute(out, "fsdp", [(i, (i + 2 * j) % shards) for i in range(shards)]).astype(f32)
    own = own.astype(bf16)
    first = jnp.stack([exchange(own[0], "dp", 2), exchange(own[1], "dp", 1)])
    both = jnp.stack([own, first], axis=1)
    second = jnp.stack([exchange(both[0], "dp", 1), exchange(both[1], "dp", 2)])
    return jnp.stack([near, far]).astype(jnp.int32), own, first, second


def assemble(place, own, first, second):
    n = own.shape[1]
    parts = []
    for k in range(2):
        near, far = place[k], place[1 - k]
        mine = jnp.where(far == 0, jnp.concatenate([own[k], first[k]]), jnp.concatenate([first[k], own[k]]))
        s = second[k]
        theirs = jnp.where(far == 0, jnp.concatenate([s[0], s[1]]), jnp.concatenate([s[1], s[0]]))
        parts.append(jnp.where(near == 0, jnp.concatenate([mine, theirs]), jnp.concatenate([theirs, mine])))
    return jnp.concatenate(parts).astype(f32)


def on_device(clean, noise, crop_labels, time_steps, *state):
    masters, moments, averages = state[0:7], state[7:14], state[14:21]
    shards = lax.axis_size("fsdp")
    index, copy = lax.axis_index("fsdp"), lax.axis_index("dp")
    tokens = jnp.sum((crop_labels > 0).astype(jnp.int32))
    direct = shards == VIRT and lax.axis_size("dp") == 4
    cp, tg = patches(clean), patches(noise)
    if direct:
        packed, cp, tg = gather_weights(*pack_weights(masters, copy, tokens), cp, tg)
        inputs = prepare(crop_labels, time_steps, 0.0, (index % 2, index // 2, copy))
    else:
        own = lax.all_gather(pack_rows([w.astype(bf16) for w in masters]), "fsdp", axis=0, tiled=False)
        packed = slots_of(repack(own, shards, VIRT))
        count = sum_over_all(PATCH * PATCH * tokens.astype(f32).reshape(1, 1))[0, 0]
        inputs = prepare(crop_labels, time_steps, count, (0, 0, 0))
    *grads, loss, total = run_step(packed, *inputs, cp, tg)
    keep, send = grads[0::2], grads[1::2]
    if not direct:
        core = index % 2
        keep, send = jnp.concatenate(keep, axis=1), jnp.concatenate(send, axis=1)
        blocks = jnp.stack([keep, send], axis=1).reshape(VIRT, PACKED, 512)
        blocks = repack(blocks, VIRT, shards)
        blocks = blocks.reshape(shards // 2, 2, *blocks.shape[1:])
        keep = lax.dynamic_index_in_dim(blocks, core, 1, keepdims=False)
        send = lax.dynamic_index_in_dim(blocks, 1 - core, 1, keepdims=False)
        n = keep.shape[1] // 2
        keep, send = [keep[:, :n], keep[:, n:]], [send[:, :n], send[:, n:]]
    place, own, first, second = reduce_grads(keep, send)
    if direct:
        return update_fused(place, total, own, first, second, masters, moments, averages)
    rate = lr_scale * jnp.sqrt(count)
    total_loss = sum_over_all(jnp.sum(loss).reshape(1, 1))[0, 0]
    cut = [masters[1].shape[0], masters[0].shape[0], masters[3].shape[0], masters[2].shape[0]]
    grads = unpack_rows(assemble(place, own, first, second), *cut)
    moment_next = tuple(momentum_rate * m + g for m, g in zip(moments, grads))
    master_next = tuple(w - rate * (g + momentum_rate * m) for w, g, m in zip(masters, grads, moment_next))
    average_next = tuple(average_rate * a + (1.0 - average_rate) * w for a, w in zip(averages, master_next))
    return (total_loss / count,) + moment_next + master_next + average_next


def solution(mesh):
    split = P(("dp", "fsdp"), None)
    in_specs = (split, split, P(("dp", "fsdp"), None, None), split) + (P("fsdp", None),) * 21
    out_specs = (P(),) + (P("fsdp", None),) * 21
    return jax.shard_map(on_device, mesh=mesh, in_specs=in_specs, out_specs=out_specs, check_vma=False)
```
